32 devices in a mesh: dp: 4 (over z), seq: 8 (over y, x, core).
Axes of the slice: x: 2, y: 2, z: 4, core: 2. Of those that a mesh axis runs over, the one named last changes fastest.
Arguments:
- saved_codes: bfloat16 [4, 1024, 1536], P('dp', 'seq'), may hold values from -6 to 6
- code_scales: float32 [4, 12, 1024], P('dp', None, 'seq'), may hold values from 0.25 to 4
- lengths: int32 [4], replicated, may hold values from 128 to 1024, as said below
- in_weight: bfloat16 [3072, 1536], P('dp'), may hold values from -0.15625 to 0.15625
- conv_kernel: float32 [31, 1536], replicated, may hold values from -1 to 1
- bn_gain: float32 [1536], replicated, may hold values from 0.1 to 1.9
- bn_shift: float32 [1536], replicated, may hold values from -3 to 3
- out_grad: bfloat16 [4, 1024, 1536], P('dp', 'seq'), may hold values from -6 to 6
Outputs:
- in_grad: bfloat16 [4, 1024, 1536], P('dp', 'seq')
- weight_grad: float32 [3072, 1536], P('dp')
- kernel_grad: float32 [31, 1536], replicated
- gain_grad: float32 [1536], replicated
- shift_grad: float32 [1536], replicated
The draws below stay inside these ranges and needn't reach their ends.
Inputs may be any that keep to these rules, and one draw needn't show every extreme that they name: `lengths`: at least one recording has exactly 1024 valid frames.
All inputs are finite; a program needn't handle non-finite values.
Results may differ from the reference program's by a relative error of at most 0.0067.
Values may be sent and summed in bfloat16 or wider, within the bound.
A program may use at most 128 MiB of HBM per device.

```python
import math
import jax
import jax.numpy as jnp
from jax import lax

D = 1536
KERNEL = 31
GROUPS = 4
FRAMES = 1024


def draw_lengths(key, part):
    first_key, second_key = jax.random.split(jax.random.fold_in(key, 11))
    cubes = jax.random.randint(first_key, (GROUPS,), 0, 16)
    drawn = FRAMES // 8 + (FRAMES - FRAMES // 8) * (cubes * cubes * cubes) // 3375
    longest = jax.random.randint(second_key, (), 0, GROUPS)
    return jnp.where(jnp.arange(GROUPS) == longest, FRAMES, drawn).astype(jnp.int32)


def levels(own_key, extent, cuts, smallest, largest):
    factor_of, own = 1.0, jax.random.fold_in(own_key, 6)
    for axis_at, shards_of in cuts:
        draws = jnp.exp(jax.random.uniform(jax.random.fold_in(own, axis_at), (shards_of,), jnp.float32, smallest / len(cuts), largest / len(cuts)))
        factor_of = factor_of * jnp.repeat(draws, extent[axis_at] // shards_of).reshape([-1 if axis == axis_at else 1 for axis in range(len(extent))])
    return factor_of


def centred(rng, extent, deviation, reach, shards=(), held_as=jnp.bfloat16):
    result = jax.random.normal(rng, extent, jnp.float32) * deviation
    if len(shards) > 0:
        result = levels(rng, extent, shards, -0.22, 0.18) * result
    return jnp.clip(result, min=-reach, max=reach).astype(held_as)


def setup_inputs(seed: int = 0) -> dict:
    key_list = jax.random.split(jax.random.key(seed), 9)
    saved_codes = centred(key_list[0], (GROUPS, FRAMES, D), 1.0, 6.0, ((0, 4), (1, 8)))
    code_scales = jnp.clip(jnp.exp(math.log(4.0) - 2.7725887 * jax.random.uniform(key_list[1], (GROUPS, D // 128, FRAMES), jnp.float32) ** levels(key_list[1], (GROUPS, D // 128, FRAMES), ((0, 4), (2, 8)), -0.2, 0.2)), 0.25, 4.0)
    lengths = draw_lengths(jax.random.fold_in(key_list[8], 71), 0)
    in_weight = centred(key_list[3], (2 * D, D), D ** -0.5, 0.15625, ((0, 4),))
    conv_kernel = centred(key_list[4], (KERNEL, D), KERNEL ** -0.5, 1.0, (), jnp.float32)
    bn_gain = jnp.clip(1.0 + 0.18 * jax.random.normal(key_list[5], (D,), jnp.float32), 0.1, 1.9)
    bn_shift = centred(key_list[6], (D,), 0.5, 3.0, (), jnp.float32)
    out_grad = centred(key_list[7], (GROUPS, FRAMES, D), 1.0, 6.0, ((0, 4), (1, 8)))
    return dict(saved_codes=saved_codes, code_scales=code_scales, lengths=lengths, in_weight=in_weight, conv_kernel=conv_kernel, bn_gain=bn_gain, bn_shift=bn_shift, out_grad=out_grad)


EPS = 1e-05

def restore(quantized, scales):
    per_channel = jnp.repeat(scales.T, 128, axis=1)
    return (quantized.astype(jnp.float32) * per_channel).astype(jnp.bfloat16)

def depthwise(padded, kernel, frames):
    running = jnp.zeros((frames, padded.shape[1]), jnp.float32)
    for offset in range(kernel.shape[0]):
        running = running + kernel[offset] * padded[offset:offset + frames].astype(jnp.float32)
    return running

def reference(saved_codes, code_scales, lengths, in_weight, conv_kernel, bn_gain, bn_shift, out_grad):
    frames = saved_codes.shape[1]
    feature_width = saved_codes.shape[2]
    tap_count = conv_kernel.shape[0]
    half_span = (tap_count - 1) // 2
    positions = jnp.arange(frames, dtype=jnp.int32)
    counted = jnp.sum(lengths).astype(jnp.float32)
    flipped = conv_kernel[::-1]

    def forward_group(inputs):
        quantized, scales, length = inputs
        valid_mask = (positions < length).astype(jnp.float32)[:, None]
        restored = restore(quantized, scales)
        pre_act = lax.dot_general(restored, in_weight, (((1,), (1,)), ((), ())), preferred_element_type=jnp.float32)
        gated = (pre_act[:, :feature_width] * jax.nn.sigmoid(pre_act[:, feature_width:]) * valid_mask).astype(jnp.bfloat16)
        padded = jnp.pad(gated, ((half_span, half_span), (0, 0)))
        return (pre_act, gated, depthwise(padded, conv_kernel, frames))
    pre_all, gated_all, conv_all = lax.map(forward_group, (saved_codes, code_scales, lengths))
    mask_all = (positions[None, :] < lengths[:, None]).astype(jnp.float32)[:, :, None]
    mean_value = lax.optimization_barrier(jnp.sum(conv_all * mask_all, axis=(0, 1))) / counted
    centered = (conv_all - mean_value) * mask_all
    variance = lax.optimization_barrier(jnp.sum(centered * centered, axis=(0, 1))) / counted
    inverse = lax.rsqrt(variance + EPS)

    def shaped_grad(conv_out, upstream, valid_mask):
        normed = (conv_out - mean_value) * inverse
        shaped = bn_gain * normed + bn_shift
        smooth = jax.nn.sigmoid(shaped)
        grad_shaped = upstream.astype(jnp.float32) * valid_mask * smooth * (1.0 + shaped * (1.0 - smooth))
        return (normed, grad_shaped)

    def sums_group(inputs):
        conv_out, upstream, length = inputs
        valid_mask = (positions < length).astype(jnp.float32)[:, None]
        normed, grad_shaped = shaped_grad(conv_out, upstream, valid_mask)
        return (lax.optimization_barrier(jnp.sum(grad_shaped, axis=0)), lax.optimization_barrier(jnp.sum(grad_shaped * normed, axis=0)))
    shift_parts, gain_parts = lax.map(sums_group, (conv_all, out_grad, lengths))
    shift_grad = lax.optimization_barrier(jnp.sum(shift_parts, axis=0))
    gain_grad = lax.optimization_barrier(jnp.sum(gain_parts, axis=0))

    def backward_group(inputs):
        pre_act, gated, conv_out, quantized, scales, length, upstream = inputs
        valid_mask = (positions < length).astype(jnp.float32)[:, None]
        restored = restore(quantized, scales)
        normed, grad_shaped = shaped_grad(conv_out, upstream, valid_mask)
        grad_conv = bn_gain * inverse * (grad_shaped - (shift_grad + normed * gain_grad) / counted) * valid_mask
        gated_pad = jnp.pad(gated, ((half_span, half_span), (0, 0)))
        kernel_part = jnp.stack([lax.optimization_barrier(jnp.sum(grad_conv * gated_pad[offset:offset + frames].astype(jnp.float32), axis=0)) for offset in range(tap_count)])
        grad_pad = jnp.pad(grad_conv, ((half_span, half_span), (0, 0)))
        grad_gated = depthwise(grad_pad, flipped, frames) * valid_mask
        linear = pre_act[:, :feature_width]
        gate_part = jax.nn.sigmoid(pre_act[:, feature_width:])
        grad_pre = jnp.concatenate([grad_gated * gate_part, grad_gated * linear * gate_part * (1.0 - gate_part)], axis=1).astype(jnp.bfloat16)
        in_grad = jnp.dot(grad_pre, in_weight, preferred_element_type=jnp.float32).astype(jnp.bfloat16)
        weight_part = lax.dot_general(grad_pre, restored, (((0,), (0,)), ((), ())), preferred_element_type=jnp.float32)
        return (in_grad, kernel_part, weight_part)
    in_grad, kernel_parts, weight_parts = lax.map(backward_group, (pre_all, gated_all, conv_all, saved_codes, code_scales, lengths, out_grad))
    return (in_grad, lax.optimization_barrier(jnp.sum(weight_parts, axis=0)), lax.optimization_barrier(jnp.sum(kernel_parts, axis=0)), gain_grad, shift_grad)
```

```python
import functools

import jax
import jax.numpy as jnp
from jax import lax
from jax.experimental import pallas as pl
from jax.experimental.pallas import tpu as pltpu
from jax.sharding import PartitionSpec as P

EPS = 1e-05
MESH = pl.DeviceIdType.MESH
VM = pl.BlockSpec(memory_space=pltpu.VMEM)


def at(d, s):
    return {"dp": d, "seq": s}


def greet(peers):
    barrier = pltpu.get_barrier_semaphore()
    for peer in peers:
        pl.semaphore_signal(barrier, inc=1, device_id=peer, device_id_type=MESH)
    pl.semaphore_wait(barrier, len(peers))


def remote(src, dst, send, recv, peer):
    return pltpu.make_async_remote_copy(
        src_ref=src, dst_ref=dst, send_sem=send, recv_sem=recv, device_id=peer, device_id_type=MESH
    )


def ring_peers(me, count):
    return [lax.rem(me + k, count) for k in range(1, count)]


def merge(parts, stats):
    if not stats:
        return functools.reduce(lambda a, b: a + b, parts)
    sums = [part[0:16] for part in parts]
    squares = [part[16:32] for part in parts]
    counts = [part[32:48] for part in parts]
    total = functools.reduce(lambda a, b: a + b, sums)
    count = functools.reduce(lambda a, b: a + b, counts)
    mean = total / jnp.maximum(count, 1.0)
    spread = functools.reduce(lambda a, b: a + b, squares)
    for own, n in zip(sums, counts):
        shift = own / jnp.maximum(n, 1.0) - mean
        spread = spread + n * (shift * shift)
    return jnp.concatenate([total, spread, count], axis=0)


def sum_kernel(stats, dp_n, seq_n, x_ref, o_ref, near, far, mid, s1, r1, s2, r2):
    d, s = lax.axis_index("dp"), lax.axis_index("seq")
    plane = ring_peers(s, seq_n)
    line = ring_peers(d, dp_n)
    greet([at(d, j) for j in plane] + [at(j, s) for j in line])
    for k, j in enumerate(plane):
        remote(x_ref, near.at[s], s1.at[k], r1.at[s], at(d, j)).start()
    near[s] = x_ref[...]
    for k, j in enumerate(plane):
        copy = remote(x_ref, near.at[j], s1.at[k], r1.at[j], at(d, j))
        copy.wait_recv()
        copy.wait_send()
    mid[...] = merge([near[j] for j in range(seq_n)], stats)
    for k, j in enumerate(line):
        remote(mid, far.at[d], s2.at[k], r2.at[d], at(j, s)).start()
    far[d] = mid[...]
    for k, j in enumerate(line):
        copy = remote(mid, far.at[j], s2.at[k], r2.at[j], at(j, s))
        copy.wait_recv()
        copy.wait_send()
    o_ref[...] = merge([far[j] for j in range(dp_n)], stats)


def sum_all(vectors, stats, collective_id):
    dp_n, seq_n = lax.axis_size("dp"), lax.axis_size("seq")
    blocks = vectors[0].shape[-1] // 128
    stacked = jnp.stack([v.reshape(blocks, 128) for v in vectors])
    stacked = jnp.pad(stacked, ((0, 0), (0, 16 - blocks), (0, 0)))
    rows = 16 * len(vectors)
    shape = (rows, 128)
    out = pl.pallas_call(
        functools.partial(sum_kernel, stats, dp_n, seq_n),
        out_shape=jax.ShapeDtypeStruct(shape, jnp.float32),
        in_specs=[VM],
        out_specs=VM,
        scratch_shapes=[
            pltpu.VMEM((seq_n,) + shape, jnp.float32),
            pltpu.VMEM((dp_n,) + shape, jnp.float32),
            pltpu.VMEM(shape, jnp.float32),
            pltpu.SemaphoreType.DMA((seq_n,)),
            pltpu.SemaphoreType.DMA((seq_n,)),
            pltpu.SemaphoreType.DMA((dp_n,)),
            pltpu.SemaphoreType.DMA((dp_n,)),
        ],
        compiler_params=pltpu.CompilerParams(collective_id=collective_id, has_side_effects=True),
    )(stacked.reshape(shape))
    return out.reshape(len(vectors), 16, 128)[:, :blocks].reshape(len(vectors), blocks * 128)


HALO = 32
EDGE = 16
TAPS = 31
BF = jnp.bfloat16
F32 = jnp.float32


class Net:
    def __init__(self, send_sems, recv_sems):
        self.send_sems, self.recv_sems = send_sems, recv_sems
        self.used = 0
        self.sent = []

    def send(self, src, dst, peer):
        copy = remote(src, dst, self.send_sems.at[self.used], self.recv_sems.at[self.used], peer)
        self.used += 1
        copy.start()
        self.sent.append(copy)
        return copy

    def drain(self):
        for copy in self.sent:
            copy.wait_send()


def rows_at(start, size):
    return pl.ds(pl.multiple_of(start, 16), size)


def cols_at(start, size):
    return pl.ds(pl.multiple_of(start, 128), size)


def fused_kernel(
    len_ref, w_ref, res_ref, og_ref, ck_ref, gain_ref, shift_ref,
    ig_ref, wg_ref, kf_ref,
    W, R, O, X, G, A, S, C, D, GP, Y,
    st1, sb1, st2, sb2, vec,
    kp, kb,
    igp, igs, igr, igs2, igr2,
    P, sa, ra, sa2, ra2, F,
    send_sems, recv_sems, local_sems,
):
    z, s = lax.axis_index("dp"), lax.axis_index("seq")
    c, x, y = lax.rem(s, 2), lax.rem(s // 2, 2), s // 4
    q = s // 2
    kind, half = z // 2, lax.rem(z, 2)
    mate_z = z + 1 - 2 * half
    twin_z = z + 2 - 4 * kind
    jo, jm = half, 1 - half
    frames = res_ref.shape[0]
    span = 2 * frames
    width = res_ref.shape[1]
    hw = width // 2

    def chip_at(dy, dx):
        yy = 1 - y if dy else y
        xx = 1 - x if dx else x
        return yy * 2 + xx

    core = at(z, s + 1 - 2 * c)
    mate = at(mate_z, s)
    twin = at(twin_z, s)
    offsets = [(0, 1), (1, 0), (1, 1)]
    plane = [at(z, chip_at(dy, dx) * 2 + c) for dy, dx in offsets]
    px, py = plane[0], plane[1]
    far = [at(twin_z, chip_at(dy, dx) * 2 + c) for dy, dx in offsets]
    to_q = lax.rem(q + 2 * c + 3, 4)
    from_q = lax.rem(q + 5 - 2 * c, 4)
    net = Net(send_sems, recv_sems)
    locals_ = []

    def local(src, dst):
        copy = pltpu.make_async_copy(src, dst, local_sems.at[len(locals_)])
        copy.start()
        locals_.append(copy)
        return copy

    greet(
        [core, mate, twin] + plane + far
        + [at(mate_z, to_q * 2 + c), at(mate_z, from_q * 2 + c)]
    )

    wr = W.shape[0] // 2
    piece = wr // 4
    chunks = 3
    step = piece // chunks
    wsend = []
    for i in range(chunks):
        wsend.append(net.send(
            w_ref.at[rows_at(c * wr + q * piece + i * step, step)],
            W.at[rows_at(kind * wr + q * piece + i * step, step)], twin))
    own_w = local(w_ref.at[rows_at(c * wr, wr)], W.at[rows_at(kind * wr, wr)])

    def spread_out(src, dst, edge, window):
        mine = rows_at(edge + frames * c, frames)
        rim = rows_at((1 - c) * (edge + span), edge)
        rim_src = rows_at(c * (frames - edge), edge)
        here, there = window(half), window(1 - half)
        rims = [
            net.send(src.at[rim_src, there], dst.at[jo, rim], at(mate_z, to_q * 2 + c)),
            net.send(src.at[rim_src, here], dst.at[jo, rim], at(z, to_q * 2 + c)),
        ]
        main = net.send(src.at[:, there], dst.at[jo, mine], mate)
        own = local(src.at[:, here], dst.at[jo, mine])
        return rims, main, own, net.send(src.at[:, here], dst.at[jo, mine], core)

    def pass_on(parts, dst, edge):
        rims, main, own, over = parts
        mine = rows_at(edge + frames * c, frames)
        rim = rows_at((1 - c) * (edge + span), edge)
        got = [over]
        for copy, j, where in ((rims[1], jo, rim), (rims[0], jm, rim), (main, jm, mine)):
            copy.wait_recv()
            ref = dst.at[j, where]
            got.append(net.send(ref, ref, core))
        return got

    r_parts = spread_out(res_ref, R, HALO, lambda h: pl.ds(0, width))
    passed_w = []
    for i in range(chunks):
        wsend[i].wait_recv()
        ref = W.at[rows_at((1 - kind) * wr + q * piece + i * step, step)]
        for peer in plane:
            passed_w.append(net.send(ref, ref, peer))
    r_got = pass_on(r_parts, R, HALO)
    o_parts = spread_out(og_ref, O, EDGE, lambda h: cols_at(h * hw, hw))
    for copy in passed_w:
        copy.wait_recv()
    x_main = net.send(res_ref, X.at[jo, rows_at(frames * c, frames)], twin)
    for copy in r_got:
        copy.wait_recv()
    own_w.wait()
    r_parts[2].wait()

    blocks = wr // 128
    chan = (half * 2 + c) * wr
    lens = [len_ref[kind * 2 + j] for j in range(2)]

    def mask_rows(j, edge, rows):
        frame = q * span - edge + lax.broadcasted_iota(jnp.int32, (rows, 128), 0)
        length = jnp.where(j == 0, lens[0], lens[1])
        return (frame >= 0) & (frame < length)

    long = span + 2 * HALO
    mid = span + 2 * EDGE

    @pl.loop(0, 2)
    def _(j):
        pre = lax.dot_general(
            R[j], W[...], (((1,), (1,)), ((), ())), preferred_element_type=F32
        )
        keep = mask_rows(j, HALO, long)
        for b in range(blocks):
            lin = pre[:, b * 128:(b + 1) * 128]
            sig = jax.nn.sigmoid(pre[:, wr + b * 128:wr + (b + 1) * 128])
            G[j, b] = jnp.where(keep, lin * sig, 0.0).astype(BF).astype(F32)
            A[j, b] = lin[HALO:HALO + span]
            S[j, b] = sig[HALO:HALO + span]

    def count_at(pair, chip, j):
        n = jnp.clip(len_ref[pair * 2 + j] - chip * span, 0, span)
        return jnp.full((8, 128), n, jnp.int32).astype(F32)

    own_counts = [count_at(kind, q, j) for j in range(2)]

    @pl.loop(0, 2 * blocks)
    def _(t):
        j, b = t // blocks, lax.rem(t, blocks)
        lanes = cols_at(chan + b * 128, 128)
        acc = jnp.zeros((mid, 128), F32)
        for k in range(TAPS):
            acc = acc + ck_ref[k:k + 1, lanes] * G[j, b, pl.ds(1 + k, mid), :]
        C[j, b] = acc
        keep = mask_rows(j, 0, span)
        own = acc[EDGE:EDGE + span]
        total = jnp.sum(jnp.where(keep, own, 0.0), axis=0, keepdims=True)
        n = jnp.where(j == 0, own_counts[0][0:1], own_counts[1][0:1])
        dev = jnp.where(keep, own - total / jnp.maximum(n, 1.0), 0.0)
        st1[j, pl.ds(b, 1), :] = total
        st1[j, pl.ds(blocks + b, 1), :] = jnp.sum(dev * dev, axis=0, keepdims=True)

    me8 = kind * 4 + q
    peers8 = plane + [twin] + far

    def exchange(src, slots):
        own = local(src, slots.at[me8])
        copies = [net.send(src, slots.at[me8], peer) for peer in peers8]
        return own, copies

    own, copies = exchange(st1, sb1)
    o_got = pass_on(o_parts, O, EDGE)
    own.wait()
    for copy in copies:
        copy.wait_recv()
    counted = jnp.zeros((8, 128), F32)
    for g in range(len_ref.shape[0]):
        counted = counted + jnp.full((8, 128), len_ref[g], jnp.int32).astype(F32)
    total = jnp.zeros((8, 128), F32)
    for i in range(8):
        for j in range(2):
            total = total + sb1[i, j]
    mean = total / counted
    shift2 = jnp.zeros((8, 128), F32)
    for i in range(8):
        for j in range(2):
            n = count_at(i // 4, i % 4, j)
            d = sb1[i, j] / jnp.maximum(n, 1.0) - mean
            shift2 = shift2 + n * (d * d)
    vec[0] = total
    vec[1] = shift2
    var = (vec[0, blocks:2 * blocks] + vec[1, 0:blocks]) / counted[0:blocks]
    vec[2] = mean
    vec[3, 0:blocks] = lax.rsqrt(var + EPS)

    for copy in o_got:
        copy.wait_recv()
    o_parts[2].wait()

    @pl.loop(0, 2 * blocks)
    def _(t):
        j, b = t // blocks, lax.rem(t, blocks)
        lanes = cols_at(chan + b * 128, 128)
        normed = (C[j, b] - vec[2, pl.ds(b, 1), :]) * vec[3, pl.ds(b, 1), :]
        shaped = gain_ref[0:1, lanes] * normed + shift_ref[0:1, lanes]
        smooth = jax.nn.sigmoid(shaped)
        up = O[j, :, cols_at(c * wr + b * 128, 128)].astype(F32)
        gs = jnp.where(
            mask_rows(j, EDGE, mid), up * smooth * (1.0 + shaped * (1.0 - smooth)), 0.0
        )
        D[j, b] = gs
        own = gs[EDGE:EDGE + span]
        st1_rows = jnp.sum(own, axis=0, keepdims=True)
        gain_rows = jnp.sum(own * normed[EDGE:EDGE + span], axis=0, keepdims=True)
        st2[1 + j, pl.ds(b, 1), :] = st1_rows
        st2[1 + j, pl.ds(blocks + b, 1), :] = gain_rows

    st2[0] = st2[1] + st2[2]
    own, copies = exchange(st2.at[0], sb2)

    x_main.wait_recv()
    x_ref = X.at[jo, rows_at(frames * c, frames)]
    x_mate = net.send(x_ref, x_ref, mate)
    x_got = [net.send(x_ref, x_ref, core)]

    own.wait()
    for copy in copies:
        copy.wait_recv()
    sums = jnp.zeros((8, 128), F32)
    for i in range(8):
        sums = sums + sb2[i]
    vec[4] = sums

    @pl.loop(0, 2 * blocks)
    def _(t):
        j, b = t // blocks, lax.rem(t, blocks)
        lanes = cols_at(chan + b * 128, 128)
        inverse = vec[3, pl.ds(b, 1), :]
        normed = (C[j, b] - vec[2, pl.ds(b, 1), :]) * inverse
        add, mul = vec[4, pl.ds(b, 1), :], vec[4, pl.ds(blocks + b, 1), :]
        D[j, b] = jnp.where(
            mask_rows(j, EDGE, mid),
            gain_ref[0:1, lanes] * inverse * (D[j, b] - (add + normed * mul) / counted[0:1]),
            0.0,
        )

    def back(b):
        lanes = cols_at(chan + b * 128, 128)

        @pl.loop(0, 2)
        def _(j):
            acc = jnp.zeros((span, 128), F32)
            for k in range(TAPS):
                acc = acc + ck_ref[k:k + 1, lanes] * D[j, b, pl.ds(TAPS - k, span), :]
            acc = jnp.where(mask_rows(j, 0, span), acc, 0.0)
            sig = S[j, b]
            to_lin = acc * sig
            GP[j, :, b * 128:(b + 1) * 128] = to_lin.astype(BF)
            GP[j, :, wr + b * 128:wr + (b + 1) * 128] = (
                to_lin * A[j, b] * (1.0 - sig)
            ).astype(BF)

        return net.send(
            GP.at[:, :, cols_at((1 - kind) * wr + b * 128, 128)],
            Y.at[:, :, pl.ds(b * 128, 128)], twin)

    y_got = [back(b) for b in range(blocks)]

    tile = 512

    @pl.loop(0, 2 * (width // tile))
    def _(t):
        j, n = t // (width // tile), lax.rem(t, width // tile)
        lanes = cols_at(n * tile, tile)
        part = jnp.dot(GP[j], W[:, lanes], preferred_element_type=F32)
        igp[j, :, lanes] = part

    igs[...] = igp[:, rows_at((1 - c) * frames, frames), :].astype(BF)
    ig_core = net.send(igs, igr, core)

    x_mate.wait_recv()
    x_ref = X.at[jm, rows_at(frames * c, frames)]
    x_got.append(net.send(x_ref, x_ref, core))

    @pl.loop(0, blocks)
    def _(b):
        for k in range(TAPS):
            part = jnp.zeros((1, 128), F32)
            for j in range(2):
                part = part + jnp.sum(
                    D[j, b, pl.ds(EDGE, span), :] * G[j, b, pl.ds(EDGE + 1 + k, span), :],
                    axis=0, keepdims=True)
            kp[k // 4, b, k % 4:k % 4 + 1, :] = part
        kp[7, b, 3:4, :] = jnp.zeros((1, 128), F32)

    kown = local(kp.at[me8], kb.at[me8])
    k_idx = [kind * 4 + chip_at(dy, dx) for dy, dx in offsets]
    k_idx += [(1 - kind) * 4 + q] + [(1 - kind) * 4 + chip_at(dy, dx) for dy, dx in offsets]
    k_got = [net.send(kp.at[i], kb.at[me8], peer) for i, peer in zip(k_idx, peers8)]

    for copy in x_got:
        copy.wait_recv()

    eh = hw
    colsA, colsB = pl.ds(0, eh), pl.ds(eh, eh)

    def s1(b):
        y_got[b].wait_recv()

        @pl.loop(0, width // tile)
        def _(n):
            lanes = cols_at(n * tile, tile)
            acc = jnp.zeros((128, tile), F32)
            for j in range(2):
                mine = GP[j, :, cols_at(kind * wr + b * 128, 128)]
                acc = acc + lax.dot_general(
                    mine, R[j, pl.ds(HALO, span), lanes], (((0,), (0,)), ((), ())),
                    preferred_element_type=F32)
                acc = acc + lax.dot_general(
                    Y[j, :, b * 128:(b + 1) * 128], X[j, :, lanes], (((0,), (0,)), ((), ())),
                    preferred_element_type=F32)
            P[b, :, lanes] = acc

        sa[b, 0] = P[b, rows_at((1 - x) * 64, 64), 0:eh].astype(BF)
        sa[b, 1] = P[b, rows_at((1 - y) * 64, 64), eh:2 * eh].astype(BF)
        return [net.send(sa.at[b, 0], ra.at[b, 0], px), net.send(sa.at[b, 1], ra.at[b, 1], py)]

    def s2(b, got):
        for copy in got:
            copy.wait_recv()
        sa2[b, 0] = (
            P[b, rows_at(x * 64 + (1 - y) * 32, 32), 0:eh]
            + ra[b, 0, rows_at((1 - y) * 32, 32), :].astype(F32)).astype(BF)
        sa2[b, 1] = (
            P[b, rows_at(y * 64 + (1 - x) * 32, 32), eh:2 * eh]
            + ra[b, 1, rows_at((1 - x) * 32, 32), :].astype(F32)).astype(BF)
        return [net.send(sa2.at[b, 0], ra2.at[b, 0], py), net.send(sa2.at[b, 1], ra2.at[b, 1], px)]

    def s3(b, got):
        for copy in got:
            copy.wait_recv()
        rA, rB = rows_at(x * 64 + y * 32, 32), rows_at(y * 64 + x * 32, 32)
        F[c, b, rA, 0:eh] = (
            P[b, rA, 0:eh] + ra[b, 0, rows_at(y * 32, 32), :].astype(F32)
            + ra2[b, 0].astype(F32)).astype(BF)
        F[c, b, rB, eh:2 * eh] = (
            P[b, rB, eh:2 * eh] + ra[b, 1, rows_at(x * 32, 32), :].astype(F32)
            + ra2[b, 1].astype(F32)).astype(BF)
        fA, fB = F.at[c, b, rA, colsA], F.at[c, b, rB, colsB]
        return [net.send(fA, fA, py), net.send(fB, fB, px)]

    def s4(b, got):
        for copy in got:
            copy.wait_recv()
        fA, fB = F.at[c, b, rows_at(x * 64, 64), colsA], F.at[c, b, rows_at(y * 64, 64), colsB]
        return [net.send(fA, fA, px), net.send(fB, fB, py)]

    def s5(b, got):
        for copy in got:
            copy.wait_recv()
        ref = F.at[c, b]
        return [net.send(ref, ref, core)]

    def s6(b, got):
        wg_ref[rows_at(c * wr + b * 128, 128), :] = F[c, b].astype(F32)
        for copy in got:
            copy.wait_recv()
        wg_ref[rows_at((1 - c) * wr + b * 128, 128), :] = F[1 - c, b].astype(F32)

    def k1():
        kown.wait()
        for copy in k_got:
            copy.wait_recv()
        hc = half * 2 + c
        for b in range(blocks):
            part = jnp.zeros((8, 128), F32)
            for i in range(8):
                part = part + kb[i, b]
            kf_ref[hc, me8, b] = part
            kf_ref[hc, me8, b, 4:5, :] = vec[4, b:b + 1, :]
            kf_ref[hc, me8, b, 5:6, :] = vec[4, blocks + b:blocks + b + 1, :]
        ref = kf_ref.at[hc, me8]
        return [net.send(ref, ref, peer) for peer in peers8]

    def k2(got):
        for copy in got:
            copy.wait_recv()
        ref = kf_ref.at[half * 2 + c]
        return [net.send(ref, ref, core)]

    def k3(got):
        for copy in got:
            copy.wait_recv()
        ref = kf_ref.at[pl.ds(half * 2, 2)]
        return [net.send(ref, ref, mate)]

    def i1():
        ig_core.wait_recv()
        igs2[...] = (
            igp[jm, rows_at(c * frames, frames), :] + igr[jm].astype(F32)
        ).astype(BF)
        return [net.send(igs2, igr2, mate)]

    def i2(got):
        for copy in got:
            copy.wait_recv()
        ig_ref[...] = (
            igp[jo, rows_at(c * frames, frames), :] + igr[jo].astype(F32) + igr2[...].astype(F32)
        ).astype(BF)

    stages = [lambda b, g: s1(b), s2, s3, s4, s5, s6]
    state = [None] * blocks
    side = None
    for wave in range(blocks + len(stages) - 1):
        for b in range(blocks):
            if 0 <= wave - b < len(stages):
                state[b] = stages[wave - b](b, state[b])
        if wave == 0:
            ig_got = i1()
        elif wave == 1:
            side = k1()
        elif wave == 2:
            side = k2(side)
        elif wave == 3:
            side = k3(side)
        elif wave == 4:
            i2(ig_got)
    for copy in side:
        copy.wait_recv()
    net.drain()


def fused(lengths, in_weight, restored, out_grad, conv_kernel, bn_gain, bn_shift):
    frames, width = restored.shape
    wr = width // 4
    blocks = wr // 128
    span = 2 * frames
    long, mid = span + 2 * HALO, span + 2 * EDGE
    dma = pltpu.SemaphoreType.DMA
    hbm = pl.BlockSpec(memory_space=pl.ANY)
    smem = pl.BlockSpec(memory_space=pltpu.SMEM)

    def vm(shape, dtype=F32):
        return pltpu.VMEM(shape, dtype)

    return pl.pallas_call(
        fused_kernel,
        out_shape=(
            jax.ShapeDtypeStruct((frames, width), BF),
            jax.ShapeDtypeStruct((2 * wr, width), F32),
            jax.ShapeDtypeStruct((4, 8, blocks, 8, 128), F32),
        ),
        in_specs=[smem, hbm, VM, VM, VM, VM, VM],
        out_specs=(VM, VM, VM),
        scratch_shapes=[
            vm((2 * wr, width), BF),
            vm((2, long, width), BF),
            vm((2, mid, width // 2), BF),
            vm((2, span, width), BF),
            vm((2, blocks, long, 128)),
            vm((2, blocks, span, 128)),
            vm((2, blocks, span, 128)),
            vm((2, blocks, mid, 128)),
            vm((2, blocks, mid, 128)),
            vm((2, span, 2 * wr), BF),
            vm((2, span, wr), BF),
            vm((2, 8, 128)),
            vm((8, 2, 8, 128)),
            vm((3, 8, 128)),
            vm((8, 8, 128)),
            vm((5, 8, 128)),
            vm((8, blocks, 8, 128)),
            vm((8, blocks, 8, 128)),
            vm((2, span, width)),
            vm((2, frames, width), BF),
            vm((2, frames, width), BF),
            vm((frames, width), BF),
            vm((frames, width), BF),
            vm((blocks, 128, width)),
            vm((blocks, 2, 64, width // 2), BF),
            vm((blocks, 2, 64, width // 2), BF),
            vm((blocks, 2, 32, width // 2), BF),
            vm((blocks, 2, 32, width // 2), BF),
            vm((2, blocks, 128, width), BF),
            dma((128,)),
            dma((128,)),
            dma((8,)),
        ],
        compiler_params=pltpu.CompilerParams(
            collective_id=4, has_side_effects=True, vmem_limit_bytes=56 * 1024 * 1024
        ),
    )(lengths, in_weight, restored, out_grad, conv_kernel, bn_gain, bn_shift)


def padded_2(cells, sides, width):
    for axis, dim in sides:
        count = lax.axis_size(axis)
        ends = count - 1
        head = lax.slice_in_dim(cells, 0, width, axis=dim)
        tail = lax.slice_in_dim(cells, cells.shape[dim] - width, cells.shape[dim], axis=dim)
        cells = jnp.concatenate(
            [
                lax.ppermute(tail, axis, [(i, (i + 1) % count) for i in range(ends)]),
                cells,
                lax.ppermute(head, axis, [((i + 1) % count, i) for i in range(ends)]),
            ],
            axis=dim,
        )
    return cells


def restore(quantized, scales):
    per_channel = jnp.repeat(scales.T, 128, axis=1)
    return (quantized.astype(jnp.float32) * per_channel).astype(jnp.bfloat16)


def depthwise(padded, kernel, frames):
    running = jnp.zeros((frames, padded.shape[1]), jnp.float32)
    for offset in range(kernel.shape[0]):
        running = running + kernel[offset] * padded[offset : offset + frames].astype(jnp.float32)
    return running


def general(
    saved_codes, code_scales, lengths, in_weight, conv_kernel, bn_gain, bn_shift, out_grad
):
    frames = saved_codes.shape[1]
    feature_width = saved_codes.shape[2]
    tap_count = conv_kernel.shape[0]
    half_span = (tap_count - 1) // 2
    groups = lengths.shape[0]
    group_at = lax.axis_index("dp")
    length = jnp.sum(jnp.where(jnp.arange(groups, dtype=jnp.int32) == group_at, lengths, 0))
    counted = jnp.sum(lengths).astype(jnp.float32)
    first_frame = lax.axis_index("seq") * frames
    valid_mask = (first_frame + jnp.arange(frames, dtype=jnp.int32) < length).astype(jnp.float32)[
        :, None
    ]
    restored = restore(saved_codes[0], code_scales[0])
    weights = lax.all_gather(in_weight, "dp", axis=0, tiled=True)
    pre_act = lax.dot_general(
        restored, weights, (((1,), (1,)), ((), ())), preferred_element_type=jnp.float32
    )
    linear = pre_act[:, :feature_width]
    gate_part = jax.nn.sigmoid(pre_act[:, feature_width:])
    gated = (linear * gate_part * valid_mask).astype(jnp.bfloat16)
    gated_pad = padded_2(gated, (("seq", 0),), half_span)
    conv_out = depthwise(gated_pad, conv_kernel, frames)
    own_sum = jnp.sum(conv_out * valid_mask, axis=0)
    own_count = jnp.sum(valid_mask)
    centered = (conv_out - own_sum / jnp.maximum(own_count, 1.0)) * valid_mask
    own_square = jnp.sum(centered * centered, axis=0)
    total, spread, _ = sum_all(
        [own_sum, own_square, jnp.full_like(own_sum, own_count)], True, 0
    )
    mean_value = total / counted
    variance = spread / counted
    inverse = lax.rsqrt(variance + EPS)
    normed = (conv_out - mean_value) * inverse
    shaped = bn_gain * normed + bn_shift
    smooth = jax.nn.sigmoid(shaped)
    grad_shaped = (
        out_grad[0].astype(jnp.float32) * valid_mask * smooth * (1.0 + shaped * (1.0 - smooth))
    )
    shift_grad, gain_grad = sum_all(
        [jnp.sum(grad_shaped, axis=0), jnp.sum(grad_shaped * normed, axis=0)], False, 1
    )
    grad_conv = (
        bn_gain * inverse * (grad_shaped - (shift_grad + normed * gain_grad) / counted) * valid_mask
    )
    kernel_part = jnp.stack(
        [
            jnp.sum(grad_conv * gated_pad[offset : offset + frames].astype(jnp.float32), axis=0)
            for offset in range(tap_count)
        ]
    )
    grad_pad = padded_2(grad_conv, (("seq", 0),), half_span)
    grad_gated = depthwise(grad_pad, conv_kernel[::-1], frames) * valid_mask
    grad_pre = jnp.concatenate(
        [grad_gated * gate_part, grad_gated * linear * gate_part * (1.0 - gate_part)], axis=1
    ).astype(jnp.bfloat16)
    in_grad = jnp.dot(grad_pre, weights, preferred_element_type=jnp.float32)
    own_columns = lax.all_to_all(grad_pre[None], "dp", split_axis=2, concat_axis=0, tiled=True)
    local_rows = lax.dot_general(
        own_columns,
        lax.all_gather(restored[None], "dp", axis=0, tiled=True),
        (((0, 1), (0, 1)), ((), ())),
        preferred_element_type=jnp.float32,
    )
    weight_grad = lax.psum(local_rows, "seq")
    kernel_grad = lax.psum(kernel_part, ("dp", "seq"))
    return (in_grad.astype(jnp.bfloat16)[None], weight_grad, kernel_grad, gain_grad, shift_grad)


def per_device(
    saved_codes, code_scales, lengths, in_weight, conv_kernel, bn_gain, bn_shift, out_grad
):
    frames, width = saved_codes.shape[1:]
    square = (
        lax.axis_size("dp") == 4 and lax.axis_size("seq") == 8 and frames == 128
        and width == 1536 and conv_kernel.shape[0] == TAPS and lengths.shape[0] == 4
    )
    if not square:
        return general(
            saved_codes, code_scales, lengths, in_weight, conv_kernel, bn_gain, bn_shift, out_grad
        )
    restored = restore(saved_codes[0], code_scales[0])
    in_grad, weight_grad, taps = fused(
        lengths, in_weight, restored, out_grad[0], conv_kernel, bn_gain[None], bn_shift[None]
    )
    blocks = width // 4 // 128
    by_row = jnp.transpose(taps, (1, 3, 0, 2, 4)).reshape(8, 8, width)
    kernel_grad = by_row[:, :4].reshape(32, width)[:TAPS]
    return in_grad[None], weight_grad, kernel_grad, by_row[0, 5], by_row[0, 4]


def solution(mesh):
    in_specs = (
        P("dp", "seq", None),
        P("dp", None, "seq"),
        P(),
        P("dp", None),
        P(),
        P(),
        P(),
        P("dp", "seq", None),
    )
    out_specs = (P("dp", "seq", None), P("dp", None), P(), P(), P())
    return jax.shard_map(
        per_device, mesh=mesh, in_specs=in_specs, out_specs=out_specs, check_vma=False
    )
```

```python
import functools

import jax
import jax.numpy as jnp
from jax import lax
from jax.experimental import pallas as pl
from jax.experimental.pallas import tpu as pltpu
from jax.sharding import PartitionSpec as P

EPS = 1e-05
MESH = pl.DeviceIdType.MESH
VM = pl.BlockSpec(memory_space=pltpu.VMEM)


def at(d, s):
    return {"dp": d, "seq": s}


def greet(peers):
    barrier = pltpu.get_barrier_semaphore()
    for peer in peers:
        pl.semaphore_signal(barrier, inc=1, device_id=peer, device_id_type=MESH)
    pl.semaphore_wait(barrier, len(peers))


def remote(src, dst, send, recv, peer):
    return pltpu.make_async_remote_copy(
        src_ref=src, dst_ref=dst, send_sem=send, recv_sem=recv, device_id=peer, device_id_type=MESH
    )


def ring_peers(me, count):
    return [lax.rem(me + k, count) for k in range(1, count)]


def merge(parts, stats):
    if not stats:
        return functools.reduce(lambda a, b: a + b, parts)
    sums = [part[0:16] for part in parts]
    squares = [part[16:32] for part in parts]
    counts = [part[32:48] for part in parts]
    total = functools.reduce(lambda a, b: a + b, sums)
    count = functools.reduce(lambda a, b: a + b, counts)
    mean = total / jnp.maximum(count, 1.0)
    spread = functools.reduce(lambda a, b: a + b, squares)
    for own, n in zip(sums, counts):
        shift = own / jnp.maximum(n, 1.0) - mean
        spread = spread + n * (shift * shift)
    return jnp.concatenate([total, spread, count], axis=0)


def sum_kernel(stats, dp_n, seq_n, x_ref, o_ref, near, far, mid, s1, r1, s2, r2):
    d, s = lax.axis_index("dp"), lax.axis_index("seq")
    plane = ring_peers(s, seq_n)
    line = ring_peers(d, dp_n)
    greet([at(d, j) for j in plane] + [at(j, s) for j in line])
    for k, j in enumerate(plane):
        remote(x_ref, near.at[s], s1.at[k], r1.at[s], at(d, j)).start()
    near[s] = x_ref[...]
    for k, j in enumerate(plane):
        copy = remote(x_ref, near.at[j], s1.at[k], r1.at[j], at(d, j))
        copy.wait_recv()
        copy.wait_send()
    mid[...] = merge([near[j] for j in range(seq_n)], stats)
    for k, j in enumerate(line):
        remote(mid, far.at[d], s2.at[k], r2.at[d], at(j, s)).start()
    far[d] = mid[...]
    for k, j in enumerate(line):
        copy = remote(mid, far.at[j], s2.at[k], r2.at[j], at(j, s))
        copy.wait_recv()
        copy.wait_send()
    o_ref[...] = merge([far[j] for j in range(dp_n)], stats)


def sum_all(vectors, stats, collective_id):
    dp_n, seq_n = lax.axis_size("dp"), lax.axis_size("seq")
    blocks = vectors[0].shape[-1] // 128
    stacked = jnp.stack([v.reshape(blocks, 128) for v in vectors])
    stacked = jnp.pad(stacked, ((0, 0), (0, 16 - blocks), (0, 0)))
    rows = 16 * len(vectors)
    shape = (rows, 128)
    out = pl.pallas_call(
        functools.partial(sum_kernel, stats, dp_n, seq_n),
        out_shape=jax.ShapeDtypeStruct(shape, jnp.float32),
        in_specs=[VM],
        out_specs=VM,
        scratch_shapes=[
            pltpu.VMEM((seq_n,) + shape, jnp.float32),
            pltpu.VMEM((dp_n,) + shape, jnp.float32),
            pltpu.VMEM(shape, jnp.float32),
            pltpu.SemaphoreType.DMA((seq_n,)),
            pltpu.SemaphoreType.DMA((seq_n,)),
            pltpu.SemaphoreType.DMA((dp_n,)),
            pltpu.SemaphoreType.DMA((dp_n,)),
        ],
        compiler_params=pltpu.CompilerParams(collective_id=collective_id, has_side_effects=True),
    )(stacked.reshape(shape))
    return out.reshape(len(vectors), 16, 128)[:, :blocks].reshape(len(vectors), blocks * 128)


HALO = 32
EDGE = 16
TAPS = 31
BF = jnp.bfloat16
F32 = jnp.float32


class Net:
    def __init__(self, send_sems, recv_sems):
        self.send_sems, self.recv_sems = send_sems, recv_sems
        self.used = 0
        self.sent = []

    def send(self, src, dst, peer):
        copy = remote(src, dst, self.send_sems.at[self.used], self.recv_sems.at[self.used], peer)
        self.used += 1
        copy.start()
        self.sent.append(copy)
        return copy

    def drain(self):
        for copy in self.sent:
            copy.wait_send()


def rows_at(start, size):
    return pl.ds(pl.multiple_of(start, 16), size)


def cols_at(start, size):
    return pl.ds(pl.multiple_of(start, 128), size)


def fused_kernel(
    len_ref, w_ref, codes_ref, scale_ref, og_ref, ck_ref, gain_ref, shift_ref,
    ig_ref, F, kf_ref,
    res_ref, by_frame, W, R, O, G, A, S, C, D, GP,
    st1, sb1, st2, sb2, vec,
    kp, kb,
    igp, igs, igr, igs2, igr2,
    P, sa, ra, sa2, ra2, sz, rz,
    send_sems, recv_sems, local_sems,
):
    z, s = lax.axis_index("dp"), lax.axis_index("seq")
    c, x, y = lax.rem(s, 2), lax.rem(s // 2, 2), s // 4
    q = s // 2
    kind, half = z // 2, lax.rem(z, 2)
    mate_z = z + 1 - 2 * half
    twin_z = z + 2 - 4 * kind
    jo, jm = half, 1 - half
    frames = codes_ref.shape[0]
    span = 2 * frames
    width = codes_ref.shape[1]
    hw = width // 2

    def chip_at(dy, dx):
        yy = 1 - y if dy else y
        xx = 1 - x if dx else x
        return yy * 2 + xx

    core = at(z, s + 1 - 2 * c)
    mate = at(mate_z, s)
    twin = at(twin_z, s)
    offsets = [(0, 1), (1, 0), (1, 1)]
    plane = [at(z, chip_at(dy, dx) * 2 + c) for dy, dx in offsets]
    px, py = plane[0], plane[1]
    far = [at(twin_z, chip_at(dy, dx) * 2 + c) for dy, dx in offsets]
    to_q = lax.rem(q + 2 * c + 3, 4)
    from_q = lax.rem(q + 5 - 2 * c, 4)
    net = Net(send_sems, recv_sems)
    locals_ = []

    def local(src, dst):
        copy = pltpu.make_async_copy(src, dst, local_sems.at[len(locals_)])
        copy.start()
        locals_.append(copy)
        return copy

    for b in range(width // 128):
        by_frame[b:b + 1, :] = scale_ref[b]
    columns = jnp.transpose(by_frame[...])
    for b in range(width // 128):
        lanes = pl.ds(b * 128, 128)
        res_ref[:, lanes] = (
            codes_ref[:, lanes].astype(F32) * columns[:, b:b + 1]
        ).astype(BF)

    greet([core, mate, twin] + plane + far)

    def spread_out(src, dst, edge, window):
        mine = rows_at(edge + frames * c, frames)
        rim_src = rows_at(c * (frames - edge), edge)
        rim_dst = rows_at(edge + frames * c + c * (frames - edge), edge)
        rim = rows_at((1 - c) * (edge + span), edge)
        rest_src = rows_at((1 - c) * edge, frames - edge)
        rest_dst = rows_at(edge + frames * c + (1 - c) * edge, frames - edge)
        here, there = window(half), window(1 - half)
        side = net.send(src.at[rim_src, there], dst.at[jo, rim_dst], mate)
        rim_own = net.send(src.at[rim_src, here], dst.at[jo, rim], at(z, to_q * 2 + c))
        own = local(src.at[:, here], dst.at[jo, mine])

        def rest():
            return net.send(src.at[rest_src, there], dst.at[jo, rest_dst], mate)

        def over():
            return net.send(src.at[:, here], dst.at[jo, mine], core)

        return side, rim_own, own, rest, over

    def rims_on(parts, dst, edge):
        rim_dst = rows_at(edge + frames * c + c * (frames - edge), edge)
        rim = rows_at((1 - c) * (edge + span), edge)
        side, rim_own = parts[:2]
        side.wait_recv()
        rim_mate = net.send(dst.at[jm, rim_dst], dst.at[jm, rim], at(z, to_q * 2 + c))
        rim_own.wait_recv()
        ref = dst.at[jo, rim]
        return rim_mate, net.send(ref, ref, core)

    def mate_on(rest, rim_mate, dst, edge):
        rim = rows_at((1 - c) * (edge + span), edge)
        rim_mate.wait_recv()
        ref = dst.at[jm, rim]
        got = [net.send(ref, ref, core)]
        rest.wait_recv()
        ref = dst.at[jm, rows_at(edge + frames * c, frames)]
        return got + [net.send(ref, ref, core)]

    r_parts = spread_out(res_ref, R, HALO, lambda h: pl.ds(0, width))

    wr = W.shape[0] // 2
    piece = wr // 4
    chunks = 3
    step = piece // chunks
    wsend = []
    for i in range(chunks):
        wsend.append(net.send(
            w_ref.at[rows_at(c * wr + q * piece + i * step, step)],
            W.at[rows_at(kind * wr + q * piece + i * step, step)], twin))
    own_w = local(w_ref.at[rows_at(c * wr, wr)], W.at[rows_at(kind * wr, wr)])
    r_rest = r_parts[3]()
    r_over = r_parts[4]()
    r_rim_mate, r_rim_core = rims_on(r_parts, R, HALO)
    passed_w = []
    for i in range(chunks):
        wsend[i].wait_recv()
        ref = W.at[rows_at((1 - kind) * wr + q * piece + i * step, step)]
        for peer in plane:
            passed_w.append(net.send(ref, ref, peer))
    o_parts = spread_out(og_ref, O, EDGE, lambda h: cols_at(h * hw, hw))
    o_rest = o_parts[3]()
    o_over = o_parts[4]()
    for copy in passed_w:
        copy.wait_recv()
    own_w.wait()
    r_parts[2].wait()
    r_over.wait_recv()
    r_rim_core.wait_recv()

    blocks = wr // 128
    chan = (half * 2 + c) * wr
    lens = [len_ref[kind * 2 + j] for j in range(2)]

    def mask_rows(j, edge, rows):
        frame = q * span - edge + lax.broadcasted_iota(jnp.int32, (rows, 128), 0)
        length = jnp.where(j == 0, lens[0], lens[1])
        return (frame >= 0) & (frame < length)

    long = span + 2 * HALO
    mid = span + 2 * EDGE

    def project(j):
        pre = lax.dot_general(
            R[j], W[...], (((1,), (1,)), ((), ())), preferred_element_type=F32
        )
        keep = mask_rows(j, HALO, long)
        for b in range(blocks):
            lin = pre[:, b * 128:(b + 1) * 128]
            sig = jax.nn.sigmoid(pre[:, wr + b * 128:wr + (b + 1) * 128])
            G[j, b] = jnp.where(keep, lin * sig, 0.0).astype(BF).astype(F32)
            A[j, b] = lin[HALO:HALO + span]
            S[j, b] = sig[HALO:HALO + span]

    def count_at(pair, chip, j):
        n = jnp.clip(len_ref[pair * 2 + j] - chip * span, 0, span)
        return jnp.full((8, 128), n, jnp.int32).astype(F32)

    own_counts = [count_at(kind, q, j) for j in range(2)]

    def convolve(j, b):
        lanes = cols_at(chan + b * 128, 128)
        acc = jnp.zeros((mid, 128), F32)
        for k in range(TAPS):
            acc = acc + ck_ref[k:k + 1, lanes] * G[j, b, pl.ds(1 + k, mid), :]
        C[j, b] = acc
        keep = mask_rows(j, 0, span)
        own = acc[EDGE:EDGE + span]
        total = jnp.sum(jnp.where(keep, own, 0.0), axis=0, keepdims=True)
        n = jnp.where(j == 0, own_counts[0][0:1], own_counts[1][0:1])
        dev = jnp.where(keep, own - total / jnp.maximum(n, 1.0), 0.0)
        st1[j, pl.ds(b, 1), :] = total
        st1[j, pl.ds(blocks + b, 1), :] = jnp.sum(dev * dev, axis=0, keepdims=True)

    @pl.loop(0, 1)
    def _(_i):
        project(jo)

    @pl.loop(0, blocks)
    def _(b):
        convolve(jo, b)

    for copy in mate_on(r_rest, r_rim_mate, R, HALO):
        copy.wait_recv()
    o_rim_mate, o_rim_core = rims_on(o_parts, O, EDGE)

    @pl.loop(0, 1)
    def _(_i):
        project(jm)

    @pl.loop(0, blocks)
    def _(b):
        convolve(jm, b)

    me8 = kind * 4 + q
    peers8 = plane + [twin] + far

    def exchange(src, slots):
        own = local(src, slots.at[me8])
        copies = [net.send(src, slots.at[me8], peer) for peer in peers8]
        return own, copies

    own, copies = exchange(st1, sb1)
    o_got = mate_on(o_rest, o_rim_mate, O, EDGE)
    own.wait()
    for copy in copies:
        copy.wait_recv()
    counted = jnp.zeros((8, 128), F32)
    for g in range(len_ref.shape[0]):
        counted = counted + jnp.full((8, 128), len_ref[g], jnp.int32).astype(F32)
    total = jnp.zeros((8, 128), F32)
    for i in range(8):
        for j in range(2):
            total = total + sb1[i, j]
    mean = total / counted
    shift2 = jnp.zeros((8, 128), F32)
    for i in range(8):
        for j in range(2):
            n = count_at(i // 4, i % 4, j)
            d = sb1[i, j] / jnp.maximum(n, 1.0) - mean
            shift2 = shift2 + n * (d * d)
    vec[0] = total
    vec[1] = shift2
    var = (vec[0, blocks:2 * blocks] + vec[1, 0:blocks]) / counted[0:blocks]
    vec[2] = mean
    vec[3, 0:blocks] = lax.rsqrt(var + EPS)

    for copy in o_got + [o_over, o_rim_core]:
        copy.wait_recv()
    o_parts[2].wait()

    @pl.loop(0, 2 * blocks)
    def _(t):
        j, b = t // blocks, lax.rem(t, blocks)
        lanes = cols_at(chan + b * 128, 128)
        normed = (C[j, b] - vec[2, pl.ds(b, 1), :]) * vec[3, pl.ds(b, 1), :]
        shaped = gain_ref[lanes][None] * normed + shift_ref[lanes][None]
        smooth = jax.nn.sigmoid(shaped)
        up = O[j, :, cols_at(c * wr + b * 128, 128)].astype(F32)
        gs = jnp.where(
            mask_rows(j, EDGE, mid), up * smooth * (1.0 + shaped * (1.0 - smooth)), 0.0
        )
        D[j, b] = gs
        own = gs[EDGE:EDGE + span]
        st1_rows = jnp.sum(own, axis=0, keepdims=True)
        gain_rows = jnp.sum(own * normed[EDGE:EDGE + span], axis=0, keepdims=True)
        st2[1 + j, pl.ds(b, 1), :] = st1_rows
        st2[1 + j, pl.ds(blocks + b, 1), :] = gain_rows

    st2[0] = st2[1] + st2[2]
    own, copies = exchange(st2.at[0], sb2)

    own.wait()
    for copy in copies:
        copy.wait_recv()
    sums = jnp.zeros((8, 128), F32)
    for i in range(8):
        sums = sums + sb2[i]
    vec[4] = sums

    @pl.loop(0, 2 * blocks)
    def _(t):
        j, b = t // blocks, lax.rem(t, blocks)
        lanes = cols_at(chan + b * 128, 128)
        inverse = vec[3, pl.ds(b, 1), :]
        normed = (C[j, b] - vec[2, pl.ds(b, 1), :]) * inverse
        add, mul = vec[4, pl.ds(b, 1), :], vec[4, pl.ds(blocks + b, 1), :]
        D[j, b] = jnp.where(
            mask_rows(j, EDGE, mid),
            gain_ref[lanes][None] * inverse * (D[j, b] - (add + normed * mul) / counted[0:1]),
            0.0,
        )

    def back(b):
        lanes = cols_at(chan + b * 128, 128)

        @pl.loop(0, 2)
        def _(j):
            acc = jnp.zeros((span, 128), F32)
            for k in range(TAPS):
                acc = acc + ck_ref[k:k + 1, lanes] * D[j, b, pl.ds(TAPS - k, span), :]
            acc = jnp.where(mask_rows(j, 0, span), acc, 0.0)
            sig = S[j, b]
            to_lin = acc * sig
            GP[j, :, b * 128:(b + 1) * 128] = to_lin.astype(BF)
            GP[j, :, wr + b * 128:wr + (b + 1) * 128] = (
                to_lin * A[j, b] * (1.0 - sig)
            ).astype(BF)

    tile = 512

    def input_grad():
        @pl.loop(0, 2 * (width // tile))
        def _(t):
            j, n = t // (width // tile), lax.rem(t, width // tile)
            lanes = cols_at(n * tile, tile)
            part = jnp.dot(GP[j], W[:, lanes], preferred_element_type=F32)
            igp[j, :, lanes] = part

        igs[...] = igp[:, rows_at((1 - c) * frames, frames), :].astype(BF)
        return net.send(igs, igr, core)

    def taps():
        @pl.loop(0, blocks)
        def _(b):
            for k in range(TAPS):
                part = jnp.zeros((1, 128), F32)
                for j in range(2):
                    part = part + jnp.sum(
                        D[j, b, pl.ds(EDGE, span), :] * G[j, b, pl.ds(EDGE + 1 + k, span), :],
                        axis=0, keepdims=True)
                kp[k // 4, b, k % 4:k % 4 + 1, :] = part
            kp[7, b, 3:4, :] = jnp.zeros((1, 128), F32)

        own = local(kp.at[me8], kb.at[me8])
        index = [kind * 4 + chip_at(dy, dx) for dy, dx in offsets]
        index += [(1 - kind) * 4 + i for i in [q] + [chip_at(dy, dx) for dy, dx in offsets]]
        return own, [net.send(kp.at[i], kb.at[me8], peer) for i, peer in zip(index, peers8)]

    eh = hw
    colsA, colsB = pl.ds(0, eh), pl.ds(eh, eh)

    def s1(m, b):
        rows = cols_at((kind if m else 1 - kind) * wr + b * 128, 128)

        @pl.loop(0, width // tile)
        def _(n):
            lanes = cols_at(n * tile, tile)
            acc = jnp.zeros((128, tile), F32)
            for j in range(2):
                acc = acc + lax.dot_general(
                    GP[j, :, rows], R[j, pl.ds(HALO, span), lanes], (((0,), (0,)), ((), ())),
                    preferred_element_type=F32)
            P[m, b, :, lanes] = acc

        sa[m, b, 0] = P[m, b, rows_at((1 - x) * 64, 64), 0:eh].astype(BF)
        sa[m, b, 1] = P[m, b, rows_at((1 - y) * 64, 64), eh:2 * eh].astype(BF)
        return [
            net.send(sa.at[m, b, 0], ra.at[m, b, 0], px),
            net.send(sa.at[m, b, 1], ra.at[m, b, 1], py),
        ]

    def s2(m, b, got):
        for copy in got:
            copy.wait_recv()
        sa2[m, b, 0] = (
            P[m, b, rows_at(x * 64 + (1 - y) * 32, 32), 0:eh]
            + ra[m, b, 0, rows_at((1 - y) * 32, 32), :].astype(F32)).astype(BF)
        sa2[m, b, 1] = (
            P[m, b, rows_at(y * 64 + (1 - x) * 32, 32), eh:2 * eh]
            + ra[m, b, 1, rows_at((1 - x) * 32, 32), :].astype(F32)).astype(BF)
        return [
            net.send(sa2.at[m, b, 0], ra2.at[m, b, 0], py),
            net.send(sa2.at[m, b, 1], ra2.at[m, b, 1], px),
        ]

    row_a, row_b = x * 64 + y * 32, y * 64 + x * 32

    def summed(m, b):
        return (
            P[m, b, rows_at(row_a, 32), 0:eh] + ra[m, b, 0, rows_at(y * 32, 32), :].astype(F32)
            + ra2[m, b, 0].astype(F32),
            P[m, b, rows_at(row_b, 32), eh:2 * eh] + ra[m, b, 1, rows_at(x * 32, 32), :].astype(F32)
            + ra2[m, b, 1].astype(F32),
        )

    def to_twin(b, got):
        for copy in got:
            copy.wait_recv()
        part_a, part_b = summed(0, b)
        sz[b, 0] = part_a.astype(BF)
        sz[b, 1] = part_b.astype(BF)
        return net.send(sz.at[b], rz.at[b], twin)

    def tile_of(core_at, b, start, size, cols):
        return F.at[rows_at(core_at * wr + b * 128 + start, size), cols]

    cols_a, cols_b = pl.ds(0, eh), pl.ds(eh, eh)

    def s3(b, got, from_twin):
        for copy in got:
            copy.wait_recv()
        part_a, part_b = summed(1, b)
        from_twin.wait_recv()
        fa, fb = tile_of(c, b, row_a, 32, cols_a), tile_of(c, b, row_b, 32, cols_b)
        fa[...] = (part_a + rz[b, 0].astype(F32)).astype(BF)
        fb[...] = (part_b + rz[b, 1].astype(F32)).astype(BF)
        return [net.send(fa, fa, py), net.send(fb, fb, px)]

    def s4(b, got):
        for copy in got:
            copy.wait_recv()
        fa, fb = tile_of(c, b, x * 64, 64, cols_a), tile_of(c, b, y * 64, 64, cols_b)
        return [net.send(fa, fa, px), net.send(fb, fb, py)]

    def s5(b, got):
        for copy in got:
            copy.wait_recv()
        ref = tile_of(c, b, 0, 128, pl.ds(0, width))
        return [net.send(ref, ref, core)]

    def k1(own, got):
        own.wait()
        for copy in got:
            copy.wait_recv()
        hc = half * 2 + c
        for b in range(blocks):
            part = jnp.zeros((8, 128), F32)
            for i in range(8):
                part = part + kb[i, b]
            kf_ref[hc, me8, b] = part
            kf_ref[hc, me8, b, 4:5, :] = vec[4, b:b + 1, :]
            kf_ref[hc, me8, b, 5:6, :] = vec[4, blocks + b:blocks + b + 1, :]
        ref = kf_ref.at[hc, me8]
        return [net.send(ref, ref, peer) for peer in peers8]

    def k2(got):
        for copy in got:
            copy.wait_recv()
        ref = kf_ref.at[half * 2 + c]
        return [net.send(ref, ref, core)]

    def k3(got):
        for copy in got:
            copy.wait_recv()
        ref = kf_ref.at[pl.ds(half * 2, 2)]
        return [net.send(ref, ref, mate)]

    def i1(got):
        got.wait_recv()
        igs2[...] = (
            igp[jm, rows_at(c * frames, frames), :] + igr[jm].astype(F32)
        ).astype(BF)
        return net.send(igs2, igr2, mate)

    def i2(got):
        got.wait_recv()
        ig_ref[...] = (
            igp[jo, rows_at(c * frames, frames), :] + igr[jo].astype(F32) + igr2[...].astype(F32)
        ).astype(BF)

    back(0)
    o0 = s1(0, 0)
    back(1)
    o1 = s1(0, 1)
    o0 = s2(0, 0, o0)
    back(2)
    o2 = s1(0, 2)
    o1 = s2(0, 1, o1)
    w0 = s1(1, 0)
    t0 = to_twin(0, o0)
    o2 = s2(0, 2, o2)
    w1 = s1(1, 1)
    w0 = s2(1, 0, w0)
    t1 = to_twin(1, o1)
    w2 = s1(1, 2)
    ig = input_grad()
    w1 = s2(1, 1, w1)
    t2 = to_twin(2, o2)
    ig = i1(ig)
    kown, k = taps()
    w0 = s3(0, w0, t0)
    w2 = s2(1, 2, w2)
    w1 = s3(1, w1, t1)
    w0 = s4(0, w0)
    k = k1(kown, k)
    w2 = s3(2, w2, t2)
    w1 = s4(1, w1)
    w0 = s5(0, w0)
    k = k2(k)
    w2 = s4(2, w2)
    w1 = s5(1, w1)
    k = k3(k)
    i2(ig)
    w2 = s5(2, w2)
    for copy in w0 + w1 + w2 + k:
        copy.wait_recv()
    net.drain()


def finish_kernel(ig_in, wg_in, kf_in, ig_out, wg_out, taps_out, gain_out, shift_out, wide, sems):
    copies = []

    def put(src, dst):
        copy = pltpu.make_async_copy(src, dst, sems.at[len(copies)])
        copy.start()
        copies.append(copy)

    put(ig_in, ig_out)
    parts = 6
    rows = wg_in.shape[0] // parts
    for i in range(parts):
        where = pl.ds(i * rows, rows)
        wide[where, :] = wg_in[where, :].astype(F32)
        put(wide.at[where], wg_out.at[where])
    owners, blocks = kf_in.shape[1], kf_in.shape[2]
    for hc in range(4):
        for b in range(blocks):
            lanes = pl.ds((hc * blocks + b) * 128, 128)
            for i in range(owners):
                n = min(4, taps_out.shape[0] - 4 * i)
                taps_out[4 * i:4 * i + n, lanes] = kf_in[hc, i, b, 0:n, :]
            shift_out[lanes] = kf_in[hc, 0, b, 4, :]
            gain_out[lanes] = kf_in[hc, 0, b, 5, :]
    for copy in copies:
        copy.wait()


def finish(in_grad, weight_grad, taps):
    any_space = pl.BlockSpec(memory_space=pl.ANY)
    width = in_grad.shape[1]
    return pl.pallas_call(
        finish_kernel,
        out_shape=(
            jax.ShapeDtypeStruct(in_grad.shape, BF),
            jax.ShapeDtypeStruct(weight_grad.shape, F32),
            jax.ShapeDtypeStruct((TAPS, width), F32),
            jax.ShapeDtypeStruct((width,), F32),
            jax.ShapeDtypeStruct((width,), F32),
        ),
        in_specs=[VM, VM, VM],
        out_specs=(any_space, any_space, VM, VM, VM),
        scratch_shapes=[pltpu.VMEM(weight_grad.shape, F32), pltpu.SemaphoreType.DMA((8,))],
        compiler_params=pltpu.CompilerParams(vmem_limit_bytes=20 * 1024 * 1024),
    )(in_grad, weight_grad, taps)


def fused(lengths, in_weight, codes, scales, out_grad, conv_kernel, bn_gain, bn_shift):
    frames, width = codes.shape
    wr = width // 4
    blocks = wr // 128
    span = 2 * frames
    long, mid = span + 2 * HALO, span + 2 * EDGE
    dma = pltpu.SemaphoreType.DMA
    hbm = pl.BlockSpec(memory_space=pl.ANY)
    smem = pl.BlockSpec(memory_space=pltpu.SMEM)

    def vm(shape, dtype=F32):
        return pltpu.VMEM(shape, dtype)

    return pl.pallas_call(
        fused_kernel,
        out_shape=(
            jax.ShapeDtypeStruct((frames, width), BF),
            jax.ShapeDtypeStruct((2 * wr, width), BF),
            jax.ShapeDtypeStruct((4, 8, blocks, 8, 128), F32),
        ),
        in_specs=[smem, hbm, VM, VM, VM, VM, VM, VM],
        out_specs=(VM, VM, VM),
        scratch_shapes=[
            vm((frames, width), BF),
            vm((128, 128)),
            vm((2 * wr, width), BF),
            vm((2, long, width), BF),
            vm((2, mid, width // 2), BF),
            vm((2, blocks, long, 128)),
            vm((2, blocks, span, 128)),
            vm((2, blocks, span, 128)),
            vm((2, blocks, mid, 128)),
            vm((2, blocks, mid, 128)),
            vm((2, span, 2 * wr), BF),
            vm((2, 8, 128)),
            vm((8, 2, 8, 128)),
            vm((3, 8, 128)),
            vm((8, 8, 128)),
            vm((5, 8, 128)),
            vm((8, blocks, 8, 128)),
            vm((8, blocks, 8, 128)),
            vm((2, span, width)),
            vm((2, frames, width), BF),
            vm((2, frames, width), BF),
            vm((frames, width), BF),
            vm((frames, width), BF),
            vm((2, blocks, 128, width)),
            vm((2, blocks, 2, 64, width // 2), BF),
            vm((2, blocks, 2, 64, width // 2), BF),
            vm((2, blocks, 2, 32, width // 2), BF),
            vm((2, blocks, 2, 32, width // 2), BF),
            vm((blocks, 2, 32, width // 2), BF),
            vm((blocks, 2, 32, width // 2), BF),
            dma((128,)),
            dma((128,)),
            dma((8,)),
        ],
        compiler_params=pltpu.CompilerParams(
            collective_id=4, has_side_effects=True, vmem_limit_bytes=36 * 1024 * 1024
        ),
    )(lengths, in_weight, codes, scales, out_grad, conv_kernel, bn_gain, bn_shift)


def padded_2(cells, sides, width):
    for axis, dim in sides:
        count = lax.axis_size(axis)
        ends = count - 1
        head = lax.slice_in_dim(cells, 0, width, axis=dim)
        tail = lax.slice_in_dim(cells, cells.shape[dim] - width, cells.shape[dim], axis=dim)
        cells = jnp.concatenate(
            [
                lax.ppermute(tail, axis, [(i, (i + 1) % count) for i in range(ends)]),
                cells,
                lax.ppermute(head, axis, [((i + 1) % count, i) for i in range(ends)]),
            ],
            axis=dim,
        )
    return cells


def restore(quantized, scales):
    per_channel = jnp.repeat(scales.T, 128, axis=1)
    return (quantized.astype(jnp.float32) * per_channel).astype(jnp.bfloat16)


def depthwise(padded, kernel, frames):
    running = jnp.zeros((frames, padded.shape[1]), jnp.float32)
    for offset in range(kernel.shape[0]):
        running = running + kernel[offset] * padded[offset : offset + frames].astype(jnp.float32)
    return running


def general(
    saved_codes, code_scales, lengths, in_weight, conv_kernel, bn_gain, bn_shift, out_grad
):
    frames = saved_codes.shape[1]
    feature_width = saved_codes.shape[2]
    tap_count = conv_kernel.shape[0]
    half_span = (tap_count - 1) // 2
    groups = lengths.shape[0]
    group_at = lax.axis_index("dp")
    length = jnp.sum(jnp.where(jnp.arange(groups, dtype=jnp.int32) == group_at, lengths, 0))
    counted = jnp.sum(lengths).astype(jnp.float32)
    first_frame = lax.axis_index("seq") * frames
    valid_mask = (first_frame + jnp.arange(frames, dtype=jnp.int32) < length).astype(jnp.float32)[
        :, None
    ]
    restored = restore(saved_codes[0], code_scales[0])
    weights = lax.all_gather(in_weight, "dp", axis=0, tiled=True)
    pre_act = lax.dot_general(
        restored, weights, (((1,), (1,)), ((), ())), preferred_element_type=jnp.float32
    )
    linear = pre_act[:, :feature_width]
    gate_part = jax.nn.sigmoid(pre_act[:, feature_width:])
    gated = (linear * gate_part * valid_mask).astype(jnp.bfloat16)
    gated_pad = padded_2(gated, (("seq", 0),), half_span)
    conv_out = depthwise(gated_pad, conv_kernel, frames)
    own_sum = jnp.sum(conv_out * valid_mask, axis=0)
    own_count = jnp.sum(valid_mask)
    centered = (conv_out - own_sum / jnp.maximum(own_count, 1.0)) * valid_mask
    own_square = jnp.sum(centered * centered, axis=0)
    total, spread, _ = sum_all(
        [own_sum, own_square, jnp.full_like(own_sum, own_count)], True, 0
    )
    mean_value = total / counted
    variance = spread / counted
    inverse = lax.rsqrt(variance + EPS)
    normed = (conv_out - mean_value) * inverse
    shaped = bn_gain * normed + bn_shift
    smooth = jax.nn.sigmoid(shaped)
    grad_shaped = (
        out_grad[0].astype(jnp.float32) * valid_mask * smooth * (1.0 + shaped * (1.0 - smooth))
    )
    shift_grad, gain_grad = sum_all(
        [jnp.sum(grad_shaped, axis=0), jnp.sum(grad_shaped * normed, axis=0)], False, 1
    )
    grad_conv = (
        bn_gain * inverse * (grad_shaped - (shift_grad + normed * gain_grad) / counted) * valid_mask
    )
    kernel_part = jnp.stack(
        [
            jnp.sum(grad_conv * gated_pad[offset : offset + frames].astype(jnp.float32), axis=0)
            for offset in range(tap_count)
        ]
    )
    grad_pad = padded_2(grad_conv, (("seq", 0),), half_span)
    grad_gated = depthwise(grad_pad, conv_kernel[::-1], frames) * valid_mask
    grad_pre = jnp.concatenate(
        [grad_gated * gate_part, grad_gated * linear * gate_part * (1.0 - gate_part)], axis=1
    ).astype(jnp.bfloat16)
    in_grad = jnp.dot(grad_pre, weights, preferred_element_type=jnp.float32)
    own_columns = lax.all_to_all(grad_pre[None], "dp", split_axis=2, concat_axis=0, tiled=True)
    local_rows = lax.dot_general(
        own_columns,
        lax.all_gather(restored[None], "dp", axis=0, tiled=True),
        (((0, 1), (0, 1)), ((), ())),
        preferred_element_type=jnp.float32,
    )
    weight_grad = lax.psum(local_rows, "seq")
    kernel_grad = lax.psum(kernel_part, ("dp", "seq"))
    return (in_grad.astype(jnp.bfloat16)[None], weight_grad, kernel_grad, gain_grad, shift_grad)


def per_device(
    saved_codes, code_scales, lengths, in_weight, conv_kernel, bn_gain, bn_shift, out_grad
):
    frames, width = saved_codes.shape[1:]
    square = (
        lax.axis_size("dp") == 4 and lax.axis_size("seq") == 8 and frames == 128
        and width == 1536 and conv_kernel.shape[0] == TAPS and lengths.shape[0] == 4
    )
    if not square:
        return general(
            saved_codes, code_scales, lengths, in_weight, conv_kernel, bn_gain, bn_shift, out_grad
        )
    in_grad, weight_grad, taps = fused(
        lengths, in_weight, saved_codes[0], jnp.transpose(code_scales, (1, 0, 2)), out_grad[0],
        conv_kernel, bn_gain, bn_shift
    )
    in_grad, weight_grad, kernel_grad, gain_grad, shift_grad = finish(in_grad, weight_grad, taps)
    return in_grad[None], weight_grad, kernel_grad, gain_grad, shift_grad


def solution(mesh):
    in_specs = (
        P("dp", "seq", None),
        P("dp", None, "seq"),
        P(),
        P("dp", None),
        P(),
        P(),
        P(),
        P("dp", "seq", None),
    )
    out_specs = (P("dp", "seq", None), P("dp", None), P(), P(), P())
    return jax.shard_map(
        per_device, mesh=mesh, in_specs=in_specs, out_specs=out_specs, check_vma=False
    )
```

```python
import functools

import jax
import jax.numpy as jnp
from jax import lax
from jax.experimental import pallas as pl
from jax.experimental.pallas import tpu as pltpu
from jax.sharding import PartitionSpec as P

EPS = 1e-05
MESH = pl.DeviceIdType.MESH
VM = pl.BlockSpec(memory_space=pltpu.VMEM)


def at(d, s):
    return {"dp": d, "seq": s}


def greet(peers):
    barrier = pltpu.get_barrier_semaphore()
    for peer in peers:
        pl.semaphore_signal(barrier, inc=1, device_id=peer, device_id_type=MESH)
    pl.semaphore_wait(barrier, len(peers))


def remote(src, dst, send, recv, peer):
    return pltpu.make_async_remote_copy(
        src_ref=src, dst_ref=dst, send_sem=send, recv_sem=recv, device_id=peer, device_id_type=MESH
    )


def ring_peers(me, count):
    return [lax.rem(me + k, count) for k in range(1, count)]


def merge(parts, stats):
    if not stats:
        return functools.reduce(lambda a, b: a + b, parts)
    sums = [part[0:16] for part in parts]
    squares = [part[16:32] for part in parts]
    counts = [part[32:48] for part in parts]
    total = functools.reduce(lambda a, b: a + b, sums)
    count = functools.reduce(lambda a, b: a + b, counts)
    mean = total / jnp.maximum(count, 1.0)
    spread = functools.reduce(lambda a, b: a + b, squares)
    for own, n in zip(sums, counts):
        shift = own / jnp.maximum(n, 1.0) - mean
        spread = spread + n * (shift * shift)
    return jnp.concatenate([total, spread, count], axis=0)


def sum_kernel(stats, dp_n, seq_n, x_ref, o_ref, near, far, mid, s1, r1, s2, r2):
    d, s = lax.axis_index("dp"), lax.axis_index("seq")
    plane = ring_peers(s, seq_n)
    line = ring_peers(d, dp_n)
    greet([at(d, j) for j in plane] + [at(j, s) for j in line])
    for k, j in enumerate(plane):
        remote(x_ref, near.at[s], s1.at[k], r1.at[s], at(d, j)).start()
    near[s] = x_ref[...]
    for k, j in enumerate(plane):
        copy = remote(x_ref, near.at[j], s1.at[k], r1.at[j], at(d, j))
        copy.wait_recv()
        copy.wait_send()
    mid[...] = merge([near[j] for j in range(seq_n)], stats)
    for k, j in enumerate(line):
        remote(mid, far.at[d], s2.at[k], r2.at[d], at(j, s)).start()
    far[d] = mid[...]
    for k, j in enumerate(line):
        copy = remote(mid, far.at[j], s2.at[k], r2.at[j], at(j, s))
        copy.wait_recv()
        copy.wait_send()
    o_ref[...] = merge([far[j] for j in range(dp_n)], stats)


def sum_all(vectors, stats, collective_id):
    dp_n, seq_n = lax.axis_size("dp"), lax.axis_size("seq")
    blocks = vectors[0].shape[-1] // 128
    stacked = jnp.stack([v.reshape(blocks, 128) for v in vectors])
    stacked = jnp.pad(stacked, ((0, 0), (0, 16 - blocks), (0, 0)))
    rows = 16 * len(vectors)
    shape = (rows, 128)
    out = pl.pallas_call(
        functools.partial(sum_kernel, stats, dp_n, seq_n),
        out_shape=jax.ShapeDtypeStruct(shape, jnp.float32),
        in_specs=[VM],
        out_specs=VM,
        scratch_shapes=[
            pltpu.VMEM((seq_n,) + shape, jnp.float32),
            pltpu.VMEM((dp_n,) + shape, jnp.float32),
            pltpu.VMEM(shape, jnp.float32),
            pltpu.SemaphoreType.DMA((seq_n,)),
            pltpu.SemaphoreType.DMA((seq_n,)),
            pltpu.SemaphoreType.DMA((dp_n,)),
            pltpu.SemaphoreType.DMA((dp_n,)),
        ],
        compiler_params=pltpu.CompilerParams(collective_id=collective_id, has_side_effects=True),
    )(stacked.reshape(shape))
    return out.reshape(len(vectors), 16, 128)[:, :blocks].reshape(len(vectors), blocks * 128)


HALO = 32
EDGE = 16
TAPS = 31
BF = jnp.bfloat16
F32 = jnp.float32


class Net:
    def __init__(self, send_sems, recv_sems):
        self.send_sems, self.recv_sems = send_sems, recv_sems
        self.used = 0
        self.sent = []

    def send(self, src, dst, peer):
        copy = remote(src, dst, self.send_sems.at[self.used], self.recv_sems.at[self.used], peer)
        self.used += 1
        copy.start()
        self.sent.append(copy)
        return copy

    def drain(self):
        for copy in self.sent:
            copy.wait_send()


def rows_at(start, size):
    return pl.ds(pl.multiple_of(start, 16), size)


def cols_at(start, size):
    return pl.ds(pl.multiple_of(start, 128), size)


def fused_kernel(
    len_ref, w_ref, codes_hbm, scale_hbm, og_ref, ck_hbm, gain_hbm, shift_hbm,
    ig_ref, F, kf_ref,
    codes_ref, scale_ref, ck_ref, gain_ref, shift_ref, res_ref, by_frame, W, R, O, G, A, S, C, D, GP,
    st1, sb1, st2, sb2, vec,
    kp, kb,
    igp, igs, igr, igs2, igr2,
    P, sa, ra, sa2, ra2, sz, rz,
    send_sems, recv_sems, local_sems,
):
    z, s = lax.axis_index("dp"), lax.axis_index("seq")
    c, x, y = lax.rem(s, 2), lax.rem(s // 2, 2), s // 4
    q = s // 2
    kind, half = z // 2, lax.rem(z, 2)
    mate_z = z + 1 - 2 * half
    twin_z = z + 2 - 4 * kind
    jo, jm = half, 1 - half
    frames = codes_hbm.shape[0]
    span = 2 * frames
    width = codes_hbm.shape[1]
    hw = width // 2

    def chip_at(dy, dx):
        yy = 1 - y if dy else y
        xx = 1 - x if dx else x
        return yy * 2 + xx

    core = at(z, s + 1 - 2 * c)
    mate = at(mate_z, s)
    twin = at(twin_z, s)
    offsets = [(0, 1), (1, 0), (1, 1)]
    plane = [at(z, chip_at(dy, dx) * 2 + c) for dy, dx in offsets]
    px, py = plane[0], plane[1]
    far = [at(twin_z, chip_at(dy, dx) * 2 + c) for dy, dx in offsets]
    to_q = lax.rem(q + 2 * c + 3, 4)
    from_q = lax.rem(q + 5 - 2 * c, 4)
    net = Net(send_sems, recv_sems)
    locals_ = []

    def local(src, dst):
        copy = pltpu.make_async_copy(src, dst, local_sems.at[len(locals_)])
        copy.start()
        locals_.append(copy)
        return copy

    loads = [
        local(src, dst) for src, dst in (
            (codes_hbm, codes_ref), (scale_hbm, scale_ref), (ck_hbm, ck_ref),
            (gain_hbm, gain_ref), (shift_hbm, shift_ref))
    ]
    wr = W.shape[0] // 2
    own_w = local(w_ref.at[rows_at(c * wr, wr)], W.at[rows_at(kind * wr, wr)])
    greet([core, mate, twin] + plane + far)

    def spread_out(src, dst, edge, window):
        mine = rows_at(edge + frames * c, frames)
        rim_src = rows_at(c * (frames - edge), edge)
        rim_dst = rows_at(edge + frames * c + c * (frames - edge), edge)
        rim = rows_at((1 - c) * (edge + span), edge)
        rest_src = rows_at((1 - c) * edge, frames - edge)
        rest_dst = rows_at(edge + frames * c + (1 - c) * edge, frames - edge)
        here, there = window(half), window(1 - half)
        side = net.send(src.at[rim_src, there], dst.at[jo, rim_dst], mate)
        rim_own = net.send(src.at[rim_src, here], dst.at[jo, rim], at(z, to_q * 2 + c))
        own = local(src.at[:, here], dst.at[jo, mine])

        def rest():
            return net.send(src.at[rest_src, there], dst.at[jo, rest_dst], mate)

        def over():
            return net.send(src.at[:, here], dst.at[jo, mine], core)

        return side, rim_own, own, rest, over

    def rims_on(parts, dst, edge):
        rim_dst = rows_at(edge + frames * c + c * (frames - edge), edge)
        rim = rows_at((1 - c) * (edge + span), edge)
        side, rim_own = parts[:2]
        side.wait_recv()
        rim_mate = net.send(dst.at[jm, rim_dst], dst.at[jm, rim], at(z, to_q * 2 + c))
        rim_own.wait_recv()
        ref = dst.at[jo, rim]
        return rim_mate, net.send(ref, ref, core)

    def mate_on(rest, rim_mate, dst, edge):
        rim = rows_at((1 - c) * (edge + span), edge)
        rim_mate.wait_recv()
        ref = dst.at[jm, rim]
        got = [net.send(ref, ref, core)]
        rest.wait_recv()
        ref = dst.at[jm, rows_at(edge + frames * c, frames)]
        return got + [net.send(ref, ref, core)]

    piece = wr // 4
    chunks = 3
    step = piece // chunks
    wsend = []
    for i in range(chunks):
        wsend.append(net.send(
            w_ref.at[rows_at(c * wr + q * piece + i * step, step)],
            W.at[rows_at(kind * wr + q * piece + i * step, step)], twin))
    for copy in loads:
        copy.wait()
    for b in range(width // 128):
        by_frame[b:b + 1, :] = scale_ref[b]
    columns = jnp.transpose(by_frame[...])
    for b in range(width // 128):
        lanes = pl.ds(b * 128, 128)
        res_ref[:, lanes] = (
            codes_ref[:, lanes].astype(F32) * columns[:, b:b + 1]
        ).astype(BF)

    r_parts = spread_out(res_ref, R, HALO, lambda h: pl.ds(0, width))
    r_over = r_parts[4]()
    passed_w = []
    for i in range(chunks):
        wsend[i].wait_recv()
        ref = W.at[rows_at((1 - kind) * wr + q * piece + i * step, step)]
        for peer in plane:
            passed_w.append(net.send(ref, ref, peer))
        if i == 0:
            r_rest = r_parts[3]()
            r_rim_mate, r_rim_core = rims_on(r_parts, R, HALO)
    for copy in passed_w:
        copy.wait_recv()
    own_w.wait()
    r_parts[2].wait()
    r_over.wait_recv()
    r_rim_core.wait_recv()

    blocks = wr // 128
    chan = (half * 2 + c) * wr
    lens = [len_ref[kind * 2 + j] for j in range(2)]

    def mask_rows(j, edge, rows):
        frame = q * span - edge + lax.broadcasted_iota(jnp.int32, (rows, 128), 0)
        length = jnp.where(j == 0, lens[0], lens[1])
        return (frame >= 0) & (frame < length)

    long = span + 2 * HALO
    mid = span + 2 * EDGE

    def project(j):
        pre = lax.dot_general(
            R[j], W[...], (((1,), (1,)), ((), ())), preferred_element_type=F32
        )
        keep = mask_rows(j, HALO, long)
        for b in range(blocks):
            lin = pre[:, b * 128:(b + 1) * 128]
            sig = jax.nn.sigmoid(pre[:, wr + b * 128:wr + (b + 1) * 128])
            G[j, b] = jnp.where(keep, lin * sig, 0.0).astype(BF).astype(F32)
            A[j, b] = lin[HALO:HALO + span]
            S[j, b] = sig[HALO:HALO + span]

    def count_at(pair, chip, j):
        n = jnp.clip(len_ref[pair * 2 + j] - chip * span, 0, span)
        return jnp.full((8, 128), n, jnp.int32).astype(F32)

    own_counts = [count_at(kind, q, j) for j in range(2)]

    def convolve(j, b):
        lanes = cols_at(chan + b * 128, 128)
        acc = jnp.zeros((mid, 128), F32)
        for k in range(TAPS):
            acc = acc + ck_ref[k:k + 1, lanes] * G[j, b, pl.ds(1 + k, mid), :]
        C[j, b] = acc
        keep = mask_rows(j, 0, span)
        own = acc[EDGE:EDGE + span]
        total = jnp.sum(jnp.where(keep, own, 0.0), axis=0, keepdims=True)
        n = jnp.where(j == 0, own_counts[0][0:1], own_counts[1][0:1])
        dev = jnp.where(keep, own - total / jnp.maximum(n, 1.0), 0.0)
        st1[j, pl.ds(b, 1), :] = total
        st1[j, pl.ds(blocks + b, 1), :] = jnp.sum(dev * dev, axis=0, keepdims=True)

    @pl.loop(0, 1)
    def _(_i):
        project(jo)

    @pl.loop(0, blocks)
    def _(b):
        convolve(jo, b)

    o_parts = spread_out(og_ref, O, EDGE, lambda h: cols_at(h * hw, hw))
    o_rest = o_parts[3]()
    o_over = o_parts[4]()
    for copy in mate_on(r_rest, r_rim_mate, R, HALO):
        copy.wait_recv()

    @pl.loop(0, 1)
    def _(_i):
        project(jm)

    o_rim_mate, o_rim_core = rims_on(o_parts, O, EDGE)

    @pl.loop(0, blocks)
    def _(b):
        convolve(jm, b)

    me8 = kind * 4 + q
    peers8 = plane + [twin] + far

    def exchange(src, slots):
        own = local(src, slots.at[me8])
        copies = [net.send(src, slots.at[me8], peer) for peer in peers8]
        return own, copies

    own, copies = exchange(st1, sb1)
    o_got = mate_on(o_rest, o_rim_mate, O, EDGE)
    own.wait()
    for copy in copies:
        copy.wait_recv()
    counted = jnp.zeros((8, 128), F32)
    for g in range(len_ref.shape[0]):
        counted = counted + jnp.full((8, 128), len_ref[g], jnp.int32).astype(F32)
    total = jnp.zeros((8, 128), F32)
    for i in range(8):
        for j in range(2):
            total = total + sb1[i, j]
    mean = total / counted
    shift2 = jnp.zeros((8, 128), F32)
    for i in range(8):
        for j in range(2):
            n = count_at(i // 4, i % 4, j)
            d = sb1[i, j] / jnp.maximum(n, 1.0) - mean
            shift2 = shift2 + n * (d * d)
    vec[0] = total
    vec[1] = shift2
    var = (vec[0, blocks:2 * blocks] + vec[1, 0:blocks]) / counted[0:blocks]
    vec[2] = mean
    vec[3, 0:blocks] = lax.rsqrt(var + EPS)

    for copy in o_got + [o_over, o_rim_core]:
        copy.wait_recv()
    o_parts[2].wait()

    @pl.loop(0, 2 * blocks)
    def _(t):
        j, b = t // blocks, lax.rem(t, blocks)
        lanes = cols_at(chan + b * 128, 128)
        normed = (C[j, b] - vec[2, pl.ds(b, 1), :]) * vec[3, pl.ds(b, 1), :]
        shaped = gain_ref[lanes][None] * normed + shift_ref[lanes][None]
        smooth = jax.nn.sigmoid(shaped)
        up = O[j, :, cols_at(c * wr + b * 128, 128)].astype(F32)
        gs = jnp.where(
            mask_rows(j, EDGE, mid), up * smooth * (1.0 + shaped * (1.0 - smooth)), 0.0
        )
        D[j, b] = gs
        own = gs[EDGE:EDGE + span]
        st1_rows = jnp.sum(own, axis=0, keepdims=True)
        gain_rows = jnp.sum(own * normed[EDGE:EDGE + span], axis=0, keepdims=True)
        st2[1 + j, pl.ds(b, 1), :] = st1_rows
        st2[1 + j, pl.ds(blocks + b, 1), :] = gain_rows

    st2[0] = st2[1] + st2[2]
    own, copies = exchange(st2.at[0], sb2)

    own.wait()
    for copy in copies:
        copy.wait_recv()
    sums = jnp.zeros((8, 128), F32)
    for i in range(8):
        sums = sums + sb2[i]
    vec[4] = sums

    @pl.loop(0, 2 * blocks)
    def _(t):
        j, b = t // blocks, lax.rem(t, blocks)
        lanes = cols_at(chan + b * 128, 128)
        inverse = vec[3, pl.ds(b, 1), :]
        normed = (C[j, b] - vec[2, pl.ds(b, 1), :]) * inverse
        add, mul = vec[4, pl.ds(b, 1), :], vec[4, pl.ds(blocks + b, 1), :]
        D[j, b] = jnp.where(
            mask_rows(j, EDGE, mid),
            gain_ref[lanes][None] * inverse * (D[j, b] - (add + normed * mul) / counted[0:1]),
            0.0,
        )

    def back(b):
        lanes = cols_at(chan + b * 128, 128)

        @pl.loop(0, 2)
        def _(j):
            acc = jnp.zeros((span, 128), F32)
            for k in range(TAPS):
                acc = acc + ck_ref[k:k + 1, lanes] * D[j, b, pl.ds(TAPS - k, span), :]
            acc = jnp.where(mask_rows(j, 0, span), acc, 0.0)
            sig = S[j, b]
            to_lin = acc * sig
            GP[j, :, b * 128:(b + 1) * 128] = to_lin.astype(BF)
            GP[j, :, wr + b * 128:wr + (b + 1) * 128] = (
                to_lin * A[j, b] * (1.0 - sig)
            ).astype(BF)

    tile = 512

    def input_grad():
        @pl.loop(0, 2 * (width // tile))
        def _(t):
            j, n = t // (width // tile), lax.rem(t, width // tile)
            lanes = cols_at(n * tile, tile)
            part = jnp.dot(GP[j], W[:, lanes], preferred_element_type=F32)
            igp[j, :, lanes] = part

        igs[...] = igp[:, rows_at((1 - c) * frames, frames), :].astype(BF)
        return net.send(igs, igr, core)

    def taps():
        @pl.loop(0, blocks)
        def _(b):
            for k in range(TAPS):
                part = jnp.zeros((1, 128), F32)
                for j in range(2):
                    part = part + jnp.sum(
                        D[j, b, pl.ds(EDGE, span), :] * G[j, b, pl.ds(EDGE + 1 + k, span), :],
                        axis=0, keepdims=True)
                kp[k // 4, b, k % 4:k % 4 + 1, :] = part
            kp[7, b, 3:4, :] = jnp.zeros((1, 128), F32)

        own = local(kp.at[me8], kb.at[me8])
        index = [kind * 4 + chip_at(dy, dx) for dy, dx in offsets]
        index += [(1 - kind) * 4 + i for i in [q] + [chip_at(dy, dx) for dy, dx in offsets]]
        return own, [net.send(kp.at[i], kb.at[me8], peer) for i, peer in zip(index, peers8)]

    eh = hw
    colsA, colsB = pl.ds(0, eh), pl.ds(eh, eh)

    def s1(m, b):
        rows = cols_at((kind if m else 1 - kind) * wr + b * 128, 128)

        @pl.loop(0, width // tile)
        def _(n):
            lanes = cols_at(n * tile, tile)
            acc = jnp.zeros((128, tile), F32)
            for j in range(2):
                acc = acc + lax.dot_general(
                    GP[j, :, rows], R[j, pl.ds(HALO, span), lanes], (((0,), (0,)), ((), ())),
                    preferred_element_type=F32)
            P[m, b, :, lanes] = acc

        sa[m, b, 0] = P[m, b, rows_at((1 - x) * 64, 64), 0:eh].astype(BF)
        sa[m, b, 1] = P[m, b, rows_at((1 - y) * 64, 64), eh:2 * eh].astype(BF)
        return [
            net.send(sa.at[m, b, 0], ra.at[m, b, 0], px),
            net.send(sa.at[m, b, 1], ra.at[m, b, 1], py),
        ]

    def s2(m, b, got):
        for copy in got:
            copy.wait_recv()
        sa2[m, b, 0] = (
            P[m, b, rows_at(x * 64 + (1 - y) * 32, 32), 0:eh]
            + ra[m, b, 0, rows_at((1 - y) * 32, 32), :].astype(F32)).astype(BF)
        sa2[m, b, 1] = (
            P[m, b, rows_at(y * 64 + (1 - x) * 32, 32), eh:2 * eh]
            + ra[m, b, 1, rows_at((1 - x) * 32, 32), :].astype(F32)).astype(BF)
        return [
            net.send(sa2.at[m, b, 0], ra2.at[m, b, 0], py),
            net.send(sa2.at[m, b, 1], ra2.at[m, b, 1], px),
        ]

    row_a, row_b = x * 64 + y * 32, y * 64 + x * 32

    def summed(m, b):
        return (
            P[m, b, rows_at(row_a, 32), 0:eh] + ra[m, b, 0, rows_at(y * 32, 32), :].astype(F32)
            + ra2[m, b, 0].astype(F32),
            P[m, b, rows_at(row_b, 32), eh:2 * eh] + ra[m, b, 1, rows_at(x * 32, 32), :].astype(F32)
            + ra2[m, b, 1].astype(F32),
        )

    def to_twin(b, got):
        for copy in got:
            copy.wait_recv()
        part_a, part_b = summed(0, b)
        sz[b, 0] = part_a.astype(BF)
        sz[b, 1] = part_b.astype(BF)
        return net.send(sz.at[b], rz.at[b], twin)

    def tile_of(core_at, b, start, size, cols):
        return F.at[rows_at(core_at * wr + b * 128 + start, size), cols]

    cols_a, cols_b = pl.ds(0, eh), pl.ds(eh, eh)

    def s3(b, got, from_twin):
        for copy in got:
            copy.wait_recv()
        part_a, part_b = summed(1, b)
        from_twin.wait_recv()
        fa, fb = tile_of(c, b, row_a, 32, cols_a), tile_of(c, b, row_b, 32, cols_b)
        fa[...] = (part_a + rz[b, 0].astype(F32)).astype(BF)
        fb[...] = (part_b + rz[b, 1].astype(F32)).astype(BF)
        return [net.send(fa, fa, py), net.send(fb, fb, px)]

    def s4(b, got):
        for copy in got:
            copy.wait_recv()
        fa, fb = tile_of(c, b, x * 64, 64, cols_a), tile_of(c, b, y * 64, 64, cols_b)
        return [net.send(fa, fa, px), net.send(fb, fb, py)]

    def s5(b, got):
        for copy in got:
            copy.wait_recv()
        ref = tile_of(c, b, 0, 128, pl.ds(0, width))
        return [net.send(ref, ref, core)]

    def k1(own, got):
        own.wait()
        for copy in got:
            copy.wait_recv()
        hc = half * 2 + c
        for b in range(blocks):
            part = jnp.zeros((8, 128), F32)
            for i in range(8):
                part = part + kb[i, b]
            kf_ref[hc, me8, b] = part
            kf_ref[hc, me8, b, 4:5, :] = vec[4, b:b + 1, :]
            kf_ref[hc, me8, b, 5:6, :] = vec[4, blocks + b:blocks + b + 1, :]
        ref = kf_ref.at[hc, me8]
        return [net.send(ref, ref, peer) for peer in peers8]

    def k2(got):
        for copy in got:
            copy.wait_recv()
        ref = kf_ref.at[half * 2 + c]
        return [net.send(ref, ref, core)]

    def k3(got):
        for copy in got:
            copy.wait_recv()
        ref = kf_ref.at[pl.ds(half * 2, 2)]
        return [net.send(ref, ref, mate)]

    def i1(got):
        got.wait_recv()
        igs2[...] = (
            igp[jm, rows_at(c * frames, frames), :] + igr[jm].astype(F32)
        ).astype(BF)
        return net.send(igs2, igr2, mate)

    def i2(got):
        got.wait_recv()
        ig_ref[...] = (
            igp[jo, rows_at(c * frames, frames), :] + igr[jo].astype(F32) + igr2[...].astype(F32)
        ).astype(BF)

    back(0)
    o0 = s1(0, 0)
    back(1)
    o1 = s1(0, 1)
    back(2)
    o2 = s1(0, 2)
    o0 = s2(0, 0, o0)
    w0 = s1(1, 0)
    o1 = s2(0, 1, o1)
    w1 = s1(1, 1)
    o2 = s2(0, 2, o2)
    t0 = to_twin(0, o0)
    ig = input_grad()
    w2 = s1(1, 2)
    t1 = to_twin(1, o1)
    w0 = s2(1, 0, w0)
    ig = i1(ig)
    t2 = to_twin(2, o2)
    kown, k = taps()
    w1 = s2(1, 1, w1)
    w2 = s2(1, 2, w2)
    k = k1(kown, k)
    w0 = s3(0, w0, t0)
    w1 = s3(1, w1, t1)
    k = k2(k)
    w0 = s4(0, w0)
    w2 = s3(2, w2, t2)
    w1 = s4(1, w1)
    k = k3(k)
    w0 = s5(0, w0)
    w2 = s4(2, w2)
    w1 = s5(1, w1)
    i2(ig)
    w2 = s5(2, w2)
    for copy in w0 + w1 + w2 + k:
        copy.wait_recv()
    net.drain()


def finish_kernel(ig_in, wg_in, kf_in, ig_out, wg_out, taps_out, gain_out, shift_out, wide, sems):
    copies = []

    def put(src, dst):
        copy = pltpu.make_async_copy(src, dst, sems.at[len(copies)])
        copy.start()
        copies.append(copy)

    put(ig_in, ig_out)
    parts = 6
    rows = wg_in.shape[0] // parts
    for i in range(parts):
        where = pl.ds(i * rows, rows)
        wide[where, :] = wg_in[where, :].astype(F32)
        put(wide.at[where], wg_out.at[where])
    owners, blocks = kf_in.shape[1], kf_in.shape[2]
    for hc in range(4):
        for b in range(blocks):
            lanes = pl.ds((hc * blocks + b) * 128, 128)
            for i in range(owners):
                n = min(4, taps_out.shape[0] - 4 * i)
                taps_out[4 * i:4 * i + n, lanes] = kf_in[hc, i, b, 0:n, :]
            shift_out[lanes] = kf_in[hc, 0, b, 4, :]
            gain_out[lanes] = kf_in[hc, 0, b, 5, :]
    for copy in copies:
        copy.wait()


def finish(in_grad, weight_grad, taps):
    any_space = pl.BlockSpec(memory_space=pl.ANY)
    width = in_grad.shape[1]
    return pl.pallas_call(
        finish_kernel,
        out_shape=(
            jax.ShapeDtypeStruct(in_grad.shape, BF),
            jax.ShapeDtypeStruct(weight_grad.shape, F32),
            jax.ShapeDtypeStruct((TAPS, width), F32),
            jax.ShapeDtypeStruct((width,), F32),
            jax.ShapeDtypeStruct((width,), F32),
        ),
        in_specs=[VM, VM, VM],
        out_specs=(any_space, any_space, VM, VM, VM),
        scratch_shapes=[pltpu.VMEM(weight_grad.shape, F32), pltpu.SemaphoreType.DMA((8,))],
        compiler_params=pltpu.CompilerParams(vmem_limit_bytes=20 * 1024 * 1024),
    )(in_grad, weight_grad, taps)


def fused(lengths, in_weight, codes, scales, out_grad, conv_kernel, bn_gain, bn_shift):
    frames, width = codes.shape
    wr = width // 4
    blocks = wr // 128
    span = 2 * frames
    long, mid = span + 2 * HALO, span + 2 * EDGE
    dma = pltpu.SemaphoreType.DMA
    hbm = pl.BlockSpec(memory_space=pltpu.HBM)
    smem = pl.BlockSpec(memory_space=pltpu.SMEM)

    def vm(shape, dtype=F32):
        return pltpu.VMEM(shape, dtype)

    return pl.pallas_call(
        fused_kernel,
        out_shape=(
            jax.ShapeDtypeStruct((frames, width), BF),
            jax.ShapeDtypeStruct((2 * wr, width), BF),
            jax.ShapeDtypeStruct((4, 8, blocks, 8, 128), F32),
        ),
        in_specs=[smem] + [hbm] * 7,
        out_specs=(VM, VM, VM),
        scratch_shapes=[
            vm((frames, width), BF),
            vm(scales.shape),
            vm(conv_kernel.shape),
            vm(bn_gain.shape),
            vm(bn_shift.shape),
            vm((frames, width), BF),
            vm((128, 128)),
            vm((2 * wr, width), BF),
            vm((2, long, width), BF),
            vm((2, mid, width // 2), BF),
            vm((2, blocks, long, 128)),
            vm((2, blocks, span, 128)),
            vm((2, blocks, span, 128)),
            vm((2, blocks, mid, 128)),
            vm((2, blocks, mid, 128)),
            vm((2, span, 2 * wr), BF),
            vm((2, 8, 128)),
            vm((8, 2, 8, 128)),
            vm((3, 8, 128)),
            vm((8, 8, 128)),
            vm((5, 8, 128)),
            vm((8, blocks, 8, 128)),
            vm((8, blocks, 8, 128)),
            vm((2, span, width)),
            vm((2, frames, width), BF),
            vm((2, frames, width), BF),
            vm((frames, width), BF),
            vm((frames, width), BF),
            vm((2, blocks, 128, width)),
            vm((2, blocks, 2, 64, width // 2), BF),
            vm((2, blocks, 2, 64, width // 2), BF),
            vm((2, blocks, 2, 32, width // 2), BF),
            vm((2, blocks, 2, 32, width // 2), BF),
            vm((blocks, 2, 32, width // 2), BF),
            vm((blocks, 2, 32, width // 2), BF),
            dma((128,)),
            dma((128,)),
            dma((16,)),
        ],
        compiler_params=pltpu.CompilerParams(
            collective_id=4, has_side_effects=True, vmem_limit_bytes=36 * 1024 * 1024
        ),
    )(*[
        pltpu.with_memory_space_constraint(operand, pltpu.HBM)
        for operand in (
            lengths, in_weight, codes, scales, out_grad, conv_kernel, bn_gain, bn_shift)
    ])


def padded_2(cells, sides, width):
    for axis, dim in sides:
        count = lax.axis_size(axis)
        ends = count - 1
        head = lax.slice_in_dim(cells, 0, width, axis=dim)
        tail = lax.slice_in_dim(cells, cells.shape[dim] - width, cells.shape[dim], axis=dim)
        cells = jnp.concatenate(
            [
                lax.ppermute(tail, axis, [(i, (i + 1) % count) for i in range(ends)]),
                cells,
                lax.ppermute(head, axis, [((i + 1) % count, i) for i in range(ends)]),
            ],
            axis=dim,
        )
    return cells


def restore(quantized, scales):
    per_channel = jnp.repeat(scales.T, 128, axis=1)
    return (quantized.astype(jnp.float32) * per_channel).astype(jnp.bfloat16)


def depthwise(padded, kernel, frames):
    running = jnp.zeros((frames, padded.shape[1]), jnp.float32)
    for offset in range(kernel.shape[0]):
        running = running + kernel[offset] * padded[offset : offset + frames].astype(jnp.float32)
    return running


def general(
    saved_codes, code_scales, lengths, in_weight, conv_kernel, bn_gain, bn_shift, out_grad
):
    frames = saved_codes.shape[1]
    feature_width = saved_codes.shape[2]
    tap_count = conv_kernel.shape[0]
    half_span = (tap_count - 1) // 2
    groups = lengths.shape[0]
    group_at = lax.axis_index("dp")
    length = jnp.sum(jnp.where(jnp.arange(groups, dtype=jnp.int32) == group_at, lengths, 0))
    counted = jnp.sum(lengths).astype(jnp.float32)
    first_frame = lax.axis_index("seq") * frames
    valid_mask = (first_frame + jnp.arange(frames, dtype=jnp.int32) < length).astype(jnp.float32)[
        :, None
    ]
    restored = restore(saved_codes[0], code_scales[0])
    weights = lax.all_gather(in_weight, "dp", axis=0, tiled=True)
    pre_act = lax.dot_general(
        restored, weights, (((1,), (1,)), ((), ())), preferred_element_type=jnp.float32
    )
    linear = pre_act[:, :feature_width]
    gate_part = jax.nn.sigmoid(pre_act[:, feature_width:])
    gated = (linear * gate_part * valid_mask).astype(jnp.bfloat16)
    gated_pad = padded_2(gated, (("seq", 0),), half_span)
    conv_out = depthwise(gated_pad, conv_kernel, frames)
    own_sum = jnp.sum(conv_out * valid_mask, axis=0)
    own_count = jnp.sum(valid_mask)
    centered = (conv_out - own_sum / jnp.maximum(own_count, 1.0)) * valid_mask
    own_square = jnp.sum(centered * centered, axis=0)
    total, spread, _ = sum_all(
        [own_sum, own_square, jnp.full_like(own_sum, own_count)], True, 0
    )
    mean_value = total / counted
    variance = spread / counted
    inverse = lax.rsqrt(variance + EPS)
    normed = (conv_out - mean_value) * inverse
    shaped = bn_gain * normed + bn_shift
    smooth = jax.nn.sigmoid(shaped)
    grad_shaped = (
        out_grad[0].astype(jnp.float32) * valid_mask * smooth * (1.0 + shaped * (1.0 - smooth))
    )
    shift_grad, gain_grad = sum_all(
        [jnp.sum(grad_shaped, axis=0), jnp.sum(grad_shaped * normed, axis=0)], False, 1
    )
    grad_conv = (
        bn_gain * inverse * (grad_shaped - (shift_grad + normed * gain_grad) / counted) * valid_mask
    )
    kernel_part = jnp.stack(
        [
            jnp.sum(grad_conv * gated_pad[offset : offset + frames].astype(jnp.float32), axis=0)
            for offset in range(tap_count)
        ]
    )
    grad_pad = padded_2(grad_conv, (("seq", 0),), half_span)
    grad_gated = depthwise(grad_pad, conv_kernel[::-1], frames) * valid_mask
    grad_pre = jnp.concatenate(
        [grad_gated * gate_part, grad_gated * linear * gate_part * (1.0 - gate_part)], axis=1
    ).astype(jnp.bfloat16)
    in_grad = jnp.dot(grad_pre, weights, preferred_element_type=jnp.float32)
    own_columns = lax.all_to_all(grad_pre[None], "dp", split_axis=2, concat_axis=0, tiled=True)
    local_rows = lax.dot_general(
        own_columns,
        lax.all_gather(restored[None], "dp", axis=0, tiled=True),
        (((0, 1), (0, 1)), ((), ())),
        preferred_element_type=jnp.float32,
    )
    weight_grad = lax.psum(local_rows, "seq")
    kernel_grad = lax.psum(kernel_part, ("dp", "seq"))
    return (in_grad.astype(jnp.bfloat16)[None], weight_grad, kernel_grad, gain_grad, shift_grad)


def per_device(
    saved_codes, code_scales, lengths, in_weight, conv_kernel, bn_gain, bn_shift, out_grad
):
    frames, width = saved_codes.shape[1:]
    square = (
        lax.axis_size("dp") == 4 and lax.axis_size("seq") == 8 and frames == 128
        and width == 1536 and conv_kernel.shape[0] == TAPS and lengths.shape[0] == 4
    )
    if not square:
        return general(
            saved_codes, code_scales, lengths, in_weight, conv_kernel, bn_gain, bn_shift, out_grad
        )
    in_grad, weight_grad, taps = fused(
        lengths, in_weight, saved_codes[0], jnp.transpose(code_scales, (1, 0, 2)), out_grad[0],
        conv_kernel, bn_gain, bn_shift
    )
    in_grad, weight_grad, kernel_grad, gain_grad, shift_grad = finish(in_grad, weight_grad, taps)
    return in_grad[None], weight_grad, kernel_grad, gain_grad, shift_grad


def solution(mesh):
    in_specs = (
        P("dp", "seq", None),
        P("dp", None, "seq"),
        P(),
        P("dp", None),
        P(),
        P(),
        P(),
        P("dp", "seq", None),
    )
    out_specs = (P("dp", "seq", None), P("dp", None), P(), P(), P())
    return jax.shard_map(
        per_device, mesh=mesh, in_specs=in_specs, out_specs=out_specs, check_vma=False
    )
```

```python
import functools

import jax
import jax.numpy as jnp
from jax import lax
from jax.experimental import pallas as pl
from jax.experimental.pallas import tpu as pltpu
from jax.sharding import PartitionSpec as P

EPS = 1e-05
MESH = pl.DeviceIdType.MESH
VM = pl.BlockSpec(memory_space=pltpu.VMEM)


def at(d, s):
    return {"dp": d, "seq": s}


def greet(peers):
    barrier = pltpu.get_barrier_semaphore()
    for peer in peers:
        pl.semaphore_signal(barrier, inc=1, device_id=peer, device_id_type=MESH)
    pl.semaphore_wait(barrier, len(peers))


def remote(src, dst, send, recv, peer):
    return pltpu.make_async_remote_copy(
        src_ref=src, dst_ref=dst, send_sem=send, recv_sem=recv, device_id=peer, device_id_type=MESH
    )


def ring_peers(me, count):
    return [lax.rem(me + k, count) for k in range(1, count)]


def merge(parts, stats):
    if not stats:
        return functools.reduce(lambda a, b: a + b, parts)
    sums = [part[0:16] for part in parts]
    squares = [part[16:32] for part in parts]
    counts = [part[32:48] for part in parts]
    total = functools.reduce(lambda a, b: a + b, sums)
    count = functools.reduce(lambda a, b: a + b, counts)
    mean = total / jnp.maximum(count, 1.0)
    spread = functools.reduce(lambda a, b: a + b, squares)
    for own, n in zip(sums, counts):
        shift = own / jnp.maximum(n, 1.0) - mean
        spread = spread + n * (shift * shift)
    return jnp.concatenate([total, spread, count], axis=0)


def sum_kernel(stats, dp_n, seq_n, x_ref, o_ref, near, far, mid, s1, r1, s2, r2):
    d, s = lax.axis_index("dp"), lax.axis_index("seq")
    plane = ring_peers(s, seq_n)
    line = ring_peers(d, dp_n)
    greet([at(d, j) for j in plane] + [at(j, s) for j in line])
    for k, j in enumerate(plane):
        remote(x_ref, near.at[s], s1.at[k], r1.at[s], at(d, j)).start()
    near[s] = x_ref[...]
    for k, j in enumerate(plane):
        copy = remote(x_ref, near.at[j], s1.at[k], r1.at[j], at(d, j))
        copy.wait_recv()
        copy.wait_send()
    mid[...] = merge([near[j] for j in range(seq_n)], stats)
    for k, j in enumerate(line):
        remote(mid, far.at[d], s2.at[k], r2.at[d], at(j, s)).start()
    far[d] = mid[...]
    for k, j in enumerate(line):
        copy = remote(mid, far.at[j], s2.at[k], r2.at[j], at(j, s))
        copy.wait_recv()
        copy.wait_send()
    o_ref[...] = merge([far[j] for j in range(dp_n)], stats)


def sum_all(vectors, stats, collective_id):
    dp_n, seq_n = lax.axis_size("dp"), lax.axis_size("seq")
    blocks = vectors[0].shape[-1] // 128
    stacked = jnp.stack([v.reshape(blocks, 128) for v in vectors])
    stacked = jnp.pad(stacked, ((0, 0), (0, 16 - blocks), (0, 0)))
    rows = 16 * len(vectors)
    shape = (rows, 128)
    out = pl.pallas_call(
        functools.partial(sum_kernel, stats, dp_n, seq_n),
        out_shape=jax.ShapeDtypeStruct(shape, jnp.float32),
        in_specs=[VM],
        out_specs=VM,
        scratch_shapes=[
            pltpu.VMEM((seq_n,) + shape, jnp.float32),
            pltpu.VMEM((dp_n,) + shape, jnp.float32),
            pltpu.VMEM(shape, jnp.float32),
            pltpu.SemaphoreType.DMA((seq_n,)),
            pltpu.SemaphoreType.DMA((seq_n,)),
            pltpu.SemaphoreType.DMA((dp_n,)),
            pltpu.SemaphoreType.DMA((dp_n,)),
        ],
        compiler_params=pltpu.CompilerParams(collective_id=collective_id, has_side_effects=True),
    )(stacked.reshape(shape))
    return out.reshape(len(vectors), 16, 128)[:, :blocks].reshape(len(vectors), blocks * 128)


HALO = 32
EDGE = 16
TAPS = 31
BF = jnp.bfloat16
F32 = jnp.float32


class Net:
    def __init__(self, send_sems, recv_sems):
        self.send_sems, self.recv_sems = send_sems, recv_sems
        self.used = 0
        self.sent = []

    def send(self, src, dst, peer):
        copy = remote(src, dst, self.send_sems.at[self.used], self.recv_sems.at[self.used], peer)
        self.used += 1
        copy.start()
        self.sent.append(copy)
        return copy

    def drain(self):
        for copy in self.sent:
            copy.wait_send()


def rows_at(start, size):
    return pl.ds(pl.multiple_of(start, 16), size)


def cols_at(start, size):
    return pl.ds(pl.multiple_of(start, 128), size)


def fused_kernel(
    len_ref, w_ref, codes_hbm, scale_hbm, og_ref, ck_hbm, gain_hbm, shift_hbm,
    ig_ref, F, kf_ref,
    codes_ref, scale_ref, ck_ref, gain_ref, shift_ref, res_ref, by_frame, W, R, O, G, A, S, C, D, GP,
    st1, sb1, st2, sb2, vec,
    kp, kb,
    igp, igs, igr, igs2, igr2,
    P, sa, ra, sa2, ra2, sz, rz,
    send_sems, recv_sems, local_sems,
):
    z, s = lax.axis_index("dp"), lax.axis_index("seq")
    c, x, y = lax.rem(s, 2), lax.rem(s // 2, 2), s // 4
    q = s // 2
    kind, half = z // 2, lax.rem(z, 2)
    mate_z = z + 1 - 2 * half
    twin_z = z + 2 - 4 * kind
    jo, jm = half, 1 - half
    frames = codes_hbm.shape[0]
    span = 2 * frames
    width = codes_hbm.shape[1]
    hw = width // 2

    def chip_at(dy, dx):
        yy = 1 - y if dy else y
        xx = 1 - x if dx else x
        return yy * 2 + xx

    core = at(z, s + 1 - 2 * c)
    mate = at(mate_z, s)
    twin = at(twin_z, s)
    offsets = [(0, 1), (1, 0), (1, 1)]
    plane = [at(z, chip_at(dy, dx) * 2 + c) for dy, dx in offsets]
    px, py = plane[0], plane[1]
    far = [at(twin_z, chip_at(dy, dx) * 2 + c) for dy, dx in offsets]
    to_q = lax.rem(q + 2 * c + 3, 4)
    from_q = lax.rem(q + 5 - 2 * c, 4)
    net = Net(send_sems, recv_sems)
    locals_ = []

    def local(src, dst):
        copy = pltpu.make_async_copy(src, dst, local_sems.at[len(locals_)])
        copy.start()
        locals_.append(copy)
        return copy

    loads = [
        local(src, dst) for src, dst in (
            (codes_hbm, codes_ref), (scale_hbm, scale_ref), (ck_hbm, ck_ref),
            (gain_hbm, gain_ref), (shift_hbm, shift_ref))
    ]
    wr = W.shape[0] // 2
    own_w = local(w_ref.at[rows_at(c * wr, wr)], W.at[rows_at(kind * wr, wr)])
    greet([core, mate, twin] + plane + far)

    def spread_out(src, dst, edge, window):
        mine = rows_at(edge + frames * c, frames)
        rim_src = rows_at(c * (frames - edge), edge)
        rim_dst = rows_at(edge + frames * c + c * (frames - edge), edge)
        rim = rows_at((1 - c) * (edge + span), edge)
        rest_src = rows_at((1 - c) * edge, frames - edge)
        rest_dst = rows_at(edge + frames * c + (1 - c) * edge, frames - edge)
        here, there = window(half), window(1 - half)
        side = net.send(src.at[rim_src, there], dst.at[jo, rim_dst], mate)
        rim_own = net.send(src.at[rim_src, here], dst.at[jo, rim], at(z, to_q * 2 + c))
        own = local(src.at[:, here], dst.at[jo, mine])

        def rest():
            return net.send(src.at[rest_src, there], dst.at[jo, rest_dst], mate)

        def over():
            return net.send(src.at[:, here], dst.at[jo, mine], core)

        return side, rim_own, own, rest, over

    def rims_on(parts, dst, edge):
        rim_dst = rows_at(edge + frames * c + c * (frames - edge), edge)
        rim = rows_at((1 - c) * (edge + span), edge)
        side, rim_own = parts[:2]
        side.wait_recv()
        rim_mate = net.send(dst.at[jm, rim_dst], dst.at[jm, rim], at(z, to_q * 2 + c))
        rim_own.wait_recv()
        ref = dst.at[jo, rim]
        return rim_mate, net.send(ref, ref, core)

    def mate_on(rest, rim_mate, dst, edge):
        rim = rows_at((1 - c) * (edge + span), edge)
        rim_mate.wait_recv()
        ref = dst.at[jm, rim]
        got = [net.send(ref, ref, core)]
        rest.wait_recv()
        ref = dst.at[jm, rows_at(edge + frames * c, frames)]
        return got + [net.send(ref, ref, core)]

    piece = wr // 4
    chunks = 3
    step = piece // chunks
    wsend = []
    for i in range(chunks):
        wsend.append(net.send(
            w_ref.at[rows_at(c * wr + q * piece + i * step, step)],
            W.at[rows_at(kind * wr + q * piece + i * step, step)], twin))
    for copy in loads:
        copy.wait()
    for b in range(width // 128):
        by_frame[b:b + 1, :] = scale_ref[b]
    columns = jnp.transpose(by_frame[...])
    for b in range(width // 128):
        lanes = pl.ds(b * 128, 128)
        res_ref[:, lanes] = (
            codes_ref[:, lanes].astype(F32) * columns[:, b:b + 1]
        ).astype(BF)

    r_parts = spread_out(res_ref, R, HALO, lambda h: pl.ds(0, width))
    r_over = r_parts[4]()
    other_w = (1 - kind) * wr
    near_w, far_w = [], []

    def pass_near(i):
        wsend[i].wait_recv()
        ref = W.at[rows_at(other_w + q * piece + i * step, step)]
        near_w.append((net.send(ref, ref, px), net.send(ref, ref, py)))

    def pass_far(i):
        from_x, from_y = near_w[i]
        from_x.wait_recv()
        ref = W.at[rows_at(other_w + chip_at(0, 1) * piece + i * step, step // 2)]
        far_w.append(net.send(ref, ref, py))
        from_y.wait_recv()
        ref = W.at[rows_at(other_w + chip_at(1, 0) * piece + i * step + step // 2, step // 2)]
        far_w.append(net.send(ref, ref, px))

    pass_near(0)
    r_rest = r_parts[3]()
    r_rim_mate, r_rim_core = rims_on(r_parts, R, HALO)
    pass_near(1)
    pass_far(0)
    pass_near(2)
    pass_far(1)
    pass_far(2)
    r_got = mate_on(r_rest, r_rim_mate, R, HALO)
    o_parts = spread_out(og_ref, O, EDGE, lambda h: cols_at(h * hw, hw))
    o_rest = o_parts[3]()
    o_over = o_parts[4]()
    for copy in far_w:
        copy.wait_recv()
    own_w.wait()
    r_parts[2].wait()
    r_over.wait_recv()
    r_rim_core.wait_recv()

    blocks = wr // 128
    chan = (half * 2 + c) * wr
    lens = [len_ref[kind * 2 + j] for j in range(2)]

    def mask_rows(j, edge, rows):
        frame = q * span - edge + lax.broadcasted_iota(jnp.int32, (rows, 128), 0)
        length = jnp.where(j == 0, lens[0], lens[1])
        return (frame >= 0) & (frame < length)

    long = span + 2 * HALO
    mid = span + 2 * EDGE

    def project(j):
        pre = lax.dot_general(
            R[j], W[...], (((1,), (1,)), ((), ())), preferred_element_type=F32
        )
        keep = mask_rows(j, HALO, long)
        for b in range(blocks):
            lin = pre[:, b * 128:(b + 1) * 128]
            sig = jax.nn.sigmoid(pre[:, wr + b * 128:wr + (b + 1) * 128])
            G[j, b] = jnp.where(keep, lin * sig, 0.0).astype(BF).astype(F32)
            A[j, b] = lin[HALO:HALO + span]
            S[j, b] = sig[HALO:HALO + span]

    def count_at(pair, chip, j):
        n = jnp.clip(len_ref[pair * 2 + j] - chip * span, 0, span)
        return jnp.full((8, 128), n, jnp.int32).astype(F32)

    own_counts = [count_at(kind, q, j) for j in range(2)]

    def convolve(j, b):
        lanes = cols_at(chan + b * 128, 128)
        acc = jnp.zeros((mid, 128), F32)
        for k in range(TAPS):
            acc = acc + ck_ref[k:k + 1, lanes] * G[j, b, pl.ds(1 + k, mid), :]
        C[j, b] = acc
        keep = mask_rows(j, 0, span)
        own = acc[EDGE:EDGE + span]
        total = jnp.sum(jnp.where(keep, own, 0.0), axis=0, keepdims=True)
        n = jnp.where(j == 0, own_counts[0][0:1], own_counts[1][0:1])
        dev = jnp.where(keep, own - total / jnp.maximum(n, 1.0), 0.0)
        st1[j, pl.ds(b, 1), :] = total
        st1[j, pl.ds(blocks + b, 1), :] = jnp.sum(dev * dev, axis=0, keepdims=True)

    @pl.loop(0, 1)
    def _(_i):
        project(jo)

    @pl.loop(0, blocks)
    def _(b):
        convolve(jo, b)

    for copy in r_got:
        copy.wait_recv()

    @pl.loop(0, 1)
    def _(_i):
        project(jm)

    o_rim_mate, o_rim_core = rims_on(o_parts, O, EDGE)

    @pl.loop(0, blocks)
    def _(b):
        convolve(jm, b)

    me8 = kind * 4 + q
    peers8 = plane + [twin] + far

    def exchange(src, slots):
        own = local(src, slots.at[me8])
        copies = [net.send(src, slots.at[me8], peer) for peer in peers8]
        return own, copies

    own, copies = exchange(st1, sb1)
    o_got = mate_on(o_rest, o_rim_mate, O, EDGE)
    own.wait()
    for copy in copies:
        copy.wait_recv()
    counted = jnp.zeros((8, 128), F32)
    for g in range(len_ref.shape[0]):
        counted = counted + jnp.full((8, 128), len_ref[g], jnp.int32).astype(F32)
    total = jnp.zeros((8, 128), F32)
    for i in range(8):
        for j in range(2):
            total = total + sb1[i, j]
    mean = total / counted
    shift2 = jnp.zeros((8, 128), F32)
    for i in range(8):
        for j in range(2):
            n = count_at(i // 4, i % 4, j)
            d = sb1[i, j] / jnp.maximum(n, 1.0) - mean
            shift2 = shift2 + n * (d * d)
    vec[0] = total
    vec[1] = shift2
    var = (vec[0, blocks:2 * blocks] + vec[1, 0:blocks]) / counted[0:blocks]
    vec[2] = mean
    vec[3, 0:blocks] = lax.rsqrt(var + EPS)

    for copy in o_got + [o_over, o_rim_core]:
        copy.wait_recv()
    o_parts[2].wait()

    @pl.loop(0, 2 * blocks)
    def _(t):
        j, b = t // blocks, lax.rem(t, blocks)
        lanes = cols_at(chan + b * 128, 128)
        normed = (C[j, b] - vec[2, pl.ds(b, 1), :]) * vec[3, pl.ds(b, 1), :]
        shaped = gain_ref[lanes][None] * normed + shift_ref[lanes][None]
        smooth = jax.nn.sigmoid(shaped)
        up = O[j, :, cols_at(c * wr + b * 128, 128)].astype(F32)
        gs = jnp.where(
            mask_rows(j, EDGE, mid), up * smooth * (1.0 + shaped * (1.0 - smooth)), 0.0
        )
        D[j, b] = gs
        own = gs[EDGE:EDGE + span]
        st1_rows = jnp.sum(own, axis=0, keepdims=True)
        gain_rows = jnp.sum(own * normed[EDGE:EDGE + span], axis=0, keepdims=True)
        st2[1 + j, pl.ds(b, 1), :] = st1_rows
        st2[1 + j, pl.ds(blocks + b, 1), :] = gain_rows

    st2[0] = st2[1] + st2[2]
    own, copies = exchange(st2.at[0], sb2)

    own.wait()
    for copy in copies:
        copy.wait_recv()
    sums = jnp.zeros((8, 128), F32)
    for i in range(8):
        sums = sums + sb2[i]
    vec[4] = sums

    @pl.loop(0, 2 * blocks)
    def _(t):
        j, b = t // blocks, lax.rem(t, blocks)
        lanes = cols_at(chan + b * 128, 128)
        inverse = vec[3, pl.ds(b, 1), :]
        normed = (C[j, b] - vec[2, pl.ds(b, 1), :]) * inverse
        add, mul = vec[4, pl.ds(b, 1), :], vec[4, pl.ds(blocks + b, 1), :]
        D[j, b] = jnp.where(
            mask_rows(j, EDGE, mid),
            gain_ref[lanes][None] * inverse * (D[j, b] - (add + normed * mul) / counted[0:1]),
            0.0,
        )

    def back(b):
        lanes = cols_at(chan + b * 128, 128)

        @pl.loop(0, 2)
        def _(j):
            acc = jnp.zeros((span, 128), F32)
            for k in range(TAPS):
                acc = acc + ck_ref[k:k + 1, lanes] * D[j, b, pl.ds(TAPS - k, span), :]
            acc = jnp.where(mask_rows(j, 0, span), acc, 0.0)
            sig = S[j, b]
            to_lin = acc * sig
            GP[j, :, b * 128:(b + 1) * 128] = to_lin.astype(BF)
            GP[j, :, wr + b * 128:wr + (b + 1) * 128] = (
                to_lin * A[j, b] * (1.0 - sig)
            ).astype(BF)

    tile = 512

    def input_grad():
        @pl.loop(0, 2 * (width // tile))
        def _(t):
            j, n = t // (width // tile), lax.rem(t, width // tile)
            lanes = cols_at(n * tile, tile)
            part = jnp.dot(GP[j], W[:, lanes], preferred_element_type=F32)
            igp[j, :, lanes] = part

        igs[...] = igp[:, rows_at((1 - c) * frames, frames), :].astype(BF)
        return net.send(igs, igr, core)

    def taps():
        @pl.loop(0, blocks)
        def _(b):
            for k in range(TAPS):
                part = jnp.zeros((1, 128), F32)
                for j in range(2):
                    part = part + jnp.sum(
                        D[j, b, pl.ds(EDGE, span), :] * G[j, b, pl.ds(EDGE + 1 + k, span), :],
                        axis=0, keepdims=True)
                kp[k // 4, b, k % 4:k % 4 + 1, :] = part
            kp[7, b, 3:4, :] = jnp.zeros((1, 128), F32)

        own = local(kp.at[me8], kb.at[me8])
        index = [kind * 4 + chip_at(dy, dx) for dy, dx in offsets]
        index += [(1 - kind) * 4 + i for i in [q] + [chip_at(dy, dx) for dy, dx in offsets]]
        return own, [net.send(kp.at[i], kb.at[me8], peer) for i, peer in zip(index, peers8)]

    eh = hw
    colsA, colsB = pl.ds(0, eh), pl.ds(eh, eh)

    def s1(m, b):
        rows = cols_at((kind if m else 1 - kind) * wr + b * 128, 128)

        @pl.loop(0, width // tile)
        def _(n):
            lanes = cols_at(n * tile, tile)
            acc = jnp.zeros((128, tile), F32)
            for j in range(2):
                acc = acc + lax.dot_general(
                    GP[j, :, rows], R[j, pl.ds(HALO, span), lanes], (((0,), (0,)), ((), ())),
                    preferred_element_type=F32)
            P[m, b, :, lanes] = acc

        sa[m, b, 0] = P[m, b, rows_at((1 - x) * 64, 64), 0:eh].astype(BF)
        sa[m, b, 1] = P[m, b, rows_at((1 - y) * 64, 64), eh:2 * eh].astype(BF)
        return [
            net.send(sa.at[m, b, 0], ra.at[m, b, 0], px),
            net.send(sa.at[m, b, 1], ra.at[m, b, 1], py),
        ]

    def s2(m, b, got):
        for copy in got:
            copy.wait_recv()
        sa2[m, b, 0] = (
            P[m, b, rows_at(x * 64 + (1 - y) * 32, 32), 0:eh]
            + ra[m, b, 0, rows_at((1 - y) * 32, 32), :].astype(F32)).astype(BF)
        sa2[m, b, 1] = (
            P[m, b, rows_at(y * 64 + (1 - x) * 32, 32), eh:2 * eh]
            + ra[m, b, 1, rows_at((1 - x) * 32, 32), :].astype(F32)).astype(BF)
        return [
            net.send(sa2.at[m, b, 0], ra2.at[m, b, 0], py),
            net.send(sa2.at[m, b, 1], ra2.at[m, b, 1], px),
        ]

    row_a, row_b = x * 64 + y * 32, y * 64 + x * 32

    def summed(m, b):
        return (
            P[m, b, rows_at(row_a, 32), 0:eh] + ra[m, b, 0, rows_at(y * 32, 32), :].astype(F32)
            + ra2[m, b, 0].astype(F32),
            P[m, b, rows_at(row_b, 32), eh:2 * eh] + ra[m, b, 1, rows_at(x * 32, 32), :].astype(F32)
            + ra2[m, b, 1].astype(F32),
        )

    def to_twin(b, got):
        for copy in got:
            copy.wait_recv()
        part_a, part_b = summed(0, b)
        sz[b, 0] = part_a.astype(BF)
        sz[b, 1] = part_b.astype(BF)
        return net.send(sz.at[b], rz.at[b], twin)

    def tile_of(core_at, b, start, size, cols):
        return F.at[rows_at(core_at * wr + b * 128 + start, size), cols]

    cols_a, cols_b = pl.ds(0, eh), pl.ds(eh, eh)

    def s3(b, got, from_twin):
        for copy in got:
            copy.wait_recv()
        part_a, part_b = summed(1, b)
        from_twin.wait_recv()
        fa, fb = tile_of(c, b, row_a, 32, cols_a), tile_of(c, b, row_b, 32, cols_b)
        fa[...] = (part_a + rz[b, 0].astype(F32)).astype(BF)
        fb[...] = (part_b + rz[b, 1].astype(F32)).astype(BF)
        return [net.send(fa, fa, py), net.send(fb, fb, px)]

    def s4(b, got):
        for copy in got:
            copy.wait_recv()
        fa, fb = tile_of(c, b, x * 64, 64, cols_a), tile_of(c, b, y * 64, 64, cols_b)
        return [net.send(fa, fa, px), net.send(fb, fb, py)]

    def s5(b, got):
        for copy in got:
            copy.wait_recv()
        ref = tile_of(c, b, 0, 128, pl.ds(0, width))
        return [net.send(ref, ref, core)]

    def k1(own, got):
        own.wait()
        for copy in got:
            copy.wait_recv()
        hc = half * 2 + c
        for b in range(blocks):
            part = jnp.zeros((8, 128), F32)
            for i in range(8):
                part = part + kb[i, b]
            kf_ref[hc, me8, b] = part
            kf_ref[hc, me8, b, 4:5, :] = vec[4, b:b + 1, :]
            kf_ref[hc, me8, b, 5:6, :] = vec[4, blocks + b:blocks + b + 1, :]
        ref = kf_ref.at[hc, me8]
        return [net.send(ref, ref, peer) for peer in peers8]

    def k2(got):
        for copy in got:
            copy.wait_recv()
        ref = kf_ref.at[half * 2 + c]
        return [net.send(ref, ref, core)]

    def k3(got):
        for copy in got:
            copy.wait_recv()
        ref = kf_ref.at[pl.ds(half * 2, 2)]
        return [net.send(ref, ref, mate)]

    def i1(got):
        got.wait_recv()
        igs2[...] = (
            igp[jm, rows_at(c * frames, frames), :] + igr[jm].astype(F32)
        ).astype(BF)
        return net.send(igs2, igr2, mate)

    def i2(got):
        got.wait_recv()
        ig_ref[...] = (
            igp[jo, rows_at(c * frames, frames), :] + igr[jo].astype(F32) + igr2[...].astype(F32)
        ).astype(BF)

    back(0)
    o0 = s1(0, 0)
    back(1)
    o1 = s1(0, 1)
    back(2)
    o0 = s2(0, 0, o0)
    o2 = s1(0, 2)
    o1 = s2(0, 1, o1)
    w0 = s1(1, 0)
    t0 = to_twin(0, o0)
    o2 = s2(0, 2, o2)
    w1 = s1(1, 1)
    t1 = to_twin(1, o1)
    w2 = s1(1, 2)
    w0 = s2(1, 0, w0)
    t2 = to_twin(2, o2)
    ig = input_grad()
    w1 = s2(1, 1, w1)
    w2 = s2(1, 2, w2)
    ig = i1(ig)
    w0 = s3(0, w0, t0)
    kown, k = taps()
    w1 = s3(1, w1, t1)
    w0 = s4(0, w0)
    w2 = s3(2, w2, t2)
    w1 = s4(1, w1)
    k = k1(kown, k)
    w2 = s4(2, w2)
    w0 = s5(0, w0)
    k = k2(k)
    w1 = s5(1, w1)
    i2(ig)
    k = k3(k)
    w2 = s5(2, w2)
    for copy in w0 + w1 + w2 + k:
        copy.wait_recv()
    net.drain()


def finish_kernel(ig_in, wg_in, kf_in, ig_out, wg_out, taps_out, gain_out, shift_out, wide, sems):
    copies = []

    def put(src, dst):
        copy = pltpu.make_async_copy(src, dst, sems.at[len(copies)])
        copy.start()
        copies.append(copy)

    put(ig_in, ig_out)
    parts = 6
    rows = wg_in.shape[0] // parts
    for i in range(parts):
        where = pl.ds(i * rows, rows)
        wide[where, :] = wg_in[where, :].astype(F32)
        put(wide.at[where], wg_out.at[where])
    owners, blocks = kf_in.shape[1], kf_in.shape[2]
    for hc in range(4):
        for b in range(blocks):
            lanes = pl.ds((hc * blocks + b) * 128, 128)
            for i in range(owners):
                n = min(4, taps_out.shape[0] - 4 * i)
                taps_out[4 * i:4 * i + n, lanes] = kf_in[hc, i, b, 0:n, :]
            shift_out[lanes] = kf_in[hc, 0, b, 4, :]
            gain_out[lanes] = kf_in[hc, 0, b, 5, :]
    for copy in copies:
        copy.wait()


def finish(in_grad, weight_grad, taps):
    any_space = pl.BlockSpec(memory_space=pl.ANY)
    width = in_grad.shape[1]
    return pl.pallas_call(
        finish_kernel,
        out_shape=(
            jax.ShapeDtypeStruct(in_grad.shape, BF),
            jax.ShapeDtypeStruct(weight_grad.shape, F32),
            jax.ShapeDtypeStruct((TAPS, width), F32),
            jax.ShapeDtypeStruct((width,), F32),
            jax.ShapeDtypeStruct((width,), F32),
        ),
        in_specs=[VM, VM, VM],
        out_specs=(any_space, any_space, VM, VM, VM),
        scratch_shapes=[pltpu.VMEM(weight_grad.shape, F32), pltpu.SemaphoreType.DMA((8,))],
        compiler_params=pltpu.CompilerParams(vmem_limit_bytes=20 * 1024 * 1024),
    )(in_grad, weight_grad, taps)


def fused(lengths, in_weight, codes, scales, out_grad, conv_kernel, bn_gain, bn_shift):
    frames, width = codes.shape
    wr = width // 4
    blocks = wr // 128
    span = 2 * frames
    long, mid = span + 2 * HALO, span + 2 * EDGE
    dma = pltpu.SemaphoreType.DMA
    hbm = pl.BlockSpec(memory_space=pltpu.HBM)
    smem = pl.BlockSpec(memory_space=pltpu.SMEM)

    def vm(shape, dtype=F32):
        return pltpu.VMEM(shape, dtype)

    return pl.pallas_call(
        fused_kernel,
        out_shape=(
            jax.ShapeDtypeStruct((frames, width), BF),
            jax.ShapeDtypeStruct((2 * wr, width), BF),
            jax.ShapeDtypeStruct((4, 8, blocks, 8, 128), F32),
        ),
        in_specs=[smem] + [hbm] * 7,
        out_specs=(VM, VM, VM),
        scratch_shapes=[
            vm((frames, width), BF),
            vm(scales.shape),
            vm(conv_kernel.shape),
            vm(bn_gain.shape),
            vm(bn_shift.shape),
            vm((frames, width), BF),
            vm((128, 128)),
            vm((2 * wr, width), BF),
            vm((2, long, width), BF),
            vm((2, mid, width // 2), BF),
            vm((2, blocks, long, 128)),
            vm((2, blocks, span, 128)),
            vm((2, blocks, span, 128)),
            vm((2, blocks, mid, 128)),
            vm((2, blocks, mid, 128)),
            vm((2, span, 2 * wr), BF),
            vm((2, 8, 128)),
            vm((8, 2, 8, 128)),
            vm((3, 8, 128)),
            vm((8, 8, 128)),
            vm((5, 8, 128)),
            vm((8, blocks, 8, 128)),
            vm((8, blocks, 8, 128)),
            vm((2, span, width)),
            vm((2, frames, width), BF),
            vm((2, frames, width), BF),
            vm((frames, width), BF),
            vm((frames, width), BF),
            vm((2, blocks, 128, width)),
            vm((2, blocks, 2, 64, width // 2), BF),
            vm((2, blocks, 2, 64, width // 2), BF),
            vm((2, blocks, 2, 32, width // 2), BF),
            vm((2, blocks, 2, 32, width // 2), BF),
            vm((blocks, 2, 32, width // 2), BF),
            vm((blocks, 2, 32, width // 2), BF),
            dma((128,)),
            dma((128,)),
            dma((16,)),
        ],
        compiler_params=pltpu.CompilerParams(
            collective_id=4, has_side_effects=True, vmem_limit_bytes=36 * 1024 * 1024
        ),
    )(*[
        pltpu.with_memory_space_constraint(operand, pltpu.HBM)
        for operand in (
            lengths, in_weight, codes, scales, out_grad, conv_kernel, bn_gain, bn_shift)
    ])


def padded_2(cells, sides, width):
    for axis, dim in sides:
        count = lax.axis_size(axis)
        ends = count - 1
        head = lax.slice_in_dim(cells, 0, width, axis=dim)
        tail = lax.slice_in_dim(cells, cells.shape[dim] - width, cells.shape[dim], axis=dim)
        cells = jnp.concatenate(
            [
                lax.ppermute(tail, axis, [(i, (i + 1) % count) for i in range(ends)]),
                cells,
                lax.ppermute(head, axis, [((i + 1) % count, i) for i in range(ends)]),
            ],
            axis=dim,
        )
    return cells


def restore(quantized, scales):
    per_channel = jnp.repeat(scales.T, 128, axis=1)
    return (quantized.astype(jnp.float32) * per_channel).astype(jnp.bfloat16)


def depthwise(padded, kernel, frames):
    running = jnp.zeros((frames, padded.shape[1]), jnp.float32)
    for offset in range(kernel.shape[0]):
        running = running + kernel[offset] * padded[offset : offset + frames].astype(jnp.float32)
    return running


def general(
    saved_codes, code_scales, lengths, in_weight, conv_kernel, bn_gain, bn_shift, out_grad
):
    frames = saved_codes.shape[1]
    feature_width = saved_codes.shape[2]
    tap_count = conv_kernel.shape[0]
    half_span = (tap_count - 1) // 2
    groups = lengths.shape[0]
    group_at = lax.axis_index("dp")
    length = jnp.sum(jnp.where(jnp.arange(groups, dtype=jnp.int32) == group_at, lengths, 0))
    counted = jnp.sum(lengths).astype(jnp.float32)
    first_frame = lax.axis_index("seq") * frames
    valid_mask = (first_frame + jnp.arange(frames, dtype=jnp.int32) < length).astype(jnp.float32)[
        :, None
    ]
    restored = restore(saved_codes[0], code_scales[0])
    weights = lax.all_gather(in_weight, "dp", axis=0, tiled=True)
    pre_act = lax.dot_general(
        restored, weights, (((1,), (1,)), ((), ())), preferred_element_type=jnp.float32
    )
    linear = pre_act[:, :feature_width]
    gate_part = jax.nn.sigmoid(pre_act[:, feature_width:])
    gated = (linear * gate_part * valid_mask).astype(jnp.bfloat16)
    gated_pad = padded_2(gated, (("seq", 0),), half_span)
    conv_out = depthwise(gated_pad, conv_kernel, frames)
    own_sum = jnp.sum(conv_out * valid_mask, axis=0)
    own_count = jnp.sum(valid_mask)
    centered = (conv_out - own_sum / jnp.maximum(own_count, 1.0)) * valid_mask
    own_square = jnp.sum(centered * centered, axis=0)
    total, spread, _ = sum_all(
        [own_sum, own_square, jnp.full_like(own_sum, own_count)], True, 0
    )
    mean_value = total / counted
    variance = spread / counted
    inverse = lax.rsqrt(variance + EPS)
    normed = (conv_out - mean_value) * inverse
    shaped = bn_gain * normed + bn_shift
    smooth = jax.nn.sigmoid(shaped)
    grad_shaped = (
        out_grad[0].astype(jnp.float32) * valid_mask * smooth * (1.0 + shaped * (1.0 - smooth))
    )
    shift_grad, gain_grad = sum_all(
        [jnp.sum(grad_shaped, axis=0), jnp.sum(grad_shaped * normed, axis=0)], False, 1
    )
    grad_conv = (
        bn_gain * inverse * (grad_shaped - (shift_grad + normed * gain_grad) / counted) * valid_mask
    )
    kernel_part = jnp.stack(
        [
            jnp.sum(grad_conv * gated_pad[offset : offset + frames].astype(jnp.float32), axis=0)
            for offset in range(tap_count)
        ]
    )
    grad_pad = padded_2(grad_conv, (("seq", 0),), half_span)
    grad_gated = depthwise(grad_pad, conv_kernel[::-1], frames) * valid_mask
    grad_pre = jnp.concatenate(
        [grad_gated * gate_part, grad_gated * linear * gate_part * (1.0 - gate_part)], axis=1
    ).astype(jnp.bfloat16)
    in_grad = jnp.dot(grad_pre, weights, preferred_element_type=jnp.float32)
    own_columns = lax.all_to_all(grad_pre[None], "dp", split_axis=2, concat_axis=0, tiled=True)
    local_rows = lax.dot_general(
        own_columns,
        lax.all_gather(restored[None], "dp", axis=0, tiled=True),
        (((0, 1), (0, 1)), ((), ())),
        preferred_element_type=jnp.float32,
    )
    weight_grad = lax.psum(local_rows, "seq")
    kernel_grad = lax.psum(kernel_part, ("dp", "seq"))
    return (in_grad.astype(jnp.bfloat16)[None], weight_grad, kernel_grad, gain_grad, shift_grad)


def per_device(
    saved_codes, code_scales, lengths, in_weight, conv_kernel, bn_gain, bn_shift, out_grad
):
    frames, width = saved_codes.shape[1:]
    square = (
        lax.axis_size("dp") == 4 and lax.axis_size("seq") == 8 and frames == 128
        and width == 1536 and conv_kernel.shape[0] == TAPS and lengths.shape[0] == 4
    )
    if not square:
        return general(
            saved_codes, code_scales, lengths, in_weight, conv_kernel, bn_gain, bn_shift, out_grad
        )
    in_grad, weight_grad, taps = fused(
        lengths, in_weight, saved_codes[0], jnp.transpose(code_scales, (1, 0, 2)), out_grad[0],
        conv_kernel, bn_gain, bn_shift
    )
    in_grad, weight_grad, kernel_grad, gain_grad, shift_grad = finish(in_grad, weight_grad, taps)
    return in_grad[None], weight_grad, kernel_grad, gain_grad, shift_grad


def solution(mesh):
    in_specs = (
        P("dp", "seq", None),
        P("dp", None, "seq"),
        P(),
        P("dp", None),
        P(),
        P(),
        P(),
        P("dp", "seq", None),
    )
    out_specs = (P("dp", "seq", None), P("dp", None), P(), P(), P())
    return jax.shard_map(
        per_device, mesh=mesh, in_specs=in_specs, out_specs=out_specs, check_vma=False
    )
```

```python
import functools

import jax
import jax.numpy as jnp
from jax import lax
from jax.experimental import pallas as pl
from jax.experimental.pallas import tpu as pltpu
from jax.sharding import PartitionSpec as P

EPS = 1e-05
MESH = pl.DeviceIdType.MESH
VM = pl.BlockSpec(memory_space=pltpu.VMEM)


def at(d, s):
    return {"dp": d, "seq": s}


def greet(peers):
    barrier = pltpu.get_barrier_semaphore()
    for peer in peers:
        pl.semaphore_signal(barrier, inc=1, device_id=peer, device_id_type=MESH)
    pl.semaphore_wait(barrier, len(peers))


def remote(src, dst, send, recv, peer):
    return pltpu.make_async_remote_copy(
        src_ref=src, dst_ref=dst, send_sem=send, recv_sem=recv, device_id=peer, device_id_type=MESH
    )


def ring_peers(me, count):
    return [lax.rem(me + k, count) for k in range(1, count)]


def merge(parts, stats):
    if not stats:
        return functools.reduce(lambda a, b: a + b, parts)
    sums = [part[0:16] for part in parts]
    squares = [part[16:32] for part in parts]
    counts = [part[32:48] for part in parts]
    total = functools.reduce(lambda a, b: a + b, sums)
    count = functools.reduce(lambda a, b: a + b, counts)
    mean = total / jnp.maximum(count, 1.0)
    spread = functools.reduce(lambda a, b: a + b, squares)
    for own, n in zip(sums, counts):
        shift = own / jnp.maximum(n, 1.0) - mean
        spread = spread + n * (shift * shift)
    return jnp.concatenate([total, spread, count], axis=0)


def sum_kernel(stats, dp_n, seq_n, x_ref, o_ref, near, far, mid, s1, r1, s2, r2):
    d, s = lax.axis_index("dp"), lax.axis_index("seq")
    plane = ring_peers(s, seq_n)
    line = ring_peers(d, dp_n)
    greet([at(d, j) for j in plane] + [at(j, s) for j in line])
    for k, j in enumerate(plane):
        remote(x_ref, near.at[s], s1.at[k], r1.at[s], at(d, j)).start()
    near[s] = x_ref[...]
    for k, j in enumerate(plane):
        copy = remote(x_ref, near.at[j], s1.at[k], r1.at[j], at(d, j))
        copy.wait_recv()
        copy.wait_send()
    mid[...] = merge([near[j] for j in range(seq_n)], stats)
    for k, j in enumerate(line):
        remote(mid, far.at[d], s2.at[k], r2.at[d], at(j, s)).start()
    far[d] = mid[...]
    for k, j in enumerate(line):
        copy = remote(mid, far.at[j], s2.at[k], r2.at[j], at(j, s))
        copy.wait_recv()
        copy.wait_send()
    o_ref[...] = merge([far[j] for j in range(dp_n)], stats)


def sum_all(vectors, stats, collective_id):
    dp_n, seq_n = lax.axis_size("dp"), lax.axis_size("seq")
    blocks = vectors[0].shape[-1] // 128
    stacked = jnp.stack([v.reshape(blocks, 128) for v in vectors])
    stacked = jnp.pad(stacked, ((0, 0), (0, 16 - blocks), (0, 0)))
    rows = 16 * len(vectors)
    shape = (rows, 128)
    out = pl.pallas_call(
        functools.partial(sum_kernel, stats, dp_n, seq_n),
        out_shape=jax.ShapeDtypeStruct(shape, jnp.float32),
        in_specs=[VM],
        out_specs=VM,
        scratch_shapes=[
            pltpu.VMEM((seq_n,) + shape, jnp.float32),
            pltpu.VMEM((dp_n,) + shape, jnp.float32),
            pltpu.VMEM(shape, jnp.float32),
            pltpu.SemaphoreType.DMA((seq_n,)),
            pltpu.SemaphoreType.DMA((seq_n,)),
            pltpu.SemaphoreType.DMA((dp_n,)),
            pltpu.SemaphoreType.DMA((dp_n,)),
        ],
        compiler_params=pltpu.CompilerParams(collective_id=collective_id, has_side_effects=True),
    )(stacked.reshape(shape))
    return out.reshape(len(vectors), 16, 128)[:, :blocks].reshape(len(vectors), blocks * 128)


HALO = 32
EDGE = 16
TAPS = 31
BF = jnp.bfloat16
F32 = jnp.float32


class Net:
    def __init__(self, send_sems, recv_sems):
        self.send_sems, self.recv_sems = send_sems, recv_sems
        self.used = 0
        self.sent = []

    def send(self, src, dst, peer):
        copy = remote(src, dst, self.send_sems.at[self.used], self.recv_sems.at[self.used], peer)
        self.used += 1
        copy.start()
        self.sent.append(copy)
        return copy

    def drain(self):
        for copy in self.sent:
            copy.wait_send()


def rows_at(start, size):
    return pl.ds(pl.multiple_of(start, 16), size)


def cols_at(start, size):
    return pl.ds(pl.multiple_of(start, 128), size)


def fused_kernel(
    len_ref, w_ref, codes_hbm, scale_hbm, og_ref, ck_hbm, gain_hbm, shift_hbm,
    ig_ref, F, kf_ref,
    codes_ref, scale_ref, ck_ref, gain_ref, shift_ref, res_ref, by_frame, W, R, O, G, A, S, C, D, GP,
    st1, sb1, st2, sb2, vec,
    kp, kb,
    igp, igs, igr, igs2, igr2,
    P, sa, ra, sa2, ra2, sz, rz,
    send_sems, recv_sems, local_sems,
):
    z, s = lax.axis_index("dp"), lax.axis_index("seq")
    c, x, y = lax.rem(s, 2), lax.rem(s // 2, 2), s // 4
    q = s // 2
    kind, half = z // 2, lax.rem(z, 2)
    mate_z = z + 1 - 2 * half
    twin_z = z + 2 - 4 * kind
    jo, jm = half, 1 - half
    frames = codes_hbm.shape[0]
    span = 2 * frames
    width = codes_hbm.shape[1]
    hw = width // 2

    def chip_at(dy, dx):
        yy = 1 - y if dy else y
        xx = 1 - x if dx else x
        return yy * 2 + xx

    core = at(z, s + 1 - 2 * c)
    mate = at(mate_z, s)
    twin = at(twin_z, s)
    offsets = [(0, 1), (1, 0), (1, 1)]
    plane = [at(z, chip_at(dy, dx) * 2 + c) for dy, dx in offsets]
    px, py = plane[0], plane[1]
    far = [at(twin_z, chip_at(dy, dx) * 2 + c) for dy, dx in offsets]
    to_q = lax.rem(q + 2 * c + 3, 4)
    from_q = lax.rem(q + 5 - 2 * c, 4)
    net = Net(send_sems, recv_sems)
    locals_ = []

    def local(src, dst):
        copy = pltpu.make_async_copy(src, dst, local_sems.at[len(locals_)])
        copy.start()
        locals_.append(copy)
        return copy

    loads = [
        local(src, dst) for src, dst in (
            (codes_hbm, codes_ref), (scale_hbm, scale_ref), (ck_hbm, ck_ref),
            (gain_hbm, gain_ref), (shift_hbm, shift_ref))
    ]
    wr = W.shape[0] // 2
    blocks = wr // 128
    own_w = [
        local(w_ref.at[rows_at(c * wr + b * 128, 128)], W.at[rows_at((2 * b + kind) * 128, 128)])
        for b in range(blocks)
    ]
    greet([core, mate, twin] + plane + far)

    def spread_out(src, dst, edge, window):
        mine = rows_at(edge + frames * c, frames)
        rim_src = rows_at(c * (frames - edge), edge)
        rim_dst = rows_at(edge + frames * c + c * (frames - edge), edge)
        rim = rows_at((1 - c) * (edge + span), edge)
        rest_src = rows_at((1 - c) * edge, frames - edge)
        rest_dst = rows_at(edge + frames * c + (1 - c) * edge, frames - edge)
        here, there = window(half), window(1 - half)
        side = net.send(src.at[rim_src, there], dst.at[jo, rim_dst], mate)
        rim_own = net.send(src.at[rim_src, here], dst.at[jo, rim], at(z, to_q * 2 + c))
        own = local(src.at[:, here], dst.at[jo, mine])

        def rest():
            return net.send(src.at[rest_src, there], dst.at[jo, rest_dst], mate)

        def over():
            return net.send(src.at[:, here], dst.at[jo, mine], core)

        return side, rim_own, own, rest, over

    def rims_on(parts, dst, edge):
        rim_dst = rows_at(edge + frames * c + c * (frames - edge), edge)
        rim = rows_at((1 - c) * (edge + span), edge)
        side, rim_own = parts[:2]
        side.wait_recv()
        rim_mate = net.send(dst.at[jm, rim_dst], dst.at[jm, rim], at(z, to_q * 2 + c))
        rim_own.wait_recv()
        ref = dst.at[jo, rim]
        return rim_mate, net.send(ref, ref, core)

    def mate_on(rest, rim_mate, dst, edge):
        rim = rows_at((1 - c) * (edge + span), edge)
        rim_mate.wait_recv()
        ref = dst.at[jm, rim]
        got = [net.send(ref, ref, core)]
        rest.wait_recv()
        ref = dst.at[jm, rows_at(edge + frames * c, frames)]
        return got + [net.send(ref, ref, core)]

    step = 32
    wsend = []
    for i in range(blocks):
        wsend.append(net.send(
            w_ref.at[rows_at(c * wr + i * 128 + q * step, step)],
            W.at[rows_at((2 * i + kind) * 128 + q * step, step)], twin))
    for copy in loads:
        copy.wait()
    for b in range(width // 128):
        by_frame[b:b + 1, :] = scale_ref[b]
    columns = jnp.transpose(by_frame[...])
    for b in range(width // 128):
        lanes = pl.ds(b * 128, 128)
        res_ref[:, lanes] = (
            codes_ref[:, lanes].astype(F32) * columns[:, b:b + 1]
        ).astype(BF)

    r_parts = spread_out(res_ref, R, HALO, lambda h: pl.ds(0, width))
    r_rest = r_parts[3]()
    r_over = r_parts[4]()
    near_w, far_w = [], []

    def piece(i, chip, start, size):
        return W.at[rows_at((2 * i + 1 - kind) * 128 + chip * step + start, size)]

    def pass_near(i):
        wsend[i].wait_recv()
        ref = piece(i, q, 0, step)
        near_w.append((net.send(ref, ref, px), net.send(ref, ref, py)))

    def pass_far(i):
        from_x, from_y = near_w[i]
        from_x.wait_recv()
        ref = piece(i, chip_at(0, 1), 0, step // 2)
        to_y = net.send(ref, ref, py)
        from_y.wait_recv()
        ref = piece(i, chip_at(1, 0), step // 2, step // 2)
        far_w.append((to_y, net.send(ref, ref, px)))

    def block_here(i):
        own_w[i].wait()
        for copy in far_w[i]:
            copy.wait_recv()

    chan = (half * 2 + c) * wr
    lens = [len_ref[kind * 2 + j] for j in range(2)]

    def mask_rows(j, edge, rows):
        frame = q * span - edge + lax.broadcasted_iota(jnp.int32, (rows, 128), 0)
        length = jnp.where(j == 0, lens[0], lens[1])
        return (frame >= 0) & (frame < length)

    long = span + 2 * HALO
    mid = span + 2 * EDGE

    def project(j, b):
        pre = lax.dot_general(
            R[j], W[rows_at(b * 256, 256), :], (((1,), (1,)), ((), ())),
            preferred_element_type=F32
        )
        lin = pre[:, 0:128]
        sig = jax.nn.sigmoid(pre[:, 128:256])
        G[j, b] = jnp.where(mask_rows(j, HALO, long), lin * sig, 0.0).astype(BF).astype(F32)
        A[j, b] = lin[HALO:HALO + span]
        S[j, b] = sig[HALO:HALO + span]

    def count_at(pair, chip, j):
        n = jnp.clip(len_ref[pair * 2 + j] - chip * span, 0, span)
        return jnp.full((8, 128), n, jnp.int32).astype(F32)

    own_counts = [count_at(kind, q, j) for j in range(2)]

    def convolve(j, b):
        lanes = cols_at(chan + b * 128, 128)
        acc = jnp.zeros((mid, 128), F32)
        for k in range(TAPS):
            acc = acc + ck_ref[k:k + 1, lanes] * G[j, b, pl.ds(1 + k, mid), :]
        C[j, b] = acc
        keep = mask_rows(j, 0, span)
        own = acc[EDGE:EDGE + span]
        total = jnp.sum(jnp.where(keep, own, 0.0), axis=0, keepdims=True)
        n = jnp.where(j == 0, own_counts[0][0:1], own_counts[1][0:1])
        dev = jnp.where(keep, own - total / jnp.maximum(n, 1.0), 0.0)
        st1[j, pl.ds(b, 1), :] = total
        st1[j, pl.ds(blocks + b, 1), :] = jnp.sum(dev * dev, axis=0, keepdims=True)

    def forward(j, first, last):
        @pl.loop(first, last)
        def _(b):
            project(j, b)
            convolve(j, b)

    pass_near(0)
    r_rim_mate, r_rim_core = rims_on(r_parts, R, HALO)
    pass_near(1)
    pass_far(0)
    for copy in (r_over, r_rim_core):
        copy.wait_recv()
    r_parts[2].wait()
    block_here(0)
    pass_near(2)
    pass_far(1)
    r_got = mate_on(r_rest, r_rim_mate, R, HALO)
    o_parts = spread_out(og_ref, O, EDGE, lambda h: cols_at(h * hw, hw))
    o_rest = o_parts[3]()
    o_over = o_parts[4]()
    pass_far(2)
    forward(jo, 0, 1)
    block_here(1)
    for copy in r_got:
        copy.wait_recv()
    forward(jo, 1, 2)
    forward(jm, 0, 2)
    block_here(2)
    forward(jo, 2, 3)
    o_rim_mate, o_rim_core = rims_on(o_parts, O, EDGE)
    forward(jm, 2, 3)

    me8 = kind * 4 + q
    peers8 = plane + [twin] + far

    def exchange(src, slots):
        own = local(src, slots.at[me8])
        copies = [net.send(src, slots.at[me8], peer) for peer in peers8]
        return own, copies

    own, copies = exchange(st1, sb1)
    o_got = mate_on(o_rest, o_rim_mate, O, EDGE)
    own.wait()
    for copy in copies:
        copy.wait_recv()
    counted = jnp.zeros((8, 128), F32)
    for g in range(len_ref.shape[0]):
        counted = counted + jnp.full((8, 128), len_ref[g], jnp.int32).astype(F32)
    total = jnp.zeros((8, 128), F32)
    for i in range(8):
        for j in range(2):
            total = total + sb1[i, j]
    mean = total / counted
    shift2 = jnp.zeros((8, 128), F32)
    for i in range(8):
        for j in range(2):
            n = count_at(i // 4, i % 4, j)
            d = sb1[i, j] / jnp.maximum(n, 1.0) - mean
            shift2 = shift2 + n * (d * d)
    vec[0] = total
    vec[1] = shift2
    var = (vec[0, blocks:2 * blocks] + vec[1, 0:blocks]) / counted[0:blocks]
    vec[2] = mean
    vec[3, 0:blocks] = lax.rsqrt(var + EPS)

    for copy in o_got + [o_over, o_rim_core]:
        copy.wait_recv()
    o_parts[2].wait()

    @pl.loop(0, 2 * blocks)
    def _(t):
        j, b = t // blocks, lax.rem(t, blocks)
        lanes = cols_at(chan + b * 128, 128)
        normed = (C[j, b] - vec[2, pl.ds(b, 1), :]) * vec[3, pl.ds(b, 1), :]
        shaped = gain_ref[lanes][None] * normed + shift_ref[lanes][None]
        smooth = jax.nn.sigmoid(shaped)
        up = O[j, :, cols_at(c * wr + b * 128, 128)].astype(F32)
        gs = jnp.where(
            mask_rows(j, EDGE, mid), up * smooth * (1.0 + shaped * (1.0 - smooth)), 0.0
        )
        D[j, b] = gs
        own = gs[EDGE:EDGE + span]
        st1_rows = jnp.sum(own, axis=0, keepdims=True)
        gain_rows = jnp.sum(own * normed[EDGE:EDGE + span], axis=0, keepdims=True)
        st2[1 + j, pl.ds(b, 1), :] = st1_rows
        st2[1 + j, pl.ds(blocks + b, 1), :] = gain_rows

    st2[0] = st2[1] + st2[2]
    own, copies = exchange(st2.at[0], sb2)

    own.wait()
    for copy in copies:
        copy.wait_recv()
    sums = jnp.zeros((8, 128), F32)
    for i in range(8):
        sums = sums + sb2[i]
    vec[4] = sums

    @pl.loop(0, 2 * blocks)
    def _(t):
        j, b = t // blocks, lax.rem(t, blocks)
        lanes = cols_at(chan + b * 128, 128)
        inverse = vec[3, pl.ds(b, 1), :]
        normed = (C[j, b] - vec[2, pl.ds(b, 1), :]) * inverse
        add, mul = vec[4, pl.ds(b, 1), :], vec[4, pl.ds(blocks + b, 1), :]
        D[j, b] = jnp.where(
            mask_rows(j, EDGE, mid),
            gain_ref[lanes][None] * inverse * (D[j, b] - (add + normed * mul) / counted[0:1]),
            0.0,
        )

    def back(b):
        lanes = cols_at(chan + b * 128, 128)

        @pl.loop(0, 2)
        def _(j):
            acc = jnp.zeros((span, 128), F32)
            for k in range(TAPS):
                acc = acc + ck_ref[k:k + 1, lanes] * D[j, b, pl.ds(TAPS - k, span), :]
            acc = jnp.where(mask_rows(j, 0, span), acc, 0.0)
            sig = S[j, b]
            to_lin = acc * sig
            GP[j, :, b * 256:b * 256 + 128] = to_lin.astype(BF)
            GP[j, :, b * 256 + 128:(b + 1) * 256] = (
                to_lin * A[j, b] * (1.0 - sig)
            ).astype(BF)

    tile = 512

    def input_grad():
        @pl.loop(0, 2 * (width // tile))
        def _(t):
            j, n = t // (width // tile), lax.rem(t, width // tile)
            lanes = cols_at(n * tile, tile)
            part = jnp.dot(GP[j], W[:, lanes], preferred_element_type=F32)
            igp[j, :, lanes] = part

        igs[...] = igp[:, rows_at((1 - c) * frames, frames), :].astype(BF)
        return net.send(igs, igr, core)

    def taps():
        @pl.loop(0, blocks)
        def _(b):
            for k in range(TAPS):
                part = jnp.zeros((1, 128), F32)
                for j in range(2):
                    part = part + jnp.sum(
                        D[j, b, pl.ds(EDGE, span), :] * G[j, b, pl.ds(EDGE + 1 + k, span), :],
                        axis=0, keepdims=True)
                kp[k // 4, b, k % 4:k % 4 + 1, :] = part
            kp[7, b, 3:4, :] = jnp.zeros((1, 128), F32)

        own = local(kp.at[me8], kb.at[me8])
        index = [kind * 4 + chip_at(dy, dx) for dy, dx in offsets]
        index += [(1 - kind) * 4 + i for i in [q] + [chip_at(dy, dx) for dy, dx in offsets]]
        return own, [net.send(kp.at[i], kb.at[me8], peer) for i, peer in zip(index, peers8)]

    eh = hw
    colsA, colsB = pl.ds(0, eh), pl.ds(eh, eh)

    def s1(m, b):
        rows = cols_at((2 * b + (kind if m else 1 - kind)) * 128, 128)

        @pl.loop(0, width // tile)
        def _(n):
            lanes = cols_at(n * tile, tile)
            acc = jnp.zeros((128, tile), F32)
            for j in range(2):
                acc = acc + lax.dot_general(
                    GP[j, :, rows], R[j, pl.ds(HALO, span), lanes], (((0,), (0,)), ((), ())),
                    preferred_element_type=F32)
            P[m, b, :, lanes] = acc

        sa[m, b, 0] = P[m, b, rows_at((1 - x) * 64, 64), 0:eh].astype(BF)
        sa[m, b, 1] = P[m, b, rows_at((1 - y) * 64, 64), eh:2 * eh].astype(BF)
        return [
            net.send(sa.at[m, b, 0], ra.at[m, b, 0], px),
            net.send(sa.at[m, b, 1], ra.at[m, b, 1], py),
        ]

    def s2(m, b, got):
        for copy in got:
            copy.wait_recv()
        sa2[m, b, 0] = (
            P[m, b, rows_at(x * 64 + (1 - y) * 32, 32), 0:eh]
            + ra[m, b, 0, rows_at((1 - y) * 32, 32), :].astype(F32)).astype(BF)
        sa2[m, b, 1] = (
            P[m, b, rows_at(y * 64 + (1 - x) * 32, 32), eh:2 * eh]
            + ra[m, b, 1, rows_at((1 - x) * 32, 32), :].astype(F32)).astype(BF)
        return [
            net.send(sa2.at[m, b, 0], ra2.at[m, b, 0], py),
            net.send(sa2.at[m, b, 1], ra2.at[m, b, 1], px),
        ]

    row_a, row_b = x * 64 + y * 32, y * 64 + x * 32

    def summed(m, b):
        return (
            P[m, b, rows_at(row_a, 32), 0:eh] + ra[m, b, 0, rows_at(y * 32, 32), :].astype(F32)
            + ra2[m, b, 0].astype(F32),
            P[m, b, rows_at(row_b, 32), eh:2 * eh] + ra[m, b, 1, rows_at(x * 32, 32), :].astype(F32)
            + ra2[m, b, 1].astype(F32),
        )

    def to_twin(b, got):
        for copy in got:
            copy.wait_recv()
        part_a, part_b = summed(0, b)
        sz[b, 0] = part_a.astype(BF)
        sz[b, 1] = part_b.astype(BF)
        return net.send(sz.at[b], rz.at[b], twin)

    def tile_of(core_at, b, start, size, cols):
        return F.at[rows_at(core_at * wr + b * 128 + start, size), cols]

    cols_a, cols_b = pl.ds(0, eh), pl.ds(eh, eh)

    def s3(b, got, from_twin):
        for copy in got:
            copy.wait_recv()
        part_a, part_b = summed(1, b)
        from_twin.wait_recv()
        fa, fb = tile_of(c, b, row_a, 32, cols_a), tile_of(c, b, row_b, 32, cols_b)
        fa[...] = (part_a + rz[b, 0].astype(F32)).astype(BF)
        fb[...] = (part_b + rz[b, 1].astype(F32)).astype(BF)
        return [net.send(fa, fa, py), net.send(fb, fb, px)]

    def s4(b, got):
        for copy in got:
            copy.wait_recv()
        fa, fb = tile_of(c, b, x * 64, 64, cols_a), tile_of(c, b, y * 64, 64, cols_b)
        return [net.send(fa, fa, px), net.send(fb, fb, py)]

    def s5(b, got):
        for copy in got:
            copy.wait_recv()
        ref = tile_of(c, b, 0, 128, pl.ds(0, width))
        return [net.send(ref, ref, core)]

    def k1(own, got):
        own.wait()
        for copy in got:
            copy.wait_recv()
        hc = half * 2 + c
        for b in range(blocks):
            part = jnp.zeros((8, 128), F32)
            for i in range(8):
                part = part + kb[i, b]
            kf_ref[hc, me8, b] = part
            kf_ref[hc, me8, b, 4:5, :] = vec[4, b:b + 1, :]
            kf_ref[hc, me8, b, 5:6, :] = vec[4, blocks + b:blocks + b + 1, :]
        ref = kf_ref.at[hc, me8]
        return [net.send(ref, ref, peer) for peer in peers8]

    def k2(got):
        for copy in got:
            copy.wait_recv()
        ref = kf_ref.at[half * 2 + c]
        return [net.send(ref, ref, core)]

    def k3(got):
        for copy in got:
            copy.wait_recv()
        ref = kf_ref.at[pl.ds(half * 2, 2)]
        return [net.send(ref, ref, mate)]

    def i1(got):
        got.wait_recv()
        igs2[...] = (
            igp[jm, rows_at(c * frames, frames), :] + igr[jm].astype(F32)
        ).astype(BF)
        return net.send(igs2, igr2, mate)

    def i2(got):
        got.wait_recv()
        ig_ref[...] = (
            igp[jo, rows_at(c * frames, frames), :] + igr[jo].astype(F32) + igr2[...].astype(F32)
        ).astype(BF)

    back(0)
    o0 = s1(0, 0)
    back(1)
    o1 = s1(0, 1)
    back(2)
    o0 = s2(0, 0, o0)
    o2 = s1(0, 2)
    o1 = s2(0, 1, o1)
    w0 = s1(1, 0)
    t0 = to_twin(0, o0)
    o2 = s2(0, 2, o2)
    w1 = s1(1, 1)
    t1 = to_twin(1, o1)
    w2 = s1(1, 2)
    ig = input_grad()
    w0 = s2(1, 0, w0)
    t2 = to_twin(2, o2)
    kown, k = taps()
    w1 = s2(1, 1, w1)
    ig = i1(ig)
    w2 = s2(1, 2, w2)
    w0 = s3(0, w0, t0)
    w1 = s3(1, w1, t1)
    k = k1(kown, k)
    w0 = s4(0, w0)
    w2 = s3(2, w2, t2)
    w1 = s4(1, w1)
    k = k2(k)
    w0 = s5(0, w0)
    w2 = s4(2, w2)
    k = k3(k)
    w1 = s5(1, w1)
    i2(ig)
    w2 = s5(2, w2)
    for copy in w0 + w1 + w2 + k:
        copy.wait_recv()
    net.drain()


def finish_kernel(ig_in, wg_in, kf_in, ig_out, wg_out, taps_out, gain_out, shift_out, wide, sems):
    copies = []

    def put(src, dst):
        copy = pltpu.make_async_copy(src, dst, sems.at[len(copies)])
        copy.start()
        copies.append(copy)

    put(ig_in, ig_out)
    parts = 6
    rows = wg_in.shape[0] // parts
    for i in range(parts):
        where = pl.ds(i * rows, rows)
        wide[where, :] = wg_in[where, :].astype(F32)
        put(wide.at[where], wg_out.at[where])
    owners, blocks = kf_in.shape[1], kf_in.shape[2]
    for hc in range(4):
        for b in range(blocks):
            lanes = pl.ds((hc * blocks + b) * 128, 128)
            for i in range(owners):
                n = min(4, taps_out.shape[0] - 4 * i)
                taps_out[4 * i:4 * i + n, lanes] = kf_in[hc, i, b, 0:n, :]
            shift_out[lanes] = kf_in[hc, 0, b, 4, :]
            gain_out[lanes] = kf_in[hc, 0, b, 5, :]
    for copy in copies:
        copy.wait()


def finish(in_grad, weight_grad, taps):
    any_space = pl.BlockSpec(memory_space=pl.ANY)
    width = in_grad.shape[1]
    return pl.pallas_call(
        finish_kernel,
        out_shape=(
            jax.ShapeDtypeStruct(in_grad.shape, BF),
            jax.ShapeDtypeStruct(weight_grad.shape, F32),
            jax.ShapeDtypeStruct((TAPS, width), F32),
            jax.ShapeDtypeStruct((width,), F32),
            jax.ShapeDtypeStruct((width,), F32),
        ),
        in_specs=[VM, VM, VM],
        out_specs=(any_space, any_space, VM, VM, VM),
        scratch_shapes=[pltpu.VMEM(weight_grad.shape, F32), pltpu.SemaphoreType.DMA((8,))],
        compiler_params=pltpu.CompilerParams(vmem_limit_bytes=20 * 1024 * 1024),
    )(in_grad, weight_grad, taps)


def fused(lengths, in_weight, codes, scales, out_grad, conv_kernel, bn_gain, bn_shift):
    frames, width = codes.shape
    wr = width // 4
    blocks = wr // 128
    span = 2 * frames
    long, mid = span + 2 * HALO, span + 2 * EDGE
    dma = pltpu.SemaphoreType.DMA
    hbm = pl.BlockSpec(memory_space=pltpu.HBM)
    smem = pl.BlockSpec(memory_space=pltpu.SMEM)

    def vm(shape, dtype=F32):
        return pltpu.VMEM(shape, dtype)

    return pl.pallas_call(
        fused_kernel,
        out_shape=(
            jax.ShapeDtypeStruct((frames, width), BF),
            jax.ShapeDtypeStruct((2 * wr, width), BF),
            jax.ShapeDtypeStruct((4, 8, blocks, 8, 128), F32),
        ),
        in_specs=[smem] + [hbm] * 7,
        out_specs=(VM, VM, VM),
        scratch_shapes=[
            vm((frames, width), BF),
            vm(scales.shape),
            vm(conv_kernel.shape),
            vm(bn_gain.shape),
            vm(bn_shift.shape),
            vm((frames, width), BF),
            vm((128, 128)),
            vm((2 * wr, width), BF),
            vm((2, long, width), BF),
            vm((2, mid, width // 2), BF),
            vm((2, blocks, long, 128)),
            vm((2, blocks, span, 128)),
            vm((2, blocks, span, 128)),
            vm((2, blocks, mid, 128)),
            vm((2, blocks, mid, 128)),
            vm((2, span, 2 * wr), BF),
            vm((2, 8, 128)),
            vm((8, 2, 8, 128)),
            vm((3, 8, 128)),
            vm((8, 8, 128)),
            vm((5, 8, 128)),
            vm((8, blocks, 8, 128)),
            vm((8, blocks, 8, 128)),
            vm((2, span, width)),
            vm((2, frames, width), BF),
            vm((2, frames, width), BF),
            vm((frames, width), BF),
            vm((frames, width), BF),
            vm((2, blocks, 128, width)),
            vm((2, blocks, 2, 64, width // 2), BF),
            vm((2, blocks, 2, 64, width // 2), BF),
            vm((2, blocks, 2, 32, width // 2), BF),
            vm((2, blocks, 2, 32, width // 2), BF),
            vm((blocks, 2, 32, width // 2), BF),
            vm((blocks, 2, 32, width // 2), BF),
            dma((128,)),
            dma((128,)),
            dma((16,)),
        ],
        compiler_params=pltpu.CompilerParams(
            collective_id=4, has_side_effects=True, vmem_limit_bytes=36 * 1024 * 1024
        ),
    )(*[
        pltpu.with_memory_space_constraint(operand, pltpu.HBM)
        for operand in (
            lengths, in_weight, codes, scales, out_grad, conv_kernel, bn_gain, bn_shift)
    ])


def padded_2(cells, sides, width):
    for axis, dim in sides:
        count = lax.axis_size(axis)
        ends = count - 1
        head = lax.slice_in_dim(cells, 0, width, axis=dim)
        tail = lax.slice_in_dim(cells, cells.shape[dim] - width, cells.shape[dim], axis=dim)
        cells = jnp.concatenate(
            [
                lax.ppermute(tail, axis, [(i, (i + 1) % count) for i in range(ends)]),
                cells,
                lax.ppermute(head, axis, [((i + 1) % count, i) for i in range(ends)]),
            ],
            axis=dim,
        )
    return cells


def restore(quantized, scales):
    per_channel = jnp.repeat(scales.T, 128, axis=1)
    return (quantized.astype(jnp.float32) * per_channel).astype(jnp.bfloat16)


def depthwise(padded, kernel, frames):
    running = jnp.zeros((frames, padded.shape[1]), jnp.float32)
    for offset in range(kernel.shape[0]):
        running = running + kernel[offset] * padded[offset : offset + frames].astype(jnp.float32)
    return running


def general(
    saved_codes, code_scales, lengths, in_weight, conv_kernel, bn_gain, bn_shift, out_grad
):
    frames = saved_codes.shape[1]
    feature_width = saved_codes.shape[2]
    tap_count = conv_kernel.shape[0]
    half_span = (tap_count - 1) // 2
    groups = lengths.shape[0]
    group_at = lax.axis_index("dp")
    length = jnp.sum(jnp.where(jnp.arange(groups, dtype=jnp.int32) == group_at, lengths, 0))
    counted = jnp.sum(lengths).astype(jnp.float32)
    first_frame = lax.axis_index("seq") * frames
    valid_mask = (first_frame + jnp.arange(frames, dtype=jnp.int32) < length).astype(jnp.float32)[
        :, None
    ]
    restored = restore(saved_codes[0], code_scales[0])
    weights = lax.all_gather(in_weight, "dp", axis=0, tiled=True)
    pre_act = lax.dot_general(
        restored, weights, (((1,), (1,)), ((), ())), preferred_element_type=jnp.float32
    )
    linear = pre_act[:, :feature_width]
    gate_part = jax.nn.sigmoid(pre_act[:, feature_width:])
    gated = (linear * gate_part * valid_mask).astype(jnp.bfloat16)
    gated_pad = padded_2(gated, (("seq", 0),), half_span)
    conv_out = depthwise(gated_pad, conv_kernel, frames)
    own_sum = jnp.sum(conv_out * valid_mask, axis=0)
    own_count = jnp.sum(valid_mask)
    centered = (conv_out - own_sum / jnp.maximum(own_count, 1.0)) * valid_mask
    own_square = jnp.sum(centered * centered, axis=0)
    total, spread, _ = sum_all(
        [own_sum, own_square, jnp.full_like(own_sum, own_count)], True, 0
    )
    mean_value = total / counted
    variance = spread / counted
    inverse = lax.rsqrt(variance + EPS)
    normed = (conv_out - mean_value) * inverse
    shaped = bn_gain * normed + bn_shift
    smooth = jax.nn.sigmoid(shaped)
    grad_shaped = (
        out_grad[0].astype(jnp.float32) * valid_mask * smooth * (1.0 + shaped * (1.0 - smooth))
    )
    shift_grad, gain_grad = sum_all(
        [jnp.sum(grad_shaped, axis=0), jnp.sum(grad_shaped * normed, axis=0)], False, 1
    )
    grad_conv = (
        bn_gain * inverse * (grad_shaped - (shift_grad + normed * gain_grad) / counted) * valid_mask
    )
    kernel_part = jnp.stack(
        [
            jnp.sum(grad_conv * gated_pad[offset : offset + frames].astype(jnp.float32), axis=0)
            for offset in range(tap_count)
        ]
    )
    grad_pad = padded_2(grad_conv, (("seq", 0),), half_span)
    grad_gated = depthwise(grad_pad, conv_kernel[::-1], frames) * valid_mask
    grad_pre = jnp.concatenate(
        [grad_gated * gate_part, grad_gated * linear * gate_part * (1.0 - gate_part)], axis=1
    ).astype(jnp.bfloat16)
    in_grad = jnp.dot(grad_pre, weights, preferred_element_type=jnp.float32)
    own_columns = lax.all_to_all(grad_pre[None], "dp", split_axis=2, concat_axis=0, tiled=True)
    local_rows = lax.dot_general(
        own_columns,
        lax.all_gather(restored[None], "dp", axis=0, tiled=True),
        (((0, 1), (0, 1)), ((), ())),
        preferred_element_type=jnp.float32,
    )
    weight_grad = lax.psum(local_rows, "seq")
    kernel_grad = lax.psum(kernel_part, ("dp", "seq"))
    return (in_grad.astype(jnp.bfloat16)[None], weight_grad, kernel_grad, gain_grad, shift_grad)


def per_device(
    saved_codes, code_scales, lengths, in_weight, conv_kernel, bn_gain, bn_shift, out_grad
):
    frames, width = saved_codes.shape[1:]
    square = (
        lax.axis_size("dp") == 4 and lax.axis_size("seq") == 8 and frames == 128
        and width == 1536 and conv_kernel.shape[0] == TAPS and lengths.shape[0] == 4
    )
    if not square:
        return general(
            saved_codes, code_scales, lengths, in_weight, conv_kernel, bn_gain, bn_shift, out_grad
        )
    in_grad, weight_grad, taps = fused(
        lengths, in_weight, saved_codes[0], jnp.transpose(code_scales, (1, 0, 2)), out_grad[0],
        conv_kernel, bn_gain, bn_shift
    )
    in_grad, weight_grad, kernel_grad, gain_grad, shift_grad = finish(in_grad, weight_grad, taps)
    return in_grad[None], weight_grad, kernel_grad, gain_grad, shift_grad


def solution(mesh):
    in_specs = (
        P("dp", "seq", None),
        P("dp", None, "seq"),
        P(),
        P("dp", None),
        P(),
        P(),
        P(),
        P("dp", "seq", None),
    )
    out_specs = (P("dp", "seq", None), P("dp", None), P(), P(), P())
    return jax.shard_map(
        per_device, mesh=mesh, in_specs=in_specs, out_specs=out_specs, check_vma=False
    )
```

```python
import functools

import jax
import jax.numpy as jnp
from jax import lax
from jax.experimental import pallas as pl
from jax.experimental.pallas import tpu as pltpu
from jax.sharding import PartitionSpec as P

EPS = 1e-05
MESH = pl.DeviceIdType.MESH
VM = pl.BlockSpec(memory_space=pltpu.VMEM)


def at(d, s):
    return {"dp": d, "seq": s}


def greet(peers):
    barrier = pltpu.get_barrier_semaphore()
    for peer in peers:
        pl.semaphore_signal(barrier, inc=1, device_id=peer, device_id_type=MESH)
    pl.semaphore_wait(barrier, len(peers))


def remote(src, dst, send, recv, peer):
    return pltpu.make_async_remote_copy(
        src_ref=src, dst_ref=dst, send_sem=send, recv_sem=recv, device_id=peer, device_id_type=MESH
    )


def ring_peers(me, count):
    return [lax.rem(me + k, count) for k in range(1, count)]


def merge(parts, stats):
    if not stats:
        return functools.reduce(lambda a, b: a + b, parts)
    sums = [part[0:16] for part in parts]
    squares = [part[16:32] for part in parts]
    counts = [part[32:48] for part in parts]
    total = functools.reduce(lambda a, b: a + b, sums)
    count = functools.reduce(lambda a, b: a + b, counts)
    mean = total / jnp.maximum(count, 1.0)
    spread = functools.reduce(lambda a, b: a + b, squares)
    for own, n in zip(sums, counts):
        shift = own / jnp.maximum(n, 1.0) - mean
        spread = spread + n * (shift * shift)
    return jnp.concatenate([total, spread, count], axis=0)


def sum_kernel(stats, dp_n, seq_n, x_ref, o_ref, near, far, mid, s1, r1, s2, r2):
    d, s = lax.axis_index("dp"), lax.axis_index("seq")
    plane = ring_peers(s, seq_n)
    line = ring_peers(d, dp_n)
    greet([at(d, j) for j in plane] + [at(j, s) for j in line])
    for k, j in enumerate(plane):
        remote(x_ref, near.at[s], s1.at[k], r1.at[s], at(d, j)).start()
    near[s] = x_ref[...]
    for k, j in enumerate(plane):
        copy = remote(x_ref, near.at[j], s1.at[k], r1.at[j], at(d, j))
        copy.wait_recv()
        copy.wait_send()
    mid[...] = merge([near[j] for j in range(seq_n)], stats)
    for k, j in enumerate(line):
        remote(mid, far.at[d], s2.at[k], r2.at[d], at(j, s)).start()
    far[d] = mid[...]
    for k, j in enumerate(line):
        copy = remote(mid, far.at[j], s2.at[k], r2.at[j], at(j, s))
        copy.wait_recv()
        copy.wait_send()
    o_ref[...] = merge([far[j] for j in range(dp_n)], stats)


def sum_all(vectors, stats, collective_id):
    dp_n, seq_n = lax.axis_size("dp"), lax.axis_size("seq")
    blocks = vectors[0].shape[-1] // 128
    stacked = jnp.stack([v.reshape(blocks, 128) for v in vectors])
    stacked = jnp.pad(stacked, ((0, 0), (0, 16 - blocks), (0, 0)))
    rows = 16 * len(vectors)
    shape = (rows, 128)
    out = pl.pallas_call(
        functools.partial(sum_kernel, stats, dp_n, seq_n),
        out_shape=jax.ShapeDtypeStruct(shape, jnp.float32),
        in_specs=[VM],
        out_specs=VM,
        scratch_shapes=[
            pltpu.VMEM((seq_n,) + shape, jnp.float32),
            pltpu.VMEM((dp_n,) + shape, jnp.float32),
            pltpu.VMEM(shape, jnp.float32),
            pltpu.SemaphoreType.DMA((seq_n,)),
            pltpu.SemaphoreType.DMA((seq_n,)),
            pltpu.SemaphoreType.DMA((dp_n,)),
            pltpu.SemaphoreType.DMA((dp_n,)),
        ],
        compiler_params=pltpu.CompilerParams(collective_id=collective_id, has_side_effects=True),
    )(stacked.reshape(shape))
    return out.reshape(len(vectors), 16, 128)[:, :blocks].reshape(len(vectors), blocks * 128)


HALO = 32
EDGE = 16
TAPS = 31
BF = jnp.bfloat16
F32 = jnp.float32


class Net:
    def __init__(self, send_sems, recv_sems):
        self.send_sems, self.recv_sems = send_sems, recv_sems
        self.used = 0
        self.sent = []

    def send(self, src, dst, peer):
        copy = remote(src, dst, self.send_sems.at[self.used], self.recv_sems.at[self.used], peer)
        self.used += 1
        copy.start()
        self.sent.append(copy)
        return copy

    def drain(self):
        for copy in self.sent:
            copy.wait_send()


def rows_at(start, size):
    return pl.ds(pl.multiple_of(start, 16), size)


def cols_at(start, size):
    return pl.ds(pl.multiple_of(start, 128), size)


def fused_kernel(
    len_ref, w_ref, codes_hbm, scale_hbm, og_ref, ck_hbm, gain_hbm, shift_hbm,
    ig_ref, F, kf_ref,
    codes_ref, scale_ref, ck_ref, gain_ref, shift_ref, res_ref, by_frame, W, R, O, G, A, S, C, D, GP,
    st1, sb1, st2, sb2, vec,
    kp, kb,
    igp, igs, igr, igs2, igr2,
    P, sa, ra, sa2, ra2, sz, rz,
    send_sems, recv_sems, local_sems,
):
    z, s = lax.axis_index("dp"), lax.axis_index("seq")
    c, x, y = lax.rem(s, 2), lax.rem(s // 2, 2), s // 4
    q = s // 2
    kind, half = z // 2, lax.rem(z, 2)
    mate_z = z + 1 - 2 * half
    twin_z = z + 2 - 4 * kind
    jo, jm = half, 1 - half
    frames = codes_hbm.shape[0]
    span = 2 * frames
    width = codes_hbm.shape[1]
    hw = width // 2

    def chip_at(dy, dx):
        yy = 1 - y if dy else y
        xx = 1 - x if dx else x
        return yy * 2 + xx

    core = at(z, s + 1 - 2 * c)
    mate = at(mate_z, s)
    twin = at(twin_z, s)
    offsets = [(0, 1), (1, 0), (1, 1)]
    plane = [at(z, chip_at(dy, dx) * 2 + c) for dy, dx in offsets]
    px, py = plane[0], plane[1]
    far = [at(twin_z, chip_at(dy, dx) * 2 + c) for dy, dx in offsets]
    to_q = lax.rem(q + 2 * c + 3, 4)
    from_q = lax.rem(q + 5 - 2 * c, 4)
    net = Net(send_sems, recv_sems)
    locals_ = []

    def local(src, dst):
        copy = pltpu.make_async_copy(src, dst, local_sems.at[len(locals_)])
        copy.start()
        locals_.append(copy)
        return copy

    loads = [
        local(src, dst) for src, dst in (
            (codes_hbm, codes_ref), (scale_hbm, scale_ref), (ck_hbm, ck_ref),
            (gain_hbm, gain_ref), (shift_hbm, shift_ref))
    ]
    wr = W.shape[0] // 2
    blocks = wr // 128
    own_w = [
        local(w_ref.at[rows_at(c * wr + b * 128, 128)], W.at[rows_at((2 * b + kind) * 128, 128)])
        for b in range(blocks)
    ]
    greet([core, mate, twin] + plane + far)

    def spread_out(src, dst, edge, window):
        mine = rows_at(edge + frames * c, frames)
        rim_src = rows_at(c * (frames - edge), edge)
        rim_dst = rows_at(edge + frames * c + c * (frames - edge), edge)
        rim = rows_at((1 - c) * (edge + span), edge)
        rest_src = rows_at((1 - c) * edge, frames - edge)
        rest_dst = rows_at(edge + frames * c + (1 - c) * edge, frames - edge)
        here, there = window(half), window(1 - half)
        side = net.send(src.at[rim_src, there], dst.at[jo, rim_dst], mate)
        rim_own = net.send(src.at[rim_src, here], dst.at[jo, rim], at(z, to_q * 2 + c))
        own = local(src.at[:, here], dst.at[jo, mine])

        def rest():
            return net.send(src.at[rest_src, there], dst.at[jo, rest_dst], mate)

        def over():
            return net.send(src.at[:, here], dst.at[jo, mine], core)

        return side, rim_own, own, rest, over

    def rims_on(parts, dst, edge):
        rim_dst = rows_at(edge + frames * c + c * (frames - edge), edge)
        rim = rows_at((1 - c) * (edge + span), edge)
        side, rim_own = parts[:2]
        side.wait_recv()
        rim_mate = net.send(dst.at[jm, rim_dst], dst.at[jm, rim], at(z, to_q * 2 + c))
        rim_own.wait_recv()
        ref = dst.at[jo, rim]
        return rim_mate, net.send(ref, ref, core)

    def mate_on(rest, rim_mate, dst, edge):
        rim = rows_at((1 - c) * (edge + span), edge)
        rim_mate.wait_recv()
        ref = dst.at[jm, rim]
        got = [net.send(ref, ref, core)]
        rest.wait_recv()
        ref = dst.at[jm, rows_at(edge + frames * c, frames)]
        return got + [net.send(ref, ref, core)]

    step = 32
    wsend = []

    def weights_out(i):
        if i:
            wsend[i - 1].wait_send()
            net.sent = [copy for copy in net.sent if copy is not wsend[i - 1]]
        wsend.append(net.send(
            w_ref.at[rows_at(c * wr + i * 128 + q * step, step)],
            W.at[rows_at((2 * i + kind) * 128 + q * step, step)], twin))

    weights_out(0)
    for copy in loads:
        copy.wait()
    for b in range(width // 128):
        by_frame[b:b + 1, :] = scale_ref[b]
    columns = jnp.transpose(by_frame[...])
    for b in range(width // 128):
        lanes = pl.ds(b * 128, 128)
        res_ref[:, lanes] = (
            codes_ref[:, lanes].astype(F32) * columns[:, b:b + 1]
        ).astype(BF)

    r_parts = spread_out(res_ref, R, HALO, lambda h: pl.ds(0, width))
    r_over = r_parts[4]()
    near_w, far_w = [], []

    def piece(i, chip, start, size):
        return W.at[rows_at((2 * i + 1 - kind) * 128 + chip * step + start, size)]

    def pass_near(i):
        wsend[i].wait_recv()
        ref = piece(i, q, 0, step)
        near_w.append((net.send(ref, ref, px), net.send(ref, ref, py)))

    def pass_far(i):
        from_x, from_y = near_w[i]
        from_x.wait_recv()
        ref = piece(i, chip_at(0, 1), 0, step // 2)
        to_y = net.send(ref, ref, py)
        from_y.wait_recv()
        ref = piece(i, chip_at(1, 0), step // 2, step // 2)
        far_w.append((to_y, net.send(ref, ref, px)))

    def block_here(i):
        own_w[i].wait()
        for copy in far_w[i]:
            copy.wait_recv()

    chan = (half * 2 + c) * wr
    lens = [len_ref[kind * 2 + j] for j in range(2)]

    def mask_rows(j, edge, rows):
        frame = q * span - edge + lax.broadcasted_iota(jnp.int32, (rows, 128), 0)
        length = jnp.where(j == 0, lens[0], lens[1])
        return (frame >= 0) & (frame < length)

    long = span + 2 * HALO
    mid = span + 2 * EDGE

    def project(j, b):
        pre = lax.dot_general(
            R[j], W[rows_at(b * 256, 256), :], (((1,), (1,)), ((), ())),
            preferred_element_type=F32
        )
        lin = pre[:, 0:128]
        sig = jax.nn.sigmoid(pre[:, 128:256])
        G[j, b] = jnp.where(mask_rows(j, HALO, long), lin * sig, 0.0).astype(BF).astype(F32)
        A[j, b] = lin[HALO:HALO + span]
        S[j, b] = sig[HALO:HALO + span]

    def count_at(pair, chip, j):
        n = jnp.clip(len_ref[pair * 2 + j] - chip * span, 0, span)
        return jnp.full((8, 128), n, jnp.int32).astype(F32)

    own_counts = [count_at(kind, q, j) for j in range(2)]

    def convolve(j, b):
        lanes = cols_at(chan + b * 128, 128)
        acc = jnp.zeros((mid, 128), F32)
        for k in range(TAPS):
            acc = acc + ck_ref[k:k + 1, lanes] * G[j, b, pl.ds(1 + k, mid), :]
        C[j, b] = acc
        keep = mask_rows(j, 0, span)
        own = acc[EDGE:EDGE + span]
        total = jnp.sum(jnp.where(keep, own, 0.0), axis=0, keepdims=True)
        n = jnp.where(j == 0, own_counts[0][0:1], own_counts[1][0:1])
        dev = jnp.where(keep, own - total / jnp.maximum(n, 1.0), 0.0)
        st1[j, pl.ds(b, 1), :] = total
        st1[j, pl.ds(blocks + b, 1), :] = jnp.sum(dev * dev, axis=0, keepdims=True)

    def forward(j, first, last):
        @pl.loop(first, last)
        def _(b):
            project(j, b)
            convolve(j, b)

    weights_out(1)
    pass_near(0)
    weights_out(2)
    r_rest = r_parts[3]()
    r_rim_mate, r_rim_core = rims_on(r_parts, R, HALO)
    pass_near(1)
    pass_far(0)
    for copy in (r_over, r_rim_core):
        copy.wait_recv()
    r_parts[2].wait()
    block_here(0)
    pass_near(2)
    pass_far(1)
    r_got = mate_on(r_rest, r_rim_mate, R, HALO)
    o_parts = spread_out(og_ref, O, EDGE, lambda h: cols_at(h * hw, hw))
    o_rest = o_parts[3]()
    o_over = o_parts[4]()
    pass_far(2)
    forward(jo, 0, 1)
    block_here(1)
    for copy in r_got:
        copy.wait_recv()
    forward(jo, 1, 2)
    forward(jm, 0, 2)
    block_here(2)
    forward(jo, 2, 3)
    o_rim_mate, o_rim_core = rims_on(o_parts, O, EDGE)
    forward(jm, 2, 3)

    me8 = kind * 4 + q
    peers8 = plane + [twin] + far

    def exchange(src, slots):
        own = local(src, slots.at[me8])
        copies = [net.send(src, slots.at[me8], peer) for peer in peers8]
        return own, copies

    own, copies = exchange(st1, sb1)
    o_got = mate_on(o_rest, o_rim_mate, O, EDGE)
    own.wait()
    for copy in copies:
        copy.wait_recv()
    counted = jnp.zeros((8, 128), F32)
    for g in range(len_ref.shape[0]):
        counted = counted + jnp.full((8, 128), len_ref[g], jnp.int32).astype(F32)
    total = jnp.zeros((8, 128), F32)
    for i in range(8):
        for j in range(2):
            total = total + sb1[i, j]
    mean = total / counted
    shift2 = jnp.zeros((8, 128), F32)
    for i in range(8):
        for j in range(2):
            n = count_at(i // 4, i % 4, j)
            d = sb1[i, j] / jnp.maximum(n, 1.0) - mean
            shift2 = shift2 + n * (d * d)
    vec[0] = total
    vec[1] = shift2
    var = (vec[0, blocks:2 * blocks] + vec[1, 0:blocks]) / counted[0:blocks]
    vec[2] = mean
    vec[3, 0:blocks] = lax.rsqrt(var + EPS)

    for copy in o_got + [o_over, o_rim_core]:
        copy.wait_recv()
    o_parts[2].wait()

    @pl.loop(0, 2 * blocks)
    def _(t):
        j, b = t // blocks, lax.rem(t, blocks)
        lanes = cols_at(chan + b * 128, 128)
        normed = (C[j, b] - vec[2, pl.ds(b, 1), :]) * vec[3, pl.ds(b, 1), :]
        shaped = gain_ref[lanes][None] * normed + shift_ref[lanes][None]
        smooth = jax.nn.sigmoid(shaped)
        up = O[j, :, cols_at(c * wr + b * 128, 128)].astype(F32)
        gs = jnp.where(
            mask_rows(j, EDGE, mid), up * smooth * (1.0 + shaped * (1.0 - smooth)), 0.0
        )
        D[j, b] = gs
        own = gs[EDGE:EDGE + span]
        st1_rows = jnp.sum(own, axis=0, keepdims=True)
        gain_rows = jnp.sum(own * normed[EDGE:EDGE + span], axis=0, keepdims=True)
        st2[1 + j, pl.ds(b, 1), :] = st1_rows
        st2[1 + j, pl.ds(blocks + b, 1), :] = gain_rows

    st2[0] = st2[1] + st2[2]
    own, copies = exchange(st2.at[0], sb2)

    own.wait()
    for copy in copies:
        copy.wait_recv()
    sums = jnp.zeros((8, 128), F32)
    for i in range(8):
        sums = sums + sb2[i]
    vec[4] = sums

    @pl.loop(0, 2 * blocks)
    def _(t):
        j, b = t // blocks, lax.rem(t, blocks)
        lanes = cols_at(chan + b * 128, 128)
        inverse = vec[3, pl.ds(b, 1), :]
        normed = (C[j, b] - vec[2, pl.ds(b, 1), :]) * inverse
        add, mul = vec[4, pl.ds(b, 1), :], vec[4, pl.ds(blocks + b, 1), :]
        D[j, b] = jnp.where(
            mask_rows(j, EDGE, mid),
            gain_ref[lanes][None] * inverse * (D[j, b] - (add + normed * mul) / counted[0:1]),
            0.0,
        )

    def back(b):
        lanes = cols_at(chan + b * 128, 128)

        @pl.loop(0, 2)
        def _(j):
            acc = jnp.zeros((span, 128), F32)
            for k in range(TAPS):
                acc = acc + ck_ref[k:k + 1, lanes] * D[j, b, pl.ds(TAPS - k, span), :]
            acc = jnp.where(mask_rows(j, 0, span), acc, 0.0)
            sig = S[j, b]
            to_lin = acc * sig
            GP[j, :, b * 256:b * 256 + 128] = to_lin.astype(BF)
            GP[j, :, b * 256 + 128:(b + 1) * 256] = (
                to_lin * A[j, b] * (1.0 - sig)
            ).astype(BF)

    tile = 512

    def input_grad():
        @pl.loop(0, 2 * (width // tile))
        def _(t):
            j, n = t // (width // tile), lax.rem(t, width // tile)
            lanes = cols_at(n * tile, tile)
            part = jnp.dot(GP[j], W[:, lanes], preferred_element_type=F32)
            igp[j, :, lanes] = part

        igs[...] = igp[:, rows_at((1 - c) * frames, frames), :].astype(BF)
        return net.send(igs, igr, core)

    def taps():
        @pl.loop(0, blocks)
        def _(b):
            for k in range(TAPS):
                part = jnp.zeros((1, 128), F32)
                for j in range(2):
                    part = part + jnp.sum(
                        D[j, b, pl.ds(EDGE, span), :] * G[j, b, pl.ds(EDGE + 1 + k, span), :],
                        axis=0, keepdims=True)
                kp[k // 4, b, k % 4:k % 4 + 1, :] = part
            kp[7, b, 3:4, :] = jnp.zeros((1, 128), F32)

        own = local(kp.at[me8], kb.at[me8])
        index = [kind * 4 + chip_at(dy, dx) for dy, dx in offsets]
        index += [(1 - kind) * 4 + i for i in [q] + [chip_at(dy, dx) for dy, dx in offsets]]
        return own, [net.send(kp.at[i], kb.at[me8], peer) for i, peer in zip(index, peers8)]

    eh = hw
    colsA, colsB = pl.ds(0, eh), pl.ds(eh, eh)

    def s1(m, b):
        rows = cols_at((2 * b + (kind if m else 1 - kind)) * 128, 128)

        @pl.loop(0, width // tile)
        def _(n):
            lanes = cols_at(n * tile, tile)
            acc = jnp.zeros((128, tile), F32)
            for j in range(2):
                acc = acc + lax.dot_general(
                    GP[j, :, rows], R[j, pl.ds(HALO, span), lanes], (((0,), (0,)), ((), ())),
                    preferred_element_type=F32)
            P[m, b, :, lanes] = acc

        sa[m, b, 0] = P[m, b, rows_at((1 - x) * 64, 64), 0:eh].astype(BF)
        sa[m, b, 1] = P[m, b, rows_at((1 - y) * 64, 64), eh:2 * eh].astype(BF)
        return [
            net.send(sa.at[m, b, 0], ra.at[m, b, 0], px),
            net.send(sa.at[m, b, 1], ra.at[m, b, 1], py),
        ]

    def s2(m, b, got):
        for copy in got:
            copy.wait_recv()
        sa2[m, b, 0] = (
            P[m, b, rows_at(x * 64 + (1 - y) * 32, 32), 0:eh]
            + ra[m, b, 0, rows_at((1 - y) * 32, 32), :].astype(F32)).astype(BF)
        sa2[m, b, 1] = (
            P[m, b, rows_at(y * 64 + (1 - x) * 32, 32), eh:2 * eh]
            + ra[m, b, 1, rows_at((1 - x) * 32, 32), :].astype(F32)).astype(BF)
        return [
            net.send(sa2.at[m, b, 0], ra2.at[m, b, 0], py),
            net.send(sa2.at[m, b, 1], ra2.at[m, b, 1], px),
        ]

    row_a, row_b = x * 64 + y * 32, y * 64 + x * 32

    def summed(m, b):
        return (
            P[m, b, rows_at(row_a, 32), 0:eh] + ra[m, b, 0, rows_at(y * 32, 32), :].astype(F32)
            + ra2[m, b, 0].astype(F32),
            P[m, b, rows_at(row_b, 32), eh:2 * eh] + ra[m, b, 1, rows_at(x * 32, 32), :].astype(F32)
            + ra2[m, b, 1].astype(F32),
        )

    def to_twin(b, got):
        for copy in got:
            copy.wait_recv()
        part_a, part_b = summed(0, b)
        sz[b, 0] = part_a.astype(BF)
        sz[b, 1] = part_b.astype(BF)
        return net.send(sz.at[b], rz.at[b], twin)

    def tile_of(core_at, b, start, size, cols):
        return F.at[rows_at(core_at * wr + b * 128 + start, size), cols]

    cols_a, cols_b = pl.ds(0, eh), pl.ds(eh, eh)

    def s3(b, got, from_twin):
        for copy in got:
            copy.wait_recv()
        part_a, part_b = summed(1, b)
        from_twin.wait_recv()
        fa, fb = tile_of(c, b, row_a, 32, cols_a), tile_of(c, b, row_b, 32, cols_b)
        fa[...] = (part_a + rz[b, 0].astype(F32)).astype(BF)
        fb[...] = (part_b + rz[b, 1].astype(F32)).astype(BF)
        return [net.send(fa, fa, py), net.send(fb, fb, px)]

    def s4(b, got):
        for copy in got:
            copy.wait_recv()
        fa, fb = tile_of(c, b, x * 64, 64, cols_a), tile_of(c, b, y * 64, 64, cols_b)
        return [net.send(fa, fa, px), net.send(fb, fb, py)]

    def s5(b, got):
        for copy in got:
            copy.wait_recv()
        ref = tile_of(c, b, 0, 128, pl.ds(0, width))
        return [net.send(ref, ref, core)]

    def k1(own, got):
        own.wait()
        for copy in got:
            copy.wait_recv()
        hc = half * 2 + c
        for b in range(blocks):
            part = jnp.zeros((8, 128), F32)
            for i in range(8):
                part = part + kb[i, b]
            kf_ref[hc, me8, b] = part
            kf_ref[hc, me8, b, 4:5, :] = vec[4, b:b + 1, :]
            kf_ref[hc, me8, b, 5:6, :] = vec[4, blocks + b:blocks + b + 1, :]
        ref = kf_ref.at[hc, me8]
        return [net.send(ref, ref, peer) for peer in peers8]

    def k2(got):
        for copy in got:
            copy.wait_recv()
        ref = kf_ref.at[half * 2 + c]
        return [net.send(ref, ref, core)]

    def k3(got):
        for copy in got:
            copy.wait_recv()
        ref = kf_ref.at[pl.ds(half * 2, 2)]
        return [net.send(ref, ref, mate)]

    def i1(got):
        got.wait_recv()
        igs2[...] = (
            igp[jm, rows_at(c * frames, frames), :] + igr[jm].astype(F32)
        ).astype(BF)
        return net.send(igs2, igr2, mate)

    def i2(got):
        got.wait_recv()
        ig_ref[...] = (
            igp[jo, rows_at(c * frames, frames), :] + igr[jo].astype(F32) + igr2[...].astype(F32)
        ).astype(BF)

    back(0)
    o0 = s1(0, 0)
    back(1)
    o1 = s1(0, 1)
    back(2)
    o0 = s2(0, 0, o0)
    o2 = s1(0, 2)
    o1 = s2(0, 1, o1)
    w0 = s1(1, 0)
    t0 = to_twin(0, o0)
    o2 = s2(0, 2, o2)
    w1 = s1(1, 1)
    t1 = to_twin(1, o1)
    w2 = s1(1, 2)
    ig = input_grad()
    w0 = s2(1, 0, w0)
    t2 = to_twin(2, o2)
    kown, k = taps()
    w1 = s2(1, 1, w1)
    ig = i1(ig)
    w2 = s2(1, 2, w2)
    w0 = s3(0, w0, t0)
    w1 = s3(1, w1, t1)
    k = k1(kown, k)
    w0 = s4(0, w0)
    w2 = s3(2, w2, t2)
    w1 = s4(1, w1)
    k = k2(k)
    w0 = s5(0, w0)
    w2 = s4(2, w2)
    k = k3(k)
    w1 = s5(1, w1)
    i2(ig)
    w2 = s5(2, w2)
    for copy in w0 + w1 + w2 + k:
        copy.wait_recv()
    net.drain()


def finish_kernel(ig_in, wg_in, kf_in, ig_out, wg_out, taps_out, gain_out, shift_out, wide, sems):
    copies = []

    def put(src, dst):
        copy = pltpu.make_async_copy(src, dst, sems.at[len(copies)])
        copy.start()
        copies.append(copy)

    put(ig_in, ig_out)
    parts = 6
    rows = wg_in.shape[0] // parts
    for i in range(parts):
        where = pl.ds(i * rows, rows)
        wide[where, :] = wg_in[where, :].astype(F32)
        put(wide.at[where], wg_out.at[where])
    owners, blocks = kf_in.shape[1], kf_in.shape[2]
    for hc in range(4):
        for b in range(blocks):
            lanes = pl.ds((hc * blocks + b) * 128, 128)
            for i in range(owners):
                n = min(4, taps_out.shape[0] - 4 * i)
                taps_out[4 * i:4 * i + n, lanes] = kf_in[hc, i, b, 0:n, :]
            shift_out[lanes] = kf_in[hc, 0, b, 4, :]
            gain_out[lanes] = kf_in[hc, 0, b, 5, :]
    for copy in copies:
        copy.wait()


def finish(in_grad, weight_grad, taps):
    any_space = pl.BlockSpec(memory_space=pl.ANY)
    width = in_grad.shape[1]
    return pl.pallas_call(
        finish_kernel,
        out_shape=(
            jax.ShapeDtypeStruct(in_grad.shape, BF),
            jax.ShapeDtypeStruct(weight_grad.shape, F32),
            jax.ShapeDtypeStruct((TAPS, width), F32),
            jax.ShapeDtypeStruct((width,), F32),
            jax.ShapeDtypeStruct((width,), F32),
        ),
        in_specs=[VM, VM, VM],
        out_specs=(any_space, any_space, VM, VM, VM),
        scratch_shapes=[pltpu.VMEM(weight_grad.shape, F32), pltpu.SemaphoreType.DMA((8,))],
        compiler_params=pltpu.CompilerParams(vmem_limit_bytes=20 * 1024 * 1024),
    )(in_grad, weight_grad, taps)


def fused(lengths, in_weight, codes, scales, out_grad, conv_kernel, bn_gain, bn_shift):
    frames, width = codes.shape
    wr = width // 4
    blocks = wr // 128
    span = 2 * frames
    long, mid = span + 2 * HALO, span + 2 * EDGE
    dma = pltpu.SemaphoreType.DMA
    hbm = pl.BlockSpec(memory_space=pltpu.HBM)
    smem = pl.BlockSpec(memory_space=pltpu.SMEM)

    def vm(shape, dtype=F32):
        return pltpu.VMEM(shape, dtype)

    return pl.pallas_call(
        fused_kernel,
        out_shape=(
            jax.ShapeDtypeStruct((frames, width), BF),
            jax.ShapeDtypeStruct((2 * wr, width), BF),
            jax.ShapeDtypeStruct((4, 8, blocks, 8, 128), F32),
        ),
        in_specs=[smem] + [hbm] * 7,
        out_specs=(VM, VM, VM),
        scratch_shapes=[
            vm((frames, width), BF),
            vm(scales.shape),
            vm(conv_kernel.shape),
            vm(bn_gain.shape),
            vm(bn_shift.shape),
            vm((frames, width), BF),
            vm((128, 128)),
            vm((2 * wr, width), BF),
            vm((2, long, width), BF),
            vm((2, mid, width // 2), BF),
            vm((2, blocks, long, 128)),
            vm((2, blocks, span, 128)),
            vm((2, blocks, span, 128)),
            vm((2, blocks, mid, 128)),
            vm((2, blocks, mid, 128)),
            vm((2, span, 2 * wr), BF),
            vm((2, 8, 128)),
            vm((8, 2, 8, 128)),
            vm((3, 8, 128)),
            vm((8, 8, 128)),
            vm((5, 8, 128)),
            vm((8, blocks, 8, 128)),
            vm((8, blocks, 8, 128)),
            vm((2, span, width)),
            vm((2, frames, width), BF),
            vm((2, frames, width), BF),
            vm((frames, width), BF),
            vm((frames, width), BF),
            vm((2, blocks, 128, width)),
            vm((2, blocks, 2, 64, width // 2), BF),
            vm((2, blocks, 2, 64, width // 2), BF),
            vm((2, blocks, 2, 32, width // 2), BF),
            vm((2, blocks, 2, 32, width // 2), BF),
            vm((blocks, 2, 32, width // 2), BF),
            vm((blocks, 2, 32, width // 2), BF),
            dma((128,)),
            dma((128,)),
            dma((16,)),
        ],
        compiler_params=pltpu.CompilerParams(
            collective_id=4, has_side_effects=True, vmem_limit_bytes=36 * 1024 * 1024
        ),
    )(*[
        pltpu.with_memory_space_constraint(operand, pltpu.HBM)
        for operand in (
            lengths, in_weight, codes, scales, out_grad, conv_kernel, bn_gain, bn_shift)
    ])


def padded_2(cells, sides, width):
    for axis, dim in sides:
        count = lax.axis_size(axis)
        ends = count - 1
        head = lax.slice_in_dim(cells, 0, width, axis=dim)
        tail = lax.slice_in_dim(cells, cells.shape[dim] - width, cells.shape[dim], axis=dim)
        cells = jnp.concatenate(
            [
                lax.ppermute(tail, axis, [(i, (i + 1) % count) for i in range(ends)]),
                cells,
                lax.ppermute(head, axis, [((i + 1) % count, i) for i in range(ends)]),
            ],
            axis=dim,
        )
    return cells


def restore(quantized, scales):
    per_channel = jnp.repeat(scales.T, 128, axis=1)
    return (quantized.astype(jnp.float32) * per_channel).astype(jnp.bfloat16)


def depthwise(padded, kernel, frames):
    running = jnp.zeros((frames, padded.shape[1]), jnp.float32)
    for offset in range(kernel.shape[0]):
        running = running + kernel[offset] * padded[offset : offset + frames].astype(jnp.float32)
    return running


def general(
    saved_codes, code_scales, lengths, in_weight, conv_kernel, bn_gain, bn_shift, out_grad
):
    frames = saved_codes.shape[1]
    feature_width = saved_codes.shape[2]
    tap_count = conv_kernel.shape[0]
    half_span = (tap_count - 1) // 2
    groups = lengths.shape[0]
    group_at = lax.axis_index("dp")
    length = jnp.sum(jnp.where(jnp.arange(groups, dtype=jnp.int32) == group_at, lengths, 0))
    counted = jnp.sum(lengths).astype(jnp.float32)
    first_frame = lax.axis_index("seq") * frames
    valid_mask = (first_frame + jnp.arange(frames, dtype=jnp.int32) < length).astype(jnp.float32)[
        :, None
    ]
    restored = restore(saved_codes[0], code_scales[0])
    weights = lax.all_gather(in_weight, "dp", axis=0, tiled=True)
    pre_act = lax.dot_general(
        restored, weights, (((1,), (1,)), ((), ())), preferred_element_type=jnp.float32
    )
    linear = pre_act[:, :feature_width]
    gate_part = jax.nn.sigmoid(pre_act[:, feature_width:])
    gated = (linear * gate_part * valid_mask).astype(jnp.bfloat16)
    gated_pad = padded_2(gated, (("seq", 0),), half_span)
    conv_out = depthwise(gated_pad, conv_kernel, frames)
    own_sum = jnp.sum(conv_out * valid_mask, axis=0)
    own_count = jnp.sum(valid_mask)
    centered = (conv_out - own_sum / jnp.maximum(own_count, 1.0)) * valid_mask
    own_square = jnp.sum(centered * centered, axis=0)
    total, spread, _ = sum_all(
        [own_sum, own_square, jnp.full_like(own_sum, own_count)], True, 0
    )
    mean_value = total / counted
    variance = spread / counted
    inverse = lax.rsqrt(variance + EPS)
    normed = (conv_out - mean_value) * inverse
    shaped = bn_gain * normed + bn_shift
    smooth = jax.nn.sigmoid(shaped)
    grad_shaped = (
        out_grad[0].astype(jnp.float32) * valid_mask * smooth * (1.0 + shaped * (1.0 - smooth))
    )
    shift_grad, gain_grad = sum_all(
        [jnp.sum(grad_shaped, axis=0), jnp.sum(grad_shaped * normed, axis=0)], False, 1
    )
    grad_conv = (
        bn_gain * inverse * (grad_shaped - (shift_grad + normed * gain_grad) / counted) * valid_mask
    )
    kernel_part = jnp.stack(
        [
            jnp.sum(grad_conv * gated_pad[offset : offset + frames].astype(jnp.float32), axis=0)
            for offset in range(tap_count)
        ]
    )
    grad_pad = padded_2(grad_conv, (("seq", 0),), half_span)
    grad_gated = depthwise(grad_pad, conv_kernel[::-1], frames) * valid_mask
    grad_pre = jnp.concatenate(
        [grad_gated * gate_part, grad_gated * linear * gate_part * (1.0 - gate_part)], axis=1
    ).astype(jnp.bfloat16)
    in_grad = jnp.dot(grad_pre, weights, preferred_element_type=jnp.float32)
    own_columns = lax.all_to_all(grad_pre[None], "dp", split_axis=2, concat_axis=0, tiled=True)
    local_rows = lax.dot_general(
        own_columns,
        lax.all_gather(restored[None], "dp", axis=0, tiled=True),
        (((0, 1), (0, 1)), ((), ())),
        preferred_element_type=jnp.float32,
    )
    weight_grad = lax.psum(local_rows, "seq")
    kernel_grad = lax.psum(kernel_part, ("dp", "seq"))
    return (in_grad.astype(jnp.bfloat16)[None], weight_grad, kernel_grad, gain_grad, shift_grad)


def per_device(
    saved_codes, code_scales, lengths, in_weight, conv_kernel, bn_gain, bn_shift, out_grad
):
    frames, width = saved_codes.shape[1:]
    square = (
        lax.axis_size("dp") == 4 and lax.axis_size("seq") == 8 and frames == 128
        and width == 1536 and conv_kernel.shape[0] == TAPS and lengths.shape[0] == 4
    )
    if not square:
        return general(
            saved_codes, code_scales, lengths, in_weight, conv_kernel, bn_gain, bn_shift, out_grad
        )
    in_grad, weight_grad, taps = fused(
        lengths, in_weight, saved_codes[0], jnp.transpose(code_scales, (1, 0, 2)), out_grad[0],
        conv_kernel, bn_gain, bn_shift
    )
    in_grad, weight_grad, kernel_grad, gain_grad, shift_grad = finish(in_grad, weight_grad, taps)
    return in_grad[None], weight_grad, kernel_grad, gain_grad, shift_grad


def solution(mesh):
    in_specs = (
        P("dp", "seq", None),
        P("dp", None, "seq"),
        P(),
        P("dp", None),
        P(),
        P(),
        P(),
        P("dp", "seq", None),
    )
    out_specs = (P("dp", "seq", None), P("dp", None), P(), P(), P())
    return jax.shard_map(
        per_device, mesh=mesh, in_specs=in_specs, out_specs=out_specs, check_vma=False
    )
```

```python
import functools

import jax
import jax.numpy as jnp
from jax import lax
from jax.experimental import pallas as pl
from jax.experimental.pallas import tpu as pltpu
from jax.sharding import PartitionSpec as P

EPS = 1e-05
MESH = pl.DeviceIdType.MESH
VM = pl.BlockSpec(memory_space=pltpu.VMEM)


def at(d, s):
    return {"dp": d, "seq": s}


def greet(peers):
    barrier = pltpu.get_barrier_semaphore()
    for peer in peers:
        pl.semaphore_signal(barrier, inc=1, device_id=peer, device_id_type=MESH)
    pl.semaphore_wait(barrier, len(peers))


def remote(src, dst, send, recv, peer):
    return pltpu.make_async_remote_copy(
        src_ref=src, dst_ref=dst, send_sem=send, recv_sem=recv, device_id=peer, device_id_type=MESH
    )


def ring_peers(me, count):
    return [lax.rem(me + k, count) for k in range(1, count)]


def merge(parts, stats):
    if not stats:
        return functools.reduce(lambda a, b: a + b, parts)
    sums = [part[0:16] for part in parts]
    squares = [part[16:32] for part in parts]
    counts = [part[32:48] for part in parts]
    total = functools.reduce(lambda a, b: a + b, sums)
    count = functools.reduce(lambda a, b: a + b, counts)
    mean = total / jnp.maximum(count, 1.0)
    spread = functools.reduce(lambda a, b: a + b, squares)
    for own, n in zip(sums, counts):
        shift = own / jnp.maximum(n, 1.0) - mean
        spread = spread + n * (shift * shift)
    return jnp.concatenate([total, spread, count], axis=0)


def sum_kernel(stats, dp_n, seq_n, x_ref, o_ref, near, far, mid, s1, r1, s2, r2):
    d, s = lax.axis_index("dp"), lax.axis_index("seq")
    plane = ring_peers(s, seq_n)
    line = ring_peers(d, dp_n)
    greet([at(d, j) for j in plane] + [at(j, s) for j in line])
    for k, j in enumerate(plane):
        remote(x_ref, near.at[s], s1.at[k], r1.at[s], at(d, j)).start()
    near[s] = x_ref[...]
    for k, j in enumerate(plane):
        copy = remote(x_ref, near.at[j], s1.at[k], r1.at[j], at(d, j))
        copy.wait_recv()
        copy.wait_send()
    mid[...] = merge([near[j] for j in range(seq_n)], stats)
    for k, j in enumerate(line):
        remote(mid, far.at[d], s2.at[k], r2.at[d], at(j, s)).start()
    far[d] = mid[...]
    for k, j in enumerate(line):
        copy = remote(mid, far.at[j], s2.at[k], r2.at[j], at(j, s))
        copy.wait_recv()
        copy.wait_send()
    o_ref[...] = merge([far[j] for j in range(dp_n)], stats)


def sum_all(vectors, stats, collective_id):
    dp_n, seq_n = lax.axis_size("dp"), lax.axis_size("seq")
    blocks = vectors[0].shape[-1] // 128
    stacked = jnp.stack([v.reshape(blocks, 128) for v in vectors])
    stacked = jnp.pad(stacked, ((0, 0), (0, 16 - blocks), (0, 0)))
    rows = 16 * len(vectors)
    shape = (rows, 128)
    out = pl.pallas_call(
        functools.partial(sum_kernel, stats, dp_n, seq_n),
        out_shape=jax.ShapeDtypeStruct(shape, jnp.float32),
        in_specs=[VM],
        out_specs=VM,
        scratch_shapes=[
            pltpu.VMEM((seq_n,) + shape, jnp.float32),
            pltpu.VMEM((dp_n,) + shape, jnp.float32),
            pltpu.VMEM(shape, jnp.float32),
            pltpu.SemaphoreType.DMA((seq_n,)),
            pltpu.SemaphoreType.DMA((seq_n,)),
            pltpu.SemaphoreType.DMA((dp_n,)),
            pltpu.SemaphoreType.DMA((dp_n,)),
        ],
        compiler_params=pltpu.CompilerParams(collective_id=collective_id, has_side_effects=True),
    )(stacked.reshape(shape))
    return out.reshape(len(vectors), 16, 128)[:, :blocks].reshape(len(vectors), blocks * 128)


HALO = 32
EDGE = 16
TAPS = 31
BF = jnp.bfloat16
F32 = jnp.float32


class Net:
    def __init__(self, send_sems, recv_sems):
        self.send_sems, self.recv_sems = send_sems, recv_sems
        self.used = 0
        self.sent = []

    def send(self, src, dst, peer):
        copy = remote(src, dst, self.send_sems.at[self.used], self.recv_sems.at[self.used], peer)
        self.used += 1
        copy.start()
        self.sent.append(copy)
        return copy

    def drain(self):
        for copy in self.sent:
            copy.wait_send()


def rows_at(start, size):
    return pl.ds(pl.multiple_of(start, 16), size)


def cols_at(start, size):
    return pl.ds(pl.multiple_of(start, 128), size)


def fused_kernel(
    len_ref, w_ref, codes_hbm, scale_hbm, og_ref, ck_hbm, gain_hbm, shift_hbm,
    ig_ref, F, kf_ref,
    codes_ref, scale_ref, ck_ref, gain_ref, shift_ref, res_ref, by_frame, W, R, O, G, A, S, C, D, GP,
    st1, sb1, st2, sb2, vec,
    kp, kb,
    igp, igs, igr, igs2, igr2,
    P, sa, ra, sa2, ra2, sz, rz,
    send_sems, recv_sems, local_sems,
):
    z, s = lax.axis_index("dp"), lax.axis_index("seq")
    c, x, y = lax.rem(s, 2), lax.rem(s // 2, 2), s // 4
    q = s // 2
    kind, half = z // 2, lax.rem(z, 2)
    mate_z = z + 1 - 2 * half
    twin_z = z + 2 - 4 * kind
    jo, jm = half, 1 - half
    frames = codes_hbm.shape[0]
    span = 2 * frames
    width = codes_hbm.shape[1]
    hw = width // 2

    def chip_at(dy, dx):
        yy = 1 - y if dy else y
        xx = 1 - x if dx else x
        return yy * 2 + xx

    core = at(z, s + 1 - 2 * c)
    mate = at(mate_z, s)
    twin = at(twin_z, s)
    offsets = [(0, 1), (1, 0), (1, 1)]
    plane = [at(z, chip_at(dy, dx) * 2 + c) for dy, dx in offsets]
    px, py = plane[0], plane[1]
    far = [at(twin_z, chip_at(dy, dx) * 2 + c) for dy, dx in offsets]
    to_q = lax.rem(q + 2 * c + 3, 4)
    from_q = lax.rem(q + 5 - 2 * c, 4)
    net = Net(send_sems, recv_sems)
    locals_ = []

    def local(src, dst):
        copy = pltpu.make_async_copy(src, dst, local_sems.at[len(locals_)])
        copy.start()
        locals_.append(copy)
        return copy

    loads = [
        local(src, dst) for src, dst in (
            (codes_hbm, codes_ref), (scale_hbm, scale_ref), (ck_hbm, ck_ref),
            (gain_hbm, gain_ref), (shift_hbm, shift_ref))
    ]
    wr = W.shape[0] // 2
    blocks = wr // 128
    own_w = [
        local(w_ref.at[rows_at(c * wr + b * 128, 128)], W.at[rows_at((2 * b + kind) * 128, 128)])
        for b in range(blocks)
    ]
    greet([core, mate, twin] + plane + far)

    def spread_out(src, dst, edge, window):
        mine = rows_at(edge + frames * c, frames)
        rim_src = rows_at(c * (frames - edge), edge)
        rim_dst = rows_at(edge + frames * c + c * (frames - edge), edge)
        rim = rows_at((1 - c) * (edge + span), edge)
        rest_src = rows_at((1 - c) * edge, frames - edge)
        rest_dst = rows_at(edge + frames * c + (1 - c) * edge, frames - edge)
        here, there = window(half), window(1 - half)
        side = net.send(src.at[rim_src, there], dst.at[jo, rim_dst], mate)
        rim_own = net.send(src.at[rim_src, here], dst.at[jo, rim], at(z, to_q * 2 + c))
        own = local(src.at[:, here], dst.at[jo, mine])

        def rest():
            return net.send(src.at[rest_src, there], dst.at[jo, rest_dst], mate)

        def over():
            return net.send(src.at[:, here], dst.at[jo, mine], core)

        return side, rim_own, own, rest, over

    def rims_on(parts, dst, edge):
        rim_dst = rows_at(edge + frames * c + c * (frames - edge), edge)
        rim = rows_at((1 - c) * (edge + span), edge)
        side, rim_own = parts[:2]
        side.wait_recv()
        rim_mate = net.send(dst.at[jm, rim_dst], dst.at[jm, rim], at(z, to_q * 2 + c))
        rim_own.wait_recv()
        ref = dst.at[jo, rim]
        return rim_mate, net.send(ref, ref, core)

    def mate_on(rest, rim_mate, dst, edge):
        rim = rows_at((1 - c) * (edge + span), edge)
        rim_mate.wait_recv()
        ref = dst.at[jm, rim]
        got = [net.send(ref, ref, core)]
        rest.wait_recv()
        ref = dst.at[jm, rows_at(edge + frames * c, frames)]
        return got + [net.send(ref, ref, core)]

    step = 32
    wsend = []

    def weights_out(i):
        if i:
            wsend[i - 1].wait_send()
            net.sent = [copy for copy in net.sent if copy is not wsend[i - 1]]
        wsend.append(net.send(
            w_ref.at[rows_at(c * wr + i * 128 + q * step, step)],
            W.at[rows_at((2 * i + kind) * 128 + q * step, step)], twin))

    weights_out(0)
    for copy in loads:
        copy.wait()
    for b in range(width // 128):
        by_frame[b:b + 1, :] = scale_ref[b]
    columns = jnp.transpose(by_frame[...])
    for b in range(width // 128):
        lanes = pl.ds(b * 128, 128)
        res_ref[:, lanes] = (
            codes_ref[:, lanes].astype(F32) * columns[:, b:b + 1]
        ).astype(BF)

    r_parts = spread_out(res_ref, R, HALO, lambda h: pl.ds(0, width))
    r_over = r_parts[4]()
    near_w, far_w = [], []

    def piece(i, chip, start, size):
        return W.at[rows_at((2 * i + 1 - kind) * 128 + chip * step + start, size)]

    def pass_near(i):
        wsend[i].wait_recv()
        ref = piece(i, q, 0, step)
        near_w.append((net.send(ref, ref, px), net.send(ref, ref, py)))

    def pass_far(i):
        from_x, from_y = near_w[i]
        from_x.wait_recv()
        ref = piece(i, chip_at(0, 1), 0, step // 2)
        to_y = net.send(ref, ref, py)
        from_y.wait_recv()
        ref = piece(i, chip_at(1, 0), step // 2, step // 2)
        far_w.append((to_y, net.send(ref, ref, px)))

    def block_here(i):
        own_w[i].wait()
        for copy in far_w[i]:
            copy.wait_recv()

    chan = (half * 2 + c) * wr
    lens = [len_ref[kind * 2 + j] for j in range(2)]

    def mask_rows(j, edge, rows):
        frame = q * span - edge + lax.broadcasted_iota(jnp.int32, (rows, 128), 0)
        length = jnp.where(j == 0, lens[0], lens[1])
        return (frame >= 0) & (frame < length)

    long = span + 2 * HALO
    mid = span + 2 * EDGE

    def project(j, b):
        pre = lax.dot_general(
            R[j], W[rows_at(b * 256, 256), :], (((1,), (1,)), ((), ())),
            preferred_element_type=F32
        )
        lin = pre[:, 0:128]
        sig = jax.nn.sigmoid(pre[:, 128:256])
        G[j, b] = jnp.where(mask_rows(j, HALO, long), lin * sig, 0.0).astype(BF).astype(F32)
        A[j, b] = lin[HALO:HALO + span]
        S[j, b] = sig[HALO:HALO + span]

    def count_at(pair, chip, j):
        n = jnp.clip(len_ref[pair * 2 + j] - chip * span, 0, span)
        return jnp.full((8, 128), n, jnp.int32).astype(F32)

    own_counts = [count_at(kind, q, j) for j in range(2)]

    def convolve(j, b):
        lanes = cols_at(chan + b * 128, 128)
        acc = jnp.zeros((mid, 128), F32)
        for k in range(TAPS):
            acc = acc + ck_ref[k:k + 1, lanes] * G[j, b, pl.ds(1 + k, mid), :]
        C[j, b] = acc
        keep = mask_rows(j, 0, span)
        own = acc[EDGE:EDGE + span]
        total = jnp.sum(jnp.where(keep, own, 0.0), axis=0, keepdims=True)
        n = jnp.where(j == 0, own_counts[0][0:1], own_counts[1][0:1])
        dev = jnp.where(keep, own - total / jnp.maximum(n, 1.0), 0.0)
        st1[j, pl.ds(b, 1), :] = total
        st1[j, pl.ds(blocks + b, 1), :] = jnp.sum(dev * dev, axis=0, keepdims=True)

    def forward(j, first, last):
        @pl.loop(first, last)
        def _(b):
            project(j, b)
            convolve(j, b)

    weights_out(1)
    pass_near(0)
    weights_out(2)
    r_rest = r_parts[3]()
    r_rim_mate, r_rim_core = rims_on(r_parts, R, HALO)
    pass_near(1)
    pass_far(0)
    for copy in (r_over, r_rim_core):
        copy.wait_recv()
    r_parts[2].wait()
    block_here(0)
    pass_near(2)
    pass_far(1)
    forward(jo, 0, 1)
    r_got = mate_on(r_rest, r_rim_mate, R, HALO)
    o_parts = spread_out(og_ref, O, EDGE, lambda h: cols_at(h * hw, hw))
    o_rest = o_parts[3]()
    o_over = o_parts[4]()
    pass_far(2)
    block_here(1)
    for copy in r_got:
        copy.wait_recv()
    forward(jo, 1, 2)
    forward(jm, 0, 2)
    block_here(2)
    forward(jo, 2, 3)
    o_rim_mate, o_rim_core = rims_on(o_parts, O, EDGE)
    forward(jm, 2, 3)

    me8 = kind * 4 + q
    peers8 = plane + [twin] + far

    def exchange(src, slots):
        own = local(src, slots.at[me8])
        copies = [net.send(src, slots.at[me8], peer) for peer in peers8]
        return own, copies

    own, copies = exchange(st1, sb1)
    o_got = mate_on(o_rest, o_rim_mate, O, EDGE)
    own.wait()
    for copy in copies:
        copy.wait_recv()
    counted = jnp.zeros((8, 128), F32)
    for g in range(len_ref.shape[0]):
        counted = counted + jnp.full((8, 128), len_ref[g], jnp.int32).astype(F32)
    total = jnp.zeros((8, 128), F32)
    for i in range(8):
        for j in range(2):
            total = total + sb1[i, j]
    mean = total / counted
    shift2 = jnp.zeros((8, 128), F32)
    for i in range(8):
        for j in range(2):
            n = count_at(i // 4, i % 4, j)
            d = sb1[i, j] / jnp.maximum(n, 1.0) - mean
            shift2 = shift2 + n * (d * d)
    vec[0] = total
    vec[1] = shift2
    var = (vec[0, blocks:2 * blocks] + vec[1, 0:blocks]) / counted[0:blocks]
    vec[2] = mean
    vec[3, 0:blocks] = lax.rsqrt(var + EPS)

    for copy in o_got + [o_over, o_rim_core]:
        copy.wait_recv()
    o_parts[2].wait()

    @pl.loop(0, 2 * blocks)
    def _(t):
        j, b = t // blocks, lax.rem(t, blocks)
        lanes = cols_at(chan + b * 128, 128)
        normed = (C[j, b] - vec[2, pl.ds(b, 1), :]) * vec[3, pl.ds(b, 1), :]
        shaped = gain_ref[lanes][None] * normed + shift_ref[lanes][None]
        smooth = jax.nn.sigmoid(shaped)
        up = O[j, :, cols_at(c * wr + b * 128, 128)].astype(F32)
        gs = jnp.where(
            mask_rows(j, EDGE, mid), up * smooth * (1.0 + shaped * (1.0 - smooth)), 0.0
        )
        D[j, b] = gs
        own = gs[EDGE:EDGE + span]
        st1_rows = jnp.sum(own, axis=0, keepdims=True)
        gain_rows = jnp.sum(own * normed[EDGE:EDGE + span], axis=0, keepdims=True)
        st2[1 + j, pl.ds(b, 1), :] = st1_rows
        st2[1 + j, pl.ds(blocks + b, 1), :] = gain_rows

    st2[0] = st2[1] + st2[2]
    own, copies = exchange(st2.at[0], sb2)

    own.wait()
    for copy in copies:
        copy.wait_recv()
    sums = jnp.zeros((8, 128), F32)
    for i in range(8):
        sums = sums + sb2[i]
    vec[4] = sums

    @pl.loop(0, 2 * blocks)
    def _(t):
        j, b = t // blocks, lax.rem(t, blocks)
        lanes = cols_at(chan + b * 128, 128)
        inverse = vec[3, pl.ds(b, 1), :]
        normed = (C[j, b] - vec[2, pl.ds(b, 1), :]) * inverse
        add, mul = vec[4, pl.ds(b, 1), :], vec[4, pl.ds(blocks + b, 1), :]
        D[j, b] = jnp.where(
            mask_rows(j, EDGE, mid),
            gain_ref[lanes][None] * inverse * (D[j, b] - (add + normed * mul) / counted[0:1]),
            0.0,
        )

    def back(b):
        lanes = cols_at(chan + b * 128, 128)

        @pl.loop(0, 2)
        def _(j):
            acc = jnp.zeros((span, 128), F32)
            for k in range(TAPS):
                acc = acc + ck_ref[k:k + 1, lanes] * D[j, b, pl.ds(TAPS - k, span), :]
            acc = jnp.where(mask_rows(j, 0, span), acc, 0.0)
            sig = S[j, b]
            to_lin = acc * sig
            GP[j, :, b * 256:b * 256 + 128] = to_lin.astype(BF)
            GP[j, :, b * 256 + 128:(b + 1) * 256] = (
                to_lin * A[j, b] * (1.0 - sig)
            ).astype(BF)

    tile = 512

    def input_grad():
        @pl.loop(0, 2 * (width // tile))
        def _(t):
            j, n = t // (width // tile), lax.rem(t, width // tile)
            lanes = cols_at(n * tile, tile)
            part = jnp.dot(GP[j], W[:, lanes], preferred_element_type=F32)
            igp[j, :, lanes] = part

        igs[...] = igp[:, rows_at((1 - c) * frames, frames), :].astype(BF)
        return net.send(igs, igr, core)

    def taps():
        @pl.loop(0, blocks)
        def _(b):
            for k in range(TAPS):
                part = jnp.zeros((1, 128), F32)
                for j in range(2):
                    part = part + jnp.sum(
                        D[j, b, pl.ds(EDGE, span), :] * G[j, b, pl.ds(EDGE + 1 + k, span), :],
                        axis=0, keepdims=True)
                kp[k // 4, b, k % 4:k % 4 + 1, :] = part
            kp[7, b, 3:4, :] = jnp.zeros((1, 128), F32)

        own = local(kp.at[me8], kb.at[me8])
        index = [kind * 4 + chip_at(dy, dx) for dy, dx in offsets]
        index += [(1 - kind) * 4 + i for i in [q] + [chip_at(dy, dx) for dy, dx in offsets]]
        return own, [net.send(kp.at[i], kb.at[me8], peer) for i, peer in zip(index, peers8)]

    eh = hw
    colsA, colsB = pl.ds(0, eh), pl.ds(eh, eh)

    def s1(m, b):
        rows = cols_at((2 * b + (kind if m else 1 - kind)) * 128, 128)

        @pl.loop(0, width // tile)
        def _(n):
            lanes = cols_at(n * tile, tile)
            acc = jnp.zeros((128, tile), F32)
            for j in range(2):
                acc = acc + lax.dot_general(
                    GP[j, :, rows], R[j, pl.ds(HALO, span), lanes], (((0,), (0,)), ((), ())),
                    preferred_element_type=F32)
            P[m, b, :, lanes] = acc

        sa[m, b, 0] = P[m, b, rows_at((1 - x) * 64, 64), 0:eh].astype(BF)
        sa[m, b, 1] = P[m, b, rows_at((1 - y) * 64, 64), eh:2 * eh].astype(BF)
        return [
            net.send(sa.at[m, b, 0], ra.at[m, b, 0], px),
            net.send(sa.at[m, b, 1], ra.at[m, b, 1], py),
        ]

    def s2(m, b, got):
        for copy in got:
            copy.wait_recv()
        sa2[m, b, 0] = (
            P[m, b, rows_at(x * 64 + (1 - y) * 32, 32), 0:eh]
            + ra[m, b, 0, rows_at((1 - y) * 32, 32), :].astype(F32)).astype(BF)
        sa2[m, b, 1] = (
            P[m, b, rows_at(y * 64 + (1 - x) * 32, 32), eh:2 * eh]
            + ra[m, b, 1, rows_at((1 - x) * 32, 32), :].astype(F32)).astype(BF)
        return [
            net.send(sa2.at[m, b, 0], ra2.at[m, b, 0], py),
            net.send(sa2.at[m, b, 1], ra2.at[m, b, 1], px),
        ]

    row_a, row_b = x * 64 + y * 32, y * 64 + x * 32

    def summed(m, b):
        return (
            P[m, b, rows_at(row_a, 32), 0:eh] + ra[m, b, 0, rows_at(y * 32, 32), :].astype(F32)
            + ra2[m, b, 0].astype(F32),
            P[m, b, rows_at(row_b, 32), eh:2 * eh] + ra[m, b, 1, rows_at(x * 32, 32), :].astype(F32)
            + ra2[m, b, 1].astype(F32),
        )

    def to_twin(b, got):
        for copy in got:
            copy.wait_recv()
        part_a, part_b = summed(0, b)
        sz[b, 0] = part_a.astype(BF)
        sz[b, 1] = part_b.astype(BF)
        return net.send(sz.at[b], rz.at[b], twin)

    def tile_of(core_at, b, start, size, cols):
        return F.at[rows_at(core_at * wr + b * 128 + start, size), cols]

    cols_a, cols_b = pl.ds(0, eh), pl.ds(eh, eh)

    def s3(b, got, from_twin):
        for copy in got:
            copy.wait_recv()
        part_a, part_b = summed(1, b)
        from_twin.wait_recv()
        fa, fb = tile_of(c, b, row_a, 32, cols_a), tile_of(c, b, row_b, 32, cols_b)
        fa[...] = (part_a + rz[b, 0].astype(F32)).astype(BF)
        fb[...] = (part_b + rz[b, 1].astype(F32)).astype(BF)
        return [net.send(fa, fa, py), net.send(fb, fb, px)]

    def s4(b, got):
        for copy in got:
            copy.wait_recv()
        fa, fb = tile_of(c, b, x * 64, 64, cols_a), tile_of(c, b, y * 64, 64, cols_b)
        return [net.send(fa, fa, px), net.send(fb, fb, py)]

    def s5(b, got):
        for copy in got:
            copy.wait_recv()
        ref = tile_of(c, b, 0, 128, pl.ds(0, width))
        return [net.send(ref, ref, core)]

    def k1(own, got):
        own.wait()
        for copy in got:
            copy.wait_recv()
        hc = half * 2 + c
        for b in range(blocks):
            part = jnp.zeros((8, 128), F32)
            for i in range(8):
                part = part + kb[i, b]
            kf_ref[hc, me8, b] = part
            kf_ref[hc, me8, b, 4:5, :] = vec[4, b:b + 1, :]
            kf_ref[hc, me8, b, 5:6, :] = vec[4, blocks + b:blocks + b + 1, :]
        ref = kf_ref.at[hc, me8]
        return [net.send(ref, ref, peer) for peer in peers8]

    def k2(got):
        for copy in got:
            copy.wait_recv()
        ref = kf_ref.at[half * 2 + c]
        return [net.send(ref, ref, core)]

    def k3(got):
        for copy in got:
            copy.wait_recv()
        ref = kf_ref.at[pl.ds(half * 2, 2)]
        return [net.send(ref, ref, mate)]

    def i1(got):
        got.wait_recv()
        igs2[...] = (
            igp[jm, rows_at(c * frames, frames), :] + igr[jm].astype(F32)
        ).astype(BF)
        return net.send(igs2, igr2, mate)

    def i2(got):
        got.wait_recv()
        ig_ref[...] = (
            igp[jo, rows_at(c * frames, frames), :] + igr[jo].astype(F32) + igr2[...].astype(F32)
        ).astype(BF)

    back(0)
    o0 = s1(0, 0)
    back(1)
    o1 = s1(0, 1)
    back(2)
    o0 = s2(0, 0, o0)
    o2 = s1(0, 2)
    o1 = s2(0, 1, o1)
    w0 = s1(1, 0)
    t0 = to_twin(0, o0)
    o2 = s2(0, 2, o2)
    w1 = s1(1, 1)
    t1 = to_twin(1, o1)
    w2 = s1(1, 2)
    ig = input_grad()
    w0 = s2(1, 0, w0)
    t2 = to_twin(2, o2)
    kown, k = taps()
    w1 = s2(1, 1, w1)
    ig = i1(ig)
    w2 = s2(1, 2, w2)
    w0 = s3(0, w0, t0)
    w1 = s3(1, w1, t1)
    k = k1(kown, k)
    w0 = s4(0, w0)
    w2 = s3(2, w2, t2)
    w1 = s4(1, w1)
    k = k2(k)
    w0 = s5(0, w0)
    w2 = s4(2, w2)
    k = k3(k)
    w1 = s5(1, w1)
    i2(ig)
    w2 = s5(2, w2)
    for copy in w0 + w1 + w2 + k:
        copy.wait_recv()
    net.drain()


def finish_kernel(ig_in, wg_in, kf_in, ig_out, wg_out, taps_out, gain_out, shift_out, wide, sems):
    copies = []

    def put(src, dst):
        copy = pltpu.make_async_copy(src, dst, sems.at[len(copies)])
        copy.start()
        copies.append(copy)

    put(ig_in, ig_out)
    parts = 12
    rows = wg_in.shape[0] // parts
    for i in range(parts):
        where = pl.ds(i * rows, rows)
        wide[where, :] = wg_in[where, :].astype(F32)
        put(wide.at[where], wg_out.at[where])
    owners, blocks = kf_in.shape[1], kf_in.shape[2]
    for hc in range(4):
        for b in range(blocks):
            lanes = pl.ds((hc * blocks + b) * 128, 128)
            for i in range(owners):
                n = min(4, taps_out.shape[0] - 4 * i)
                taps_out[4 * i:4 * i + n, lanes] = kf_in[hc, i, b, 0:n, :]
            shift_out[lanes] = kf_in[hc, 0, b, 4, :]
            gain_out[lanes] = kf_in[hc, 0, b, 5, :]
    for copy in copies:
        copy.wait()


def finish(in_grad, weight_grad, taps):
    any_space = pl.BlockSpec(memory_space=pl.ANY)
    width = in_grad.shape[1]
    return pl.pallas_call(
        finish_kernel,
        out_shape=(
            jax.ShapeDtypeStruct(in_grad.shape, BF),
            jax.ShapeDtypeStruct(weight_grad.shape, F32),
            jax.ShapeDtypeStruct((TAPS, width), F32),
            jax.ShapeDtypeStruct((width,), F32),
            jax.ShapeDtypeStruct((width,), F32),
        ),
        in_specs=[VM, VM, VM],
        out_specs=(any_space, any_space, VM, VM, VM),
        scratch_shapes=[pltpu.VMEM(weight_grad.shape, F32), pltpu.SemaphoreType.DMA((16,))],
        compiler_params=pltpu.CompilerParams(vmem_limit_bytes=20 * 1024 * 1024),
    )(in_grad, weight_grad, taps)


def fused(lengths, in_weight, codes, scales, out_grad, conv_kernel, bn_gain, bn_shift):
    frames, width = codes.shape
    wr = width // 4
    blocks = wr // 128
    span = 2 * frames
    long, mid = span + 2 * HALO, span + 2 * EDGE
    dma = pltpu.SemaphoreType.DMA
    hbm = pl.BlockSpec(memory_space=pltpu.HBM)
    smem = pl.BlockSpec(memory_space=pltpu.SMEM)

    def vm(shape, dtype=F32):
        return pltpu.VMEM(shape, dtype)

    return pl.pallas_call(
        fused_kernel,
        out_shape=(
            jax.ShapeDtypeStruct((frames, width), BF),
            jax.ShapeDtypeStruct((2 * wr, width), BF),
            jax.ShapeDtypeStruct((4, 8, blocks, 8, 128), F32),
        ),
        in_specs=[smem] + [hbm] * 7,
        out_specs=(VM, VM, VM),
        scratch_shapes=[
            vm((frames, width), BF),
            vm(scales.shape),
            vm(conv_kernel.shape),
            vm(bn_gain.shape),
            vm(bn_shift.shape),
            vm((frames, width), BF),
            vm((128, 128)),
            vm((2 * wr, width), BF),
            vm((2, long, width), BF),
            vm((2, mid, width // 2), BF),
            vm((2, blocks, long, 128)),
            vm((2, blocks, span, 128)),
            vm((2, blocks, span, 128)),
            vm((2, blocks, mid, 128)),
            vm((2, blocks, mid, 128)),
            vm((2, span, 2 * wr), BF),
            vm((2, 8, 128)),
            vm((8, 2, 8, 128)),
            vm((3, 8, 128)),
            vm((8, 8, 128)),
            vm((5, 8, 128)),
            vm((8, blocks, 8, 128)),
            vm((8, blocks, 8, 128)),
            vm((2, span, width)),
            vm((2, frames, width), BF),
            vm((2, frames, width), BF),
            vm((frames, width), BF),
            vm((frames, width), BF),
            vm((2, blocks, 128, width)),
            vm((2, blocks, 2, 64, width // 2), BF),
            vm((2, blocks, 2, 64, width // 2), BF),
            vm((2, blocks, 2, 32, width // 2), BF),
            vm((2, blocks, 2, 32, width // 2), BF),
            vm((blocks, 2, 32, width // 2), BF),
            vm((blocks, 2, 32, width // 2), BF),
            dma((128,)),
            dma((128,)),
            dma((16,)),
        ],
        compiler_params=pltpu.CompilerParams(
            collective_id=4, has_side_effects=True, vmem_limit_bytes=36 * 1024 * 1024
        ),
    )(*[
        pltpu.with_memory_space_constraint(operand, pltpu.HBM)
        for operand in (
            lengths, in_weight, codes, scales, out_grad, conv_kernel, bn_gain, bn_shift)
    ])


def padded_2(cells, sides, width):
    for axis, dim in sides:
        count = lax.axis_size(axis)
        ends = count - 1
        head = lax.slice_in_dim(cells, 0, width, axis=dim)
        tail = lax.slice_in_dim(cells, cells.shape[dim] - width, cells.shape[dim], axis=dim)
        cells = jnp.concatenate(
            [
                lax.ppermute(tail, axis, [(i, (i + 1) % count) for i in range(ends)]),
                cells,
                lax.ppermute(head, axis, [((i + 1) % count, i) for i in range(ends)]),
            ],
            axis=dim,
        )
    return cells


def restore(quantized, scales):
    per_channel = jnp.repeat(scales.T, 128, axis=1)
    return (quantized.astype(jnp.float32) * per_channel).astype(jnp.bfloat16)


def depthwise(padded, kernel, frames):
    running = jnp.zeros((frames, padded.shape[1]), jnp.float32)
    for offset in range(kernel.shape[0]):
        running = running + kernel[offset] * padded[offset : offset + frames].astype(jnp.float32)
    return running


def general(
    saved_codes, code_scales, lengths, in_weight, conv_kernel, bn_gain, bn_shift, out_grad
):
    frames = saved_codes.shape[1]
    feature_width = saved_codes.shape[2]
    tap_count = conv_kernel.shape[0]
    half_span = (tap_count - 1) // 2
    groups = lengths.shape[0]
    group_at = lax.axis_index("dp")
    length = jnp.sum(jnp.where(jnp.arange(groups, dtype=jnp.int32) == group_at, lengths, 0))
    counted = jnp.sum(lengths).astype(jnp.float32)
    first_frame = lax.axis_index("seq") * frames
    valid_mask = (first_frame + jnp.arange(frames, dtype=jnp.int32) < length).astype(jnp.float32)[
        :, None
    ]
    restored = restore(saved_codes[0], code_scales[0])
    weights = lax.all_gather(in_weight, "dp", axis=0, tiled=True)
    pre_act = lax.dot_general(
        restored, weights, (((1,), (1,)), ((), ())), preferred_element_type=jnp.float32
    )
    linear = pre_act[:, :feature_width]
    gate_part = jax.nn.sigmoid(pre_act[:, feature_width:])
    gated = (linear * gate_part * valid_mask).astype(jnp.bfloat16)
    gated_pad = padded_2(gated, (("seq", 0),), half_span)
    conv_out = depthwise(gated_pad, conv_kernel, frames)
    own_sum = jnp.sum(conv_out * valid_mask, axis=0)
    own_count = jnp.sum(valid_mask)
    centered = (conv_out - own_sum / jnp.maximum(own_count, 1.0)) * valid_mask
    own_square = jnp.sum(centered * centered, axis=0)
    total, spread, _ = sum_all(
        [own_sum, own_square, jnp.full_like(own_sum, own_count)], True, 0
    )
    mean_value = total / counted
    variance = spread / counted
    inverse = lax.rsqrt(variance + EPS)
    normed = (conv_out - mean_value) * inverse
    shaped = bn_gain * normed + bn_shift
    smooth = jax.nn.sigmoid(shaped)
    grad_shaped = (
        out_grad[0].astype(jnp.float32) * valid_mask * smooth * (1.0 + shaped * (1.0 - smooth))
    )
    shift_grad, gain_grad = sum_all(
        [jnp.sum(grad_shaped, axis=0), jnp.sum(grad_shaped * normed, axis=0)], False, 1
    )
    grad_conv = (
        bn_gain * inverse * (grad_shaped - (shift_grad + normed * gain_grad) / counted) * valid_mask
    )
    kernel_part = jnp.stack(
        [
            jnp.sum(grad_conv * gated_pad[offset : offset + frames].astype(jnp.float32), axis=0)
            for offset in range(tap_count)
        ]
    )
    grad_pad = padded_2(grad_conv, (("seq", 0),), half_span)
    grad_gated = depthwise(grad_pad, conv_kernel[::-1], frames) * valid_mask
    grad_pre = jnp.concatenate(
        [grad_gated * gate_part, grad_gated * linear * gate_part * (1.0 - gate_part)], axis=1
    ).astype(jnp.bfloat16)
    in_grad = jnp.dot(grad_pre, weights, preferred_element_type=jnp.float32)
    own_columns = lax.all_to_all(grad_pre[None], "dp", split_axis=2, concat_axis=0, tiled=True)
    local_rows = lax.dot_general(
        own_columns,
        lax.all_gather(restored[None], "dp", axis=0, tiled=True),
        (((0, 1), (0, 1)), ((), ())),
        preferred_element_type=jnp.float32,
    )
    weight_grad = lax.psum(local_rows, "seq")
    kernel_grad = lax.psum(kernel_part, ("dp", "seq"))
    return (in_grad.astype(jnp.bfloat16)[None], weight_grad, kernel_grad, gain_grad, shift_grad)


def per_device(
    saved_codes, code_scales, lengths, in_weight, conv_kernel, bn_gain, bn_shift, out_grad
):
    frames, width = saved_codes.shape[1:]
    square = (
        lax.axis_size("dp") == 4 and lax.axis_size("seq") == 8 and frames == 128
        and width == 1536 and conv_kernel.shape[0] == TAPS and lengths.shape[0] == 4
    )
    if not square:
        return general(
            saved_codes, code_scales, lengths, in_weight, conv_kernel, bn_gain, bn_shift, out_grad
        )
    in_grad, weight_grad, taps = fused(
        lengths, in_weight, saved_codes[0], jnp.transpose(code_scales, (1, 0, 2)), out_grad[0],
        conv_kernel, bn_gain, bn_shift
    )
    in_grad, weight_grad, kernel_grad, gain_grad, shift_grad = finish(in_grad, weight_grad, taps)
    return in_grad[None], weight_grad, kernel_grad, gain_grad, shift_grad


def solution(mesh):
    in_specs = (
        P("dp", "seq", None),
        P("dp", None, "seq"),
        P(),
        P("dp", None),
        P(),
        P(),
        P(),
        P("dp", "seq", None),
    )
    out_specs = (P("dp", "seq", None), P("dp", None), P(), P(), P())
    return jax.shard_map(
        per_device, mesh=mesh, in_specs=in_specs, out_specs=out_specs, check_vma=False
    )
```
